32 devices in a mesh: seq: 2 (over y), fsdp: 16 (over z, x, core).
Axes of the slice: x: 2, y: 2, z: 4, core: 2. Of those that a mesh axis runs over, the one named last changes fastest.
Arguments:
- block_input: bfloat16 [16, 1024, 768], P('fsdp', 'seq'), may hold values from -6 to 6
- lead_gain: bfloat16 [768], P('fsdp'), may hold values from 0.099609375 to 1.8984375
- joint_weight: bfloat16 [768, 2304], P('fsdp'), may hold values from -0.3125 to 0.3125
- output_weight: bfloat16 [768, 768], P('fsdp'), may hold values from -0.875 to 0.875
- tail_gain: bfloat16 [768], P('fsdp'), may hold values from 0.099609375 to 1.8984375
- up_weight: bfloat16 [768, 3072], P('fsdp'), may hold values from -0.21875 to 0.21875
- down_weight: bfloat16 [3072, 768], P('fsdp'), may hold values from -0.109375 to 0.109375
- cotangent: bfloat16 [16, 1024, 768], P('fsdp', 'seq'), may hold values from -6 to 6
Outputs:
- block_output: bfloat16 [16, 1024, 768], P('fsdp', 'seq')
- input_grad: float32 [16, 1024, 768], P('fsdp', 'seq')
- lead_grad: float32 [768], P('fsdp')
- joint_grad: float32 [768, 2304], P('fsdp')
- output_grad: float32 [768, 768], P('fsdp')
- tail_grad: float32 [768], P('fsdp')
- up_grad: float32 [768, 3072], P('fsdp')
- down_grad: float32 [3072, 768], P('fsdp')
The draws below stay inside these ranges and needn't reach their ends.
All inputs are finite; a program needn't handle non-finite values.
Results may differ from the reference program's by a relative error of at most 0.014.
The reference program's roundings to bfloat16 on the way count: a program that leaves them out, or rounds other values in their place, can miss the bound.
Values may be sent and summed in bfloat16 or wider, within the bound.
No kernel may reach another device: no remote copies, remote signals or barrier semaphores. Data moves between devices by JAX's collectives and lax.ppermute only.
A program may use at most 192 MiB of HBM per device.

```python
import jax
import jax.numpy as jnp
from jax import lax

D = 768
H = 12
HD = 64
FF = 3072
SEQ_LEN = 1024
SEQS = 16


def spiked(drawn, stream_key, source, target, shards_of, factor):
    def block_of(dim):
        return (jnp.arange(drawn.shape[dim]) // (drawn.shape[dim] // shards_of)).reshape((-1,) + (1,) * (drawn.ndim - 1 - dim))

    near = jax.random.permutation(stream_key, shards_of)[block_of(target)]
    second = (block_of(target) + shards_of // 2) % shards_of
    return jnp.where((block_of(source) == near) | (block_of(source) == second), factor * drawn, drawn)


def levels(own_key, dims, pieces, smallest, top_value):
    level, own = 1.0, jax.random.fold_in(own_key, 6)
    for axis_at, parts in pieces:
        draws = jnp.exp(jax.random.uniform(jax.random.fold_in(own, axis_at), (parts,), jnp.float32, smallest / len(pieces), top_value / len(pieces)))
        level = level * jnp.repeat(draws, dims[axis_at] // parts).reshape([-1 if axis == axis_at else 1 for axis in range(len(dims))])
    return level


def noise(key, extent, width, bound, shards=(), held_as=jnp.bfloat16):
    level = levels(key, extent, shards, -0.22, 0.18) if shards else 1.0
    array = jax.random.normal(key, extent, jnp.float32) * width * level
    return jnp.minimum(jnp.maximum(array, -bound), bound).astype(held_as)


def gaussian_with(own_key, dims, scale, limit, cuts, heavy, kind=jnp.bfloat16):
    values = scale * jax.random.normal(own_key, dims, jnp.float32)
    if cuts:
        values = values * levels(own_key, dims, cuts, -0.22, 0.18)
    return jnp.clip(spiked(values, jax.random.fold_in(own_key, 3), *heavy), -limit, limit).astype(kind)


def setup_inputs(seed: int = 0) -> dict:
    splits = jax.random.split(jax.random.key(seed), 9)
    return {
        "block_input": gaussian_with(splits[0], (SEQS, SEQ_LEN, D), 1.0, 6.0, ((0, 16), (1, 2)), (0, 2, 16, 2.0)),
        "lead_gain": jnp.clip(1.0 + 0.18 * jax.random.normal(splits[1], (D,), jnp.float32), 0.099609375, 1.8984375).astype(jnp.bfloat16),
        "joint_weight": noise(splits[2], (D, 3 * D), (D // 2) ** -0.5, 0.3125, ((0, 16),)),
        "output_weight": noise(splits[3], (D, D), (D // 16) ** -0.5, 0.875, ((0, 16),)),
        "tail_gain": jnp.clip(1.0 + 0.18 * jax.random.normal(splits[4], (D,), jnp.float32), 0.099609375, 1.8984375).astype(jnp.bfloat16),
        "up_weight": noise(splits[5], (D, FF), D ** -0.5, 0.21875, ((0, 16),)),
        "down_weight": noise(splits[6], (FF, D), FF ** -0.5, 0.109375, ((0, 16),)),
        "cotangent": noise(splits[7], (SEQS, SEQ_LEN, D), 1.0, 6.0, ((0, 16), (1, 2))),
    }


@jax.custom_vjp
def low(v):
    return lax.optimization_barrier(v.astype(jnp.bfloat16)).astype(jnp.float32)

@jax.custom_vjp
def low_back(v):
    return v

def low_keep(v):
    return (low(v), None)

def low_pass(kept, grad):
    return (grad,)

def back_keep(v):
    return (v, None)

def back_low(kept, grad):
    return (low(grad),)
low.defvjp(low_keep, low_pass)
low_back.defvjp(back_keep, back_low)
EPS = 1e-05
EXACT = lax.Precision.HIGHEST

def norm_rows(values, gain):
    center = values - lax.optimization_barrier(jnp.mean(values, axis=-1, keepdims=True))
    spread = lax.optimization_barrier(jnp.mean(center * center, axis=-1, keepdims=True))
    return center * lax.rsqrt(spread + EPS) * gain

def attend(queries, keys, values):
    length = queries.shape[0]
    block = min(512, length)
    scale = HD ** (-0.5)
    key_spots = jnp.arange(length, dtype=jnp.int32)

    def one_block(start):
        query_block = lax.dynamic_slice_in_dim(queries, start, block, 0)
        raw = jnp.einsum('qhd,khd->hqk', query_block, keys, precision=EXACT)
        scores = low_back(raw * scale)
        rows = start + jnp.arange(block, dtype=jnp.int32)
        allowed = (key_spots[None, :] <= rows[:, None])[None]
        safe = jnp.where(allowed, scores, 0.0)
        top = lax.optimization_barrier(jnp.max(jnp.abs(safe), axis=-1, keepdims=True))
        upper = jnp.where(allowed, jnp.exp(safe - top), 0.0)
        lower = jnp.where(allowed, jnp.exp(-safe - top), 0.0)
        total = top + jnp.log(0.5 * lax.optimization_barrier(jnp.sum(upper + lower, axis=-1, keepdims=True)))
        weights = jnp.where(allowed, 0.5 * (jnp.exp(safe - total) - jnp.exp(-safe - total)), 0.0)
        weights = low(weights)
        return jnp.einsum('hqk,khd->qhd', weights, values, precision=EXACT)
    starts = jnp.arange(length // block, dtype=jnp.int32) * block
    result = lax.map(jax.checkpoint(one_block), starts)
    return result.reshape(length, H, HD)

def smooth_gate(values):
    return jax.nn.gelu(values, approximate=True)

def block_forward(inputs, lead_gain, joint_weight, output_weight, tail_gain, up_weight, down_weight):
    length = inputs.shape[0]
    normed_one = low(norm_rows(inputs, lead_gain))
    projected = low_back(low(jnp.dot(normed_one, joint_weight, precision=EXACT)))
    queries = projected[:, :D].reshape(length, H, HD)
    keys = projected[:, D:2 * D].reshape(length, H, HD)
    values = projected[:, 2 * D:].reshape(length, H, HD)
    mixed = attend(queries, keys, values).reshape(length, D)
    mixed = low_back(low(mixed))
    branch = low_back(jnp.dot(mixed, output_weight, precision=EXACT))
    resid = inputs + branch
    normed_two = low(norm_rows(resid, tail_gain))
    pre = low_back(jnp.dot(normed_two, up_weight, precision=EXACT))
    active = low(smooth_gate(pre))
    feed = low_back(jnp.dot(active, down_weight, precision=EXACT))
    return resid + feed

def reference(block_input, lead_gain, joint_weight, output_weight, tail_gain, up_weight, down_weight, cotangent):
    params = tuple((a.astype(jnp.float32) for a in (lead_gain, joint_weight, output_weight, tail_gain, up_weight, down_weight)))
    zeros = tuple((jnp.zeros(p.shape, jnp.float32) for p in params))

    def one_seq(carry, pair):
        sequence, grad_seq = pair
        outcome, backward = jax.vjp(block_forward, sequence.astype(jnp.float32), *params)
        grads = backward(grad_seq.astype(jnp.float32))
        carry = tuple((c + g for c, g in zip(carry, grads[1:])))
        return (carry, (outcome.astype(jnp.bfloat16), grads[0]))
    totals, (outputs, input_grad) = lax.scan(one_seq, zeros, (block_input, cotangent))
    return (outputs, input_grad, totals[0], totals[1], totals[2], totals[3], totals[4], totals[5])
```

```python
import jax
import jax.numpy as jnp
from jax import lax
from jax.experimental import pallas as pl
from jax.experimental.pallas import tpu as pltpu
from jax.sharding import PartitionSpec as P

HD = 64
EPS = 1e-05
PAIR = 2 * HD
BAND = 256
LOG2E = 1.4426950408889634
LIMIT = 56 << 20
F32 = jnp.float32
BF16 = jnp.bfloat16

VMEM = pl.BlockSpec(memory_space=pltpu.VMEM)
SMEM = pl.BlockSpec(memory_space=pltpu.SMEM)


def dot(left, right):
    return jnp.dot(left, right, preferred_element_type=F32)


def dot_t(left, right):
    return lax.dot_general(left, right, (((1,), (1,)), ((), ())), preferred_element_type=F32)


def shaped(*dims, dtype=BF16):
    return jax.ShapeDtypeStruct(dims, dtype)


def cost(microseconds):
    return pl.CostEstimate(flops=int(microseconds * 1e9), transcendentals=0, bytes_accessed=int(microseconds * 3e6))


def call(kernel, name, outs, n_in, scratch=(), took=4):
    return pl.pallas_call(
        kernel,
        name=name,
        out_shape=outs,
        in_specs=[SMEM] + [VMEM] * n_in,
        out_specs=[VMEM] * len(outs),
        scratch_shapes=list(scratch),
        compiler_params=pltpu.CompilerParams(vmem_limit_bytes=LIMIT),
        cost_estimate=cost(took),
    )


def standardize(values):
    center = values - jnp.mean(values, axis=-1, keepdims=True)
    spread = jnp.mean(center * center, axis=-1, keepdims=True)
    rstd = lax.rsqrt(spread + EPS)
    return center * rstd, rstd


def norm_back(z, rstd, g):
    return (g - jnp.mean(g, axis=-1, keepdims=True) - z * jnp.mean(g * z, axis=-1, keepdims=True)) * rstd


def half_at(index, size):
    return pl.ds(pl.multiple_of(index * size, size), size)


def rows_in_order(meta, source, target, count, size):
    for spot in range(count):
        target[spot * size : (spot + 1) * size, :] = source[pl.ds(pl.multiple_of(meta[1 + spot] * size, size), size), :]


def first_norm(meta, own, other, gains, zb, zt, turned):
    half = own.shape[0]
    for source, place in ((own, meta[0]), (other, 1 - meta[0])):
        z = (standardize(source[...].astype(F32))[0] * gains[0:1, :].astype(F32)).astype(BF16)
        zb[half_at(place, half), :] = z
        turned[:, half_at(place, half)] = z.T
    rows_in_order(meta, turned, zt, 16, turned.shape[0] // 16)


def attend(meta, zb, near, far, qkv, o_own, o_other, lse, weight, km, vt, s_sc, p_sc, ot, o_all):
    length = zb.shape[0]
    half = length // 2
    size = weight.shape[0] // 16
    for spot in range(16):
        source = (near, far)[spot // 8]
        target = pl.ds(pl.multiple_of(meta[26 + spot] * size, size), size)
        weight[target, :] = source[spot % 8 * size : (spot % 8 + 1) * size, :]
    qkv[...] = dot(zb[...], weight[...]).astype(BF16)
    lane = lax.broadcasted_iota(jnp.int32, (1, PAIR), 1)
    keys = qkv[:, PAIR : 2 * PAIR]
    zero = jnp.zeros_like(keys)
    km[0] = jnp.where(lane < HD, keys, zero)
    km[1] = jnp.where(lane < HD, zero, keys)
    vt[...] = qkv[:, 2 * PAIR :].T
    lse[...] = jnp.zeros_like(lse)
    allowed = lax.broadcasted_iota(jnp.int32, (BAND, BAND), 0) <= lax.broadcasted_iota(jnp.int32, (BAND, BAND), 1)
    for q_band in range(length // BAND):
        spots = slice(q_band * BAND, (q_band + 1) * BAND)
        queries = qkv[spots, :PAIR]
        for head in range(2):
            top = None
            for k_band in range(q_band + 1):
                rows = slice(k_band * BAND, (k_band + 1) * BAND)
                s = dot_t(km[head, rows, :], queries) * (HD ** -0.5 * LOG2E)
                if k_band == q_band:
                    s = jnp.where(allowed, s, 0.0)
                s_sc[rows, :] = s
                peak = jnp.max(jnp.abs(s), axis=0, keepdims=True)
                top = peak if top is None else jnp.maximum(top, peak)
            total = None
            for k_band in range(q_band + 1):
                rows = slice(k_band * BAND, (k_band + 1) * BAND)
                s = s_sc[rows, :]
                grow = jnp.exp2(s - top)
                shrink = jnp.exp2(-s - top)
                p_sc[rows, :] = (grow - shrink).astype(BF16)
                both = grow + shrink
                if k_band == q_band:
                    both = jnp.where(allowed, both, 0.0)
                part = jnp.sum(both, axis=0, keepdims=True)
                total = part if total is None else total + part
            end = (q_band + 1) * BAND
            mine = slice(head * HD, (head + 1) * HD)
            ot[mine, :] = dot(vt[mine, :end], p_sc[:end, :]) / total
            lse[head : head + 1, spots] = top + jnp.log2(0.5 * total)
        o_all[spots, :] = ot[...].T.astype(BF16)
    o_own[...] = o_all[half_at(meta[0], half), :]
    o_other[...] = o_all[half_at(1 - meta[0], half), :]


def attend_back(
    meta, qkv, o_own, o_other, d_own, d_other, lse, zt, g_own, g_other, keep, send, km, vm, kt, do, inner, dk, dv, dqt, dqkv
):
    length = qkv.shape[0]
    half = length // 2
    lane = lax.broadcasted_iota(jnp.int32, (1, PAIR), 1)
    low = lane < HD
    keys = qkv[:, PAIR : 2 * PAIR]
    values = qkv[:, 2 * PAIR :]
    zero = jnp.zeros_like(keys)
    km[0] = jnp.where(low, keys, zero)
    km[1] = jnp.where(low, zero, keys)
    vm[0] = jnp.where(low, values, zero)
    vm[1] = jnp.where(low, zero, values)
    kt[...] = keys.T
    pick = (
        lax.broadcasted_iota(jnp.int32, (8, PAIR), 1) // HD == lax.broadcasted_iota(jnp.int32, (8, PAIR), 0)
    ).astype(F32)
    for o_part, d_part, place in ((o_own, d_own, meta[0]), (o_other, d_other, 1 - meta[0])):
        do[half_at(place, half), :] = d_part[...]
        product = o_part[...].astype(F32) * d_part[...].astype(F32)
        inner[:, half_at(place, half)] = lax.dot_general(
            pick, product, (((1,), (1,)), ((), ())), preferred_element_type=F32, precision=lax.Precision.HIGHEST
        )
    allowed = lax.broadcasted_iota(jnp.int32, (BAND, BAND), 0) <= lax.broadcasted_iota(jnp.int32, (BAND, BAND), 1)
    small = jnp.zeros((BAND, PAIR), BF16)
    for q_band in range(length // BAND):
        spots = slice(q_band * BAND, (q_band + 1) * BAND)
        queries = qkv[spots, :PAIR]
        upstream = do[spots, :]
        for head in range(2):
            mine = slice(head * HD, (head + 1) * HD)
            q_mine = jnp.where(low, queries, small) if head == 0 else jnp.where(low, small, queries)
            d_mine = jnp.where(low, upstream, small) if head == 0 else jnp.where(low, small, upstream)
            base = lse[head : head + 1, spots] + 1.0
            mean = inner[head : head + 1, spots]
            for k_band in range(q_band + 1):
                rows = slice(k_band * BAND, (k_band + 1) * BAND)
                s = dot_t(km[head, rows, :], queries) * (HD ** -0.5 * LOG2E)
                dw = dot_t(vm[head, rows, :], upstream)
                if k_band == q_band:
                    s = jnp.where(allowed, s, 0.0)
                    dw = jnp.where(allowed, dw, 0.0)
                grow = jnp.exp2(s - base)
                shrink = jnp.exp2(-s - base)
                p = grow - shrink
                ds = ((grow + shrink) * dw - p * mean).astype(BF16)
                dv_part = dot(p.astype(BF16), d_mine)
                dk_part = dot(ds, q_mine)
                dq_part = dot(kt[mine, rows], ds)
                if q_band == k_band and head == 0:
                    dv[rows, :] = dv_part
                    dk[rows, :] = dk_part
                else:
                    dv[rows, :] += dv_part
                    dk[rows, :] += dk_part
                if k_band == 0:
                    dqt[mine, :] = dq_part
                else:
                    dqt[mine, :] += dq_part
        dqkv[spots, :PAIR] = (dqt[...].T * HD ** -0.5).astype(BF16)
    dqkv[:, PAIR : 2 * PAIR] = (dk[...] * HD ** -0.5).astype(BF16)
    dqkv[:, 2 * PAIR :] = dv[...].astype(BF16)
    g_own[...] = dqkv[half_at(meta[0], half), :]
    g_other[...] = dqkv[half_at(1 - meta[0], half), :]
    middle = keep.shape[0]
    send[...] = dot(zt[middle:, :], dqkv[...]).astype(BF16)
    keep[...] = dot(zt[:middle, :], dqkv[...]).astype(BF16)


def project_out(meta, own, o0, o1, o2, r0, r1, r2, gains, weight, resid, zb, zt, mt, mixed, turned):
    for spot, (mine, other) in enumerate(((o0, r0), (o1, r1), (o2, r2))):
        mixed[:, pl.ds(pl.multiple_of(meta[0] * 3 * PAIR + spot * PAIR, PAIR), PAIR)] = mine[...]
        mixed[:, pl.ds(pl.multiple_of((1 - meta[0]) * 3 * PAIR + spot * PAIR, PAIR), PAIR)] = other[...]
    summed = own[...].astype(F32) + dot(mixed[...], weight[...])
    resid[...] = summed
    z = (standardize(summed)[0] * gains[1:2, :].astype(F32)).astype(BF16)
    zb[...] = z
    size = turned.shape[0] // 16
    turned[...] = z.T
    rows_in_order(meta, turned, zt, 16, size)
    turned[...] = mixed[...].T
    rows_in_order(meta, turned, mt, 16, size)


def feed(
    meta, zb, zt, up, down, upstream, resid, out, g_out, up_keep, up_send, down_keep, down_send, feed_acc, g_acc, turned, picked
):
    step = pl.program_id(0)
    v = dot(zb[...], up[...])
    root = 0.7978845608028654
    square = v * v
    t = jnp.tanh(root * v * (1.0 + 0.044715 * square))
    cdf = 0.5 * (1.0 + t)
    active = (v * cdf).astype(BF16)
    slope = cdf + v * (0.5 * root) * (1.0 - t * t) * (1.0 + 0.134145 * square)
    dpre = (dot_t(upstream[...], down[...]) * slope).astype(BF16)
    feed_part = dot(active, down[...])
    g_part = dot_t(dpre, up[...])
    middle = up_keep.shape[0]
    up_keep[...] = dot(zt[:middle, :], dpre).astype(BF16)
    up_send[...] = dot(zt[middle:, :], dpre).astype(BF16)
    turned[...] = active.T
    size = turned.shape[0] // 8
    for spot in range(8):
        block = meta[17 + spot]
        picked[spot * size : (spot + 1) * size, :] = turned[pl.ds(pl.multiple_of(block * size, size), size), :]
    middle = turned.shape[0] // 2
    down_keep[0] = dot(picked[:middle, :], upstream[...]).astype(BF16)
    down_send[0] = dot(picked[middle:, :], upstream[...]).astype(BF16)

    @pl.when(step == 0)
    def _():
        feed_acc[...] = feed_part
        g_acc[...] = g_part

    @pl.when(step > 0)
    def _():
        feed_acc[...] += feed_part
        g_acc[...] += g_part

    @pl.when(step == pl.num_programs(0) - 1)
    def _():
        out[...] = (resid[...] + feed_acc[...]).astype(BF16)
        g_out[...] = g_acc[...]


def branch_back(meta, g, resid, upstream, gains, weight, dresid, db, s0, s1, s2, m0, m1, m2):
    z, rstd = standardize(resid[...])
    grad = upstream[...].astype(F32) + norm_back(z, rstd, g[...] * gains[1:2, :].astype(F32))
    dresid[...] = grad
    low = grad.astype(BF16)
    db[...] = low
    for side, targets in ((1 - meta[0], (s0, s1, s2)), (meta[0], (m0, m1, m2))):
        part = dot_t(low, weight[half_at(side, 3 * PAIR), :]).astype(BF16)
        for spot, target in enumerate(targets):
            target[...] = part[:, spot * PAIR : (spot + 1) * PAIR]


def output_back(meta, mt, db, keep, send):
    middle = keep.shape[0]
    send[...] = dot(mt[middle:, :], db[...]).astype(BF16)
    keep[...] = dot(mt[:middle, :], db[...]).astype(BF16)


def token_back(meta, g0, g1, g2, w0, w1, w2, out):
    out[...] = (dot_t(g0[...], w0[...]) + dot_t(g1[...], w1[...]) + dot_t(g2[...], w2[...])).astype(out.dtype)


def input_back(meta, own, mine, other, dresid, gains, out):
    z, rstd = standardize(own[...].astype(F32))
    g = (mine[...] + other[...].astype(F32)) * gains[0:1, :].astype(F32)
    out[...] = dresid[...] + norm_back(z, rstd, g)


SWAP = [(0, 1), (1, 0)]


def flipped(array, parts, bit):
    return lax.ppermute(array, "fsdp", [(spot, spot ^ bit) for spot in range(parts)])


def rounded_sum(terms):
    total = terms[0].astype(F32)
    for term in terms[1:]:
        total = total + term.astype(F32)
    return total.astype(BF16)


def reduced(keep, send, parts, place, steps):
    rows = keep.shape[0] // 8
    shape = (2, 2, 2, rows, keep.shape[1])
    terms = [keep.reshape(shape), flipped(send, parts, 1).reshape(shape)]
    for step in steps:
        if step == "seq":
            width = terms[0].shape[4] // 2
            away = [lax.dynamic_slice_in_dim(term, (1 - place) * width, width, 4) for term in terms]
            terms = [lax.dynamic_slice_in_dim(term, place * width, width, 4) for term in terms]
            came = lax.ppermute(rounded_sum(away), "seq", SWAP)
        else:
            axis = {8: 0, 4: 1, 2: 2}[step]
            away = [lax.slice_in_dim(term, 1, 2, axis=axis) for term in terms]
            terms = [lax.slice_in_dim(term, 0, 1, axis=axis) for term in terms]
            came = flipped(rounded_sum(away), parts, step)
        terms.append(came)
    return rounded_sum(terms).reshape(rows, -1)


def sides(mine, place):
    pair = jnp.stack([mine, lax.ppermute(mine, "seq", SWAP)])
    return jnp.where(place == 0, pair, pair[::-1])


def body(block_input, lead_gain, joint_weight, output_weight, tail_gain, up_weight, down_weight, cotangent):
    rows, triple = joint_weight.shape
    dim = block_input.shape[2]
    wide = up_weight.shape[1]
    half = block_input.shape[1]
    length = 2 * half
    parts = dim // rows
    group = triple // 6
    place = lax.axis_index("seq")
    me = lax.axis_index("fsdp")
    direct = parts == 16
    base = me if direct else jnp.zeros_like(me)
    spots = jnp.arange(16, dtype=jnp.int32)
    order = base ^ ((spots % 8) * 2 + spots // 8)
    few = jnp.arange(8, dtype=jnp.int32)
    inner_order = (base % 8) ^ ((few % 4) * 2 + few // 4)
    eight = (few % 2) * 8 + (few // 2 % 2) * 4 + few // 4 * 2
    arrived = base ^ jnp.concatenate([eight, eight ^ 1]) if direct else spots
    meta = jnp.concatenate([place[None], order, inner_order, (base // 8)[None], arrived]).astype(jnp.int32)

    joint_own = lax.dynamic_index_in_dim(joint_weight.reshape(rows, 3, 2, group), place, 2, keepdims=False)
    joint_own = joint_own.reshape(rows, 3, 3, PAIR).transpose(2, 0, 1, 3).reshape(3, rows, 3 * PAIR)
    up_turned = up_weight.reshape(rows, parts, 4, rows).transpose(0, 2, 1, 3).reshape(rows, wide)
    down_turned = down_weight.reshape(4, rows, dim).transpose(1, 0, 2).reshape(rows, 4 * dim)
    rest_shard = jnp.concatenate([output_weight, up_turned, down_turned], axis=1)

    own = block_input[0]
    upstream = cotangent[0]
    rest = lax.all_gather(rest_shard, "fsdp", axis=0, tiled=True)
    both_gains = jnp.stack([lead_gain, tail_gain])
    if direct:
        gains = lax.dynamic_update_slice(jnp.zeros((2, dim), BF16), both_gains, (0, me * rows))
        for bit in (1, 2, 4, 8):
            gains = gains + flipped(gains, parts, bit)
    else:
        gains = lax.all_gather(both_gains, "fsdp", axis=1, tiled=True)
    other = lax.ppermute(own, "seq", SWAP)
    firsts = []
    for pair in range(3):
        block = joint_own[pair]
        if direct:
            for bit in (8, 4, 2):
                block = jnp.concatenate([block, flipped(block, parts, bit)], axis=0)
            firsts.append((block, flipped(block, parts, 1)))
        else:
            block = lax.all_gather(block, "fsdp", axis=0, tiled=True)
            firsts.append((block[: dim // 2], block[dim // 2 :]))

    zb, zt = call(
        first_norm, "first_norm", (shaped(length, dim), shaped(dim, length)), 3, [pltpu.VMEM((dim, length), BF16)]
    )(meta, own, other, gains)

    kept = []
    received = []
    for pair in range(3):
        qkv, o_own, o_other, lse, weight = call(
            attend,
            "attend",
            (
                shaped(length, 3 * PAIR),
                shaped(half, PAIR),
                shaped(half, PAIR),
                shaped(8, length, dtype=F32),
                shaped(dim, 3 * PAIR),
            ),
            3,
            [
                pltpu.VMEM((2, length, PAIR), BF16),
                pltpu.VMEM((PAIR, length), BF16),
                pltpu.VMEM((length, BAND), F32),
                pltpu.VMEM((length, BAND), BF16),
                pltpu.VMEM((PAIR, BAND), F32),
                pltpu.VMEM((length, PAIR), BF16),
            ],
            took=8,
        )(meta, zb, *firsts[pair])
        kept.append((qkv, o_own, o_other, lse, weight))
        received.append(lax.ppermute(o_other, "seq", SWAP))

    rest_block = pl.BlockSpec((dim, dim), lambda *_: (0, 0))
    resid, zb_two, zt_two, mixed_t = pl.pallas_call(
        project_out,
        name="project_out",
        grid=(1,),
        out_shape=(shaped(half, dim, dtype=F32), shaped(half, dim), shaped(dim, half), shaped(dim, half)),
        in_specs=[SMEM] + [VMEM] * 8 + [rest_block],
        out_specs=[VMEM] * 4,
        cost_estimate=cost(5),
        scratch_shapes=[pltpu.VMEM((half, dim), BF16), pltpu.VMEM((dim, half), BF16)],
        compiler_params=pltpu.CompilerParams(vmem_limit_bytes=LIMIT),
    )(meta, own, *[k[1] for k in kept], *received, gains, rest)

    chunk = dim // 2
    steps = wide // chunk
    whole = lambda *dims: pl.BlockSpec(dims, lambda *_: (0,) * len(dims))
    out, g_two, up_keep, up_send, down_keep, down_send = pl.pallas_call(
        feed,
        name="feed",
        out_shape=(
            shaped(half, dim),
            shaped(half, dim, dtype=F32),
            shaped(dim // 2, wide),
            shaped(dim // 2, wide),
            shaped(2, dim // 4, 4 * dim),
            shaped(2, dim // 4, 4 * dim),
        ),
        grid_spec=pltpu.PrefetchScalarGridSpec(
            num_scalar_prefetch=1,
            grid=(steps,),
            in_specs=[
                whole(half, dim),
                whole(dim, half),
                pl.BlockSpec((dim, chunk), lambda m, meta: (0, 2 + m // 2 * 2 + (m % 2) ^ meta[25])),
                pl.BlockSpec((chunk, dim), lambda m, meta: ((m % 2) ^ meta[25], 5 + m // 2)),
                whole(half, dim),
                whole(half, dim),
            ],
            out_specs=[
                whole(half, dim),
                whole(half, dim),
                pl.BlockSpec((dim // 2, chunk), lambda m, meta: (0, m // 2 * 2 + (m % 2) ^ meta[25])),
                pl.BlockSpec((dim // 2, chunk), lambda m, meta: (0, m // 2 * 2 + (m % 2) ^ meta[25])),
                pl.BlockSpec((1, dim // 4, dim), lambda m, meta: (m % 2, 0, m // 2)),
                pl.BlockSpec((1, dim // 4, dim), lambda m, meta: (m % 2, 0, m // 2)),
            ],
            scratch_shapes=[
                pltpu.VMEM((half, dim), F32),
                pltpu.VMEM((half, dim), F32),
                pltpu.VMEM((chunk, half), BF16),
                pltpu.VMEM((chunk, half), BF16),
            ],
        ),
        compiler_params=pltpu.CompilerParams(vmem_limit_bytes=LIMIT, dimension_semantics=("arbitrary",)),
        cost_estimate=cost(29),
    )(meta, zb_two, zt_two, rest, rest, upstream, resid)

    dresid, db, *dm = pl.pallas_call(
        branch_back,
        name="branch_back",
        grid=(1,),
        out_shape=(shaped(half, dim, dtype=F32), shaped(half, dim)) + (shaped(half, PAIR),) * 6,
        in_specs=[SMEM] + [VMEM] * 4 + [rest_block],
        out_specs=[VMEM] * 8,
        compiler_params=pltpu.CompilerParams(vmem_limit_bytes=LIMIT),
        cost_estimate=cost(5),
    )(meta, g_two, resid, upstream, gains, rest)
    incoming = [lax.ppermute(part, "seq", SWAP) for part in dm[:3]]
    halves = (shaped(dim // 2, dim), shaped(dim // 2, dim))
    output_keep, output_send = call(output_back, "output_back", halves, 2)(meta, mixed_t, db)

    token_own = []
    token_other = []
    joint_parts = []
    for pair in range(3):
        qkv, o_own, o_other, lse, weight = kept[pair]
        g_own, g_other, keep, send = call(
            attend_back,
            "attend_back",
            (
                shaped(half, 3 * PAIR),
                shaped(half, 3 * PAIR),
                shaped(dim // 2, 3 * PAIR),
                shaped(dim // 2, 3 * PAIR),
            ),
            7,
            [
                pltpu.VMEM((2, length, PAIR), BF16),
                pltpu.VMEM((2, length, PAIR), BF16),
                pltpu.VMEM((PAIR, length), BF16),
                pltpu.VMEM((length, PAIR), BF16),
                pltpu.VMEM((8, length), F32),
                pltpu.VMEM((length, PAIR), F32),
                pltpu.VMEM((length, PAIR), F32),
                pltpu.VMEM((PAIR, BAND), F32),
                pltpu.VMEM((length, 3 * PAIR), BF16),
            ],
            took=9,
        )(meta, qkv, o_own, o_other, dm[3 + pair], incoming[pair], lse, zt)
        token_own.append(g_own)
        token_other.append(g_other)
        joint_parts.append((keep, send))

    weights = [k[4] for k in kept]
    (sent,) = call(token_back, "token_back", (shaped(half, dim),), 6)(meta, *token_other, *weights)
    other_part = lax.ppermute(sent, "seq", SWAP)
    (own_part,) = call(token_back, "token_back_own", (shaped(half, dim, dtype=F32),), 6)(meta, *token_own, *weights)
    (input_grad,) = call(input_back, "input_back", (shaped(half, dim, dtype=F32),), 5)(
        meta, own, own_part, other_part, dresid, gains
    )

    down_keep, down_send = (part.reshape(dim // 2, 4 * dim) for part in (down_keep, down_send))

    if direct:
        up_sum, down_sum, output_sum = (
            sides(reduced(keep, send, parts, place, steps), place).transpose(1, 0, 2).reshape(rows, -1).astype(F32)
            for keep, send, steps in (
                (up_keep, up_send, (2, "seq", 4, 8)),
                (down_keep, down_send, ("seq", 4, 2, 8)),
                (output_keep, output_send, (4, 2, "seq", 8)),
            )
        )
        joint_mine = jnp.stack(
            [reduced(keep, send, parts, place, (2, 4, 8)) for keep, send in joint_parts]
        )
    else:

        def scattered(keep, send):
            part = jnp.stack([keep, send]).reshape(2, 8, dim // 16, -1).transpose(1, 0, 2, 3).reshape(dim, -1)
            return lax.psum_scatter(part, "fsdp", scatter_dimension=0, tiled=True)

        up_sum, down_sum, output_sum = (
            lax.psum(scattered(keep, send), "seq").astype(F32)
            for keep, send in ((up_keep, up_send), (down_keep, down_send), (output_keep, output_send))
        )
        joint_mine = jnp.stack([scattered(keep, send) for keep, send in joint_parts])
    joint_sides = sides(joint_mine, place).astype(F32)
    joint_grad = joint_sides.reshape(2, 3, rows, 3, PAIR).transpose(2, 3, 0, 1, 4).reshape(rows, triple)
    lead_grad = jnp.sum(joint_grad * joint_weight.astype(F32), axis=1) / lead_gain.astype(F32)
    up_grad = up_sum.reshape(rows, 4, parts, rows).transpose(0, 2, 1, 3).reshape(rows, wide)
    tail_grad = jnp.sum(up_grad * up_weight.astype(F32), axis=1) / tail_gain.astype(F32)
    down_grad = down_sum.reshape(rows, 4, dim).transpose(1, 0, 2).reshape(4 * rows, dim)
    return (out[None], input_grad[None], lead_grad, joint_grad, output_sum, tail_grad, up_grad, down_grad)


def solution(mesh):
    split = P("fsdp", "seq", None)
    placed = (split, P("fsdp"), P("fsdp", None), P("fsdp", None), P("fsdp"), P("fsdp", None), P("fsdp", None), split)
    return jax.shard_map(
        body,
        mesh=mesh,
        in_specs=placed,
        out_specs=(split, split, P("fsdp"), P("fsdp", None), P("fsdp", None), P("fsdp"), P("fsdp", None), P("fsdp", None)),
        check_vma=False,
    )
```

```python
import functools

import jax
import jax.numpy as jnp
from jax import lax
from jax.experimental import pallas as pl
from jax.experimental.pallas import tpu as pltpu
from jax.sharding import PartitionSpec as P

HD = 64
EPS = 1e-05
PAIR = 2 * HD
BAND = 256
LOG2E = 1.4426950408889634
LIMIT = 56 << 20
F32 = jnp.float32
BF16 = jnp.bfloat16

VMEM = pl.BlockSpec(memory_space=pltpu.VMEM)
SMEM = pl.BlockSpec(memory_space=pltpu.SMEM)
ANY = pl.BlockSpec(memory_space=pl.ANY)


def dot(left, right):
    return jnp.dot(left, right, preferred_element_type=F32)


def dot_t(left, right):
    return lax.dot_general(left, right, (((1,), (1,)), ((), ())), preferred_element_type=F32)


def shaped(*dims, dtype=BF16):
    return jax.ShapeDtypeStruct(dims, dtype)


def cost(microseconds):
    return pl.CostEstimate(flops=int(microseconds * 1e7), transcendentals=0, bytes_accessed=int(microseconds * 3e4))


def waiting(kernel, fixed, after):
    def run(*refs):
        kernel(*refs[:fixed], *refs[fixed + after :])

    return run


def whole(*dims):
    return pl.BlockSpec(dims, lambda *_: (0,) * len(dims))


def column(rows, columns, pick=lambda step: step):
    return pl.BlockSpec((rows, columns), lambda *steps: (0, pick(*steps)))


def call(kernel, name, outs, meta, inputs, scratch=(), took=4, after=(), grid=(), specs=None, out_specs=None):
    return pl.pallas_call(
        waiting(kernel, 1 + len(inputs), len(after)),
        name=name,
        grid=grid,
        out_shape=outs,
        in_specs=[SMEM] + list(specs or [VMEM] * len(inputs)) + [ANY] * len(after),
        out_specs=list(out_specs or [VMEM] * len(outs)),
        scratch_shapes=list(scratch),
        compiler_params=pltpu.CompilerParams(vmem_limit_bytes=LIMIT),
        cost_estimate=cost(took),
    )(meta, *inputs, *after)


def standardize(values):
    center = values - jnp.mean(values, axis=-1, keepdims=True)
    spread = jnp.mean(center * center, axis=-1, keepdims=True)
    rstd = lax.rsqrt(spread + EPS)
    return center * rstd, rstd


def norm_back(z, rstd, g):
    return (g - jnp.mean(g, axis=-1, keepdims=True) - z * jnp.mean(g * z, axis=-1, keepdims=True)) * rstd


def half_at(index, size):
    return pl.ds(pl.multiple_of(index * size, size), size)


def rows_in_order(meta, source, target):
    size = source.shape[0] // 16
    for spot in range(16):
        rows = pl.ds(pl.multiple_of(meta[1 + spot] * size, size), size)
        target[spot * size : (spot + 1) * size, :] = source[rows, :]


def placed(meta, near, far, target):
    size = target.shape[0] // 16
    for spot in range(16):
        source = (near, far)[spot // 8]
        rows = pl.ds(pl.multiple_of(meta[17 + spot] * size, size), size)
        target[rows, :] = source[spot % 8 * size : (spot % 8 + 1) * size, :]


def first_norm(meta, own, other, z):
    half = own.shape[0]
    for source, place in ((own, meta[0]), (other, 1 - meta[0])):
        z[half_at(place, half), :] = standardize(source[...].astype(F32))[0]


def first_scale(meta, z, near, far, zb, gains, columns):
    placed(meta, near, far, columns)
    gains[...] = columns[...].T[:16, :]
    zb[...] = (z[...] * gains[0:1, :].astype(F32)).astype(BF16)


def turn(meta, zb, zt, turned):
    turned[...] = zb[...].T
    rows_in_order(meta, turned, zt)


def mix(meta, mine, other, mixed, mt, turned):
    width = mine.shape[1]
    for side, source in ((meta[0], mine), (1 - meta[0], other)):
        mixed[:, half_at(side, width)] = source[...]
    turned[...] = mixed[...].T
    rows_in_order(meta, turned, mt)


def attend(meta, zb, near, far, qkv, o_own, o_other, lse, weight, km, vt, s_sc, ot, o_all):
    length = zb.shape[0]
    half = length // 2
    placed(meta, near, far, weight)
    qkv[...] = dot(zb[...], weight[...]).astype(BF16)
    lane = lax.broadcasted_iota(jnp.int32, (1, PAIR), 1)
    keys = qkv[:, PAIR : 2 * PAIR]
    zero = jnp.zeros_like(keys)
    km[0] = jnp.where(lane < HD, keys, zero)
    km[1] = jnp.where(lane < HD, zero, keys)
    vt[...] = qkv[:, 2 * PAIR :].T
    lse[0] = jnp.zeros(lse.shape[1:], F32)
    allowed = lax.broadcasted_iota(jnp.int32, (BAND, BAND), 0) <= lax.broadcasted_iota(jnp.int32, (BAND, BAND), 1)

    def q_step(q_band, _):
        spots = half_at(q_band, BAND)
        queries = qkv[spots, :PAIR]

        def score(k_band, tops, diagonal):
            rows = half_at(k_band, BAND)
            peaks = []
            for head in range(2):
                s = dot_t(km[head, rows, :], queries) * (HD ** -0.5 * LOG2E)
                if diagonal:
                    s = jnp.where(allowed, s, 0.0)
                s_sc[head, rows, :] = s
                peaks.append(jnp.maximum(tops[head], jnp.max(jnp.abs(s), axis=0, keepdims=True)))
            return tuple(peaks)

        def weigh(k_band, carry, tops, diagonal):
            rows = half_at(k_band, BAND)
            results = []
            for head, (total, out) in enumerate(carry):
                s = s_sc[head, rows, :]
                grow = jnp.exp2(s - tops[head])
                shrink = jnp.exp2(-s - tops[head])
                both = grow + shrink
                if diagonal:
                    both = jnp.where(allowed, both, 0.0)
                part = dot(vt[head * HD : (head + 1) * HD, rows], (grow - shrink).astype(BF16))
                results.append((total + jnp.sum(both, axis=0, keepdims=True), out + part))
            return tuple(results)

        none = jnp.zeros((1, BAND), F32)
        tops = score(q_band, (none, none), True)
        tops = lax.fori_loop(0, q_band, lambda k_band, tops: score(k_band, tops, False), tops)
        start = (none, jnp.zeros((HD, BAND), F32))
        carry = weigh(q_band, (start, start), tops, True)
        carry = lax.fori_loop(0, q_band, lambda k_band, carry: weigh(k_band, carry, tops, False), carry)
        for head, (total, out) in enumerate(carry):
            ot[head * HD : (head + 1) * HD, :] = out / total
            lse[0, head : head + 1, spots] = tops[head] + jnp.log2(0.5 * total)
        o_all[spots, :] = ot[...].T.astype(BF16)
        return 0

    lax.fori_loop(0, length // BAND, q_step, 0)
    o_own[...] = o_all[half_at(meta[0], half), :]
    o_other[...] = o_all[half_at(1 - meta[0], half), :]


def attend_back(last, meta, qkv, o_own, o_other, d_own, d_other, lse, zt, weight, *refs):
    extra, refs = refs[: 3 * last], refs[3 * last :]
    keep, send, *outs = refs[: 3 + last]
    km, vm, kt, do, inner, dk, dv, dqt, dqkv, total, s_sc, w_sc, p_sc, ds_sc = refs[3 + last :]
    length = qkv.shape[0]
    half = length // 2
    lane = lax.broadcasted_iota(jnp.int32, (1, PAIR), 1)
    low = lane < HD
    keys = qkv[:, PAIR : 2 * PAIR]
    values = qkv[:, 2 * PAIR :]
    zero = jnp.zeros_like(keys)
    km[0] = jnp.where(low, keys, zero)
    km[1] = jnp.where(low, zero, keys)
    vm[0] = jnp.where(low, values, zero)
    vm[1] = jnp.where(low, zero, values)
    kt[...] = keys.T
    pick = (
        lax.broadcasted_iota(jnp.int32, (8, PAIR), 1) // HD == lax.broadcasted_iota(jnp.int32, (8, PAIR), 0)
    ).astype(F32)
    for o_part, d_part, place in ((o_own, d_own, meta[0]), (o_other, d_other, 1 - meta[0])):
        do[half_at(place, half), :] = d_part[...]
        product = o_part[...].astype(F32) * d_part[...].astype(F32)
        inner[:, half_at(place, half)] = lax.dot_general(
            pick, product, (((1,), (1,)), ((), ())), preferred_element_type=F32, precision=lax.Precision.HIGHEST
        )
    allowed = lax.broadcasted_iota(jnp.int32, (BAND, BAND), 0) <= lax.broadcasted_iota(jnp.int32, (BAND, BAND), 1)
    for q_band in range(length // BAND):
        spots = slice(q_band * BAND, (q_band + 1) * BAND)
        end = (q_band + 1) * BAND
        queries = qkv[spots, :PAIR]
        upstream = do[spots, :]
        small = jnp.zeros_like(queries)
        for head in range(2):
            mine = slice(head * HD, (head + 1) * HD)
            q_mine = jnp.where(low, queries, small) if head == 0 else jnp.where(low, small, queries)
            d_mine = jnp.where(low, upstream, small) if head == 0 else jnp.where(low, small, upstream)
            base = lse[0, head : head + 1, spots] + 1.0
            mean = inner[head : head + 1, spots]
            s_sc[head, :end, :] = dot_t(km[head, :end, :], queries)
            w_sc[head, :end, :] = dot_t(vm[head, :end, :], upstream)
            for k_band in range(q_band + 1):
                rows = slice(k_band * BAND, (k_band + 1) * BAND)
                s = s_sc[head, rows, :] * (HD ** -0.5 * LOG2E)
                dw = w_sc[head, rows, :]
                if k_band == q_band:
                    s = jnp.where(allowed, s, 0.0)
                    dw = jnp.where(allowed, dw, 0.0)
                grow = jnp.exp2(s - base)
                shrink = jnp.exp2(-s - base)
                p = grow - shrink
                p_sc[head, rows, :] = p.astype(BF16)
                ds_sc[head, rows, :] = ((grow + shrink) * dw - p * mean).astype(BF16)
            dv_part = dot(p_sc[head, :end, :], d_mine)
            dk_part = dot(ds_sc[head, :end, :], q_mine)
            dqt[mine, :] = dot(kt[mine, :end], ds_sc[head, :end, :])
            old = q_band * BAND if head == 0 else end
            if old:
                dv[:old, :] += dv_part[:old]
                dk[:old, :] += dk_part[:old]
            if head == 0:
                dv[old:end, :] = dv_part[old:]
                dk[old:end, :] = dk_part[old:]
        dqkv[spots, :PAIR] = (dqt[...].T * HD ** -0.5).astype(BF16)
    dqkv[:, PAIR : 2 * PAIR] = (dk[...] * HD ** -0.5).astype(BF16)
    dqkv[:, 2 * PAIR :] = dv[...].astype(BF16)
    middle = keep.shape[0]
    start = keep.shape[1] - 3 * PAIR
    send[:, start:] = dot(zt[middle:, :], dqkv[...]).astype(BF16)
    keep[:, start:] = dot(zt[:middle, :], dqkv[...]).astype(BF16)
    part = dot_t(dqkv[...], weight[...])
    if last:
        keep[:, :start] = extra[0][...]
        send[:, :start] = extra[1][...]
        total[...] = extra[2][...] + part
        away, mine_out = outs
        away[...] = total[half_at(1 - meta[0], half), :].astype(BF16)
        mine_out[...] = total[half_at(meta[0], half), :]
    else:
        added(pl.program_id(0), outs[0], None, part)


def added(step, total, first, part):
    @pl.when(step == 0)
    def _():
        total[...] = part if first is None else first[...] + part

    @pl.when(step > 0)
    def _():
        total[...] += part


def project_out(meta, own, mixed, gains, weight, resid, zb, natural, zt):
    summed = own[...].astype(F32) + dot(mixed[...], weight[...])
    resid[...] = summed
    z = (standardize(summed)[0] * gains[1:2, :].astype(F32)).astype(BF16)
    zb[...] = z
    natural[...] = z.T
    rows_in_order(meta, natural, zt)


def feed(split, meta, zb, zt, up, down, upstream, before, *refs):
    g_before, refs = (refs[0], refs[1:]) if split else (None, refs)
    out, g_total, *grads, total, active, dpre, turned, picked = refs
    step = pl.program_id(0)
    width = active.shape[1]
    root = 0.7978845608028654
    for part in range(3):
        mine = slice(part * width // 3, (part + 1) * width // 3)
        v = dot(zb[...], up[:, mine])
        slope_in = dot_t(upstream[...], down[mine, :])
        square = v * v
        t = jnp.tanh(root * v * (1.0 + 0.044715 * square))
        cdf = 0.5 * (1.0 + t)
        active[:, mine] = (v * cdf).astype(BF16)
        slope = cdf + v * (0.5 * root) * (1.0 - t * t) * (1.0 + 0.134145 * square)
        dpre[:, mine] = (slope_in * slope).astype(BF16)
        turned[mine, :] = active[:, mine].T
    added(step, total, before, dot(active[...], down[...]))
    added(step, g_total, g_before, dot_t(dpre[...], up[...]))
    if split:
        rows_in_order(meta, turned, picked)
        size = width // 2
        for spot in range(2):
            mine = slice(spot * size, (spot + 1) * size)
            grads[spot][...] = dot(zt[mine, :], dpre[...]).astype(BF16)
            grads[2 + spot][...] = dot(picked[mine, :], upstream[...]).astype(BF16)
    else:
        grads[0][:, :width] = dot(zt[...], dpre[...]).astype(BF16)
        grads[0][:, width:] = dot(turned[...], upstream[...]).astype(BF16)

    @pl.when(step == pl.num_programs(0) - 1)
    def _():
        out[...] = total[...].astype(out.dtype)


def branch_back(meta, g, resid, upstream, gains, weight, dresid, db, away, mine):
    z, rstd = standardize(resid[...])
    grad = upstream[...].astype(F32) + norm_back(z, rstd, g[...] * gains[1:2, :].astype(F32))
    dresid[...] = grad
    low = grad.astype(BF16)
    db[...] = low
    for side, target in ((1 - meta[0], away), (meta[0], mine)):
        target[...] = dot_t(low, weight[half_at(side, 3 * PAIR), :]).astype(BF16)


def output_back(meta, mt, db, keep, send):
    middle = keep.shape[0]
    send[...] = dot(mt[middle:, :], db[...]).astype(BF16)
    keep[...] = dot(mt[:middle, :], db[...]).astype(BF16)


def input_back(meta, own, mine, other, dresid, gains, out):
    z, rstd = standardize(own[...].astype(F32))
    g = (mine[...] + other[...].astype(F32)) * gains[0:1, :].astype(F32)
    out[...] = dresid[...] + norm_back(z, rstd, g)


def row_sums(values):
    ones = jnp.ones((8, values.shape[1]), F32)
    sums = lax.dot_general(
        ones, values, (((1,), (1,)), ((), ())), preferred_element_type=F32, precision=lax.Precision.HIGHEST
    )
    return sums[0:1, :]


def joint_out(meta, own, other, weight, gain, grad, gain_grad):
    for side, source in ((meta[0], own), (1 - meta[0], other)):
        for pair in range(3):
            for kind in range(3):
                columns = pl.ds(pl.multiple_of((kind * 6 + side * 3 + pair) * PAIR, PAIR), PAIR)
                at = (pair * 3 + kind) * PAIR
                grad[:, columns] = source[:, at : at + PAIR].astype(F32)
    gain_grad[...] = row_sums(grad[...] * weight[...].astype(F32)) / gain[...].astype(F32)


def feed_out(split, meta, first, first_too, last, last_too, weight, gain, up, down, output, gain_grad):
    rows, dim = output.shape
    output[...] = last[:, -dim:].astype(F32) + last_too[:, -dim:].astype(F32)
    for k in range(4):
        parts = []
        for kind in range(2):
            if k < 2 or not split:
                one, two = (first, first_too) if k < 2 else (last, last_too)
                at = ((2 * k + kind) if k < 2 else (2 * kind + k - 2)) * dim
                parts.append(one[:, at : at + dim].astype(F32) + two[:, at : at + dim].astype(F32))
            else:
                at = kind * dim
                parts.append(jnp.where(meta[0] == k - 2, last[:, at : at + dim], last_too[:, at : at + dim]).astype(F32))
        for owner in range(dim // rows):
            up[:, (4 * owner + k) * rows : (4 * owner + k + 1) * rows] = parts[0][:, owner * rows : (owner + 1) * rows]
        down[k * rows : (k + 1) * rows, :] = parts[1]
    gain_grad[...] = row_sums(up[...] * weight[...].astype(F32)) / gain[...].astype(F32)


SWAP = [(0, 1), (1, 0)]


def flipped(array, parts, bit):
    return lax.ppermute(array, "fsdp", [(spot, spot ^ bit) for spot in range(parts)])


def exchanged(blocks, parts):
    groups = [list(range(side, parts, 4)) for side in range(4)]
    return lax.all_to_all(blocks, "fsdp", 0, 0, axis_index_groups=groups, tiled=True)


def rounded_sum(terms):
    total = terms[0].astype(F32)
    for term in terms[1:]:
        total = total + term.astype(F32)
    return total.astype(BF16)


def pinned(array, mark):
    return lax.optimization_barrier((array, mark))[0]


class Reduction:
    def __init__(self, terms, parts, place):
        self.terms, self.parts, self.place = terms, parts, place

    def go(self, step):
        if step == "seq":
            width = self.terms[0].shape[3] // 2
            away = rounded_sum(
                [lax.dynamic_slice_in_dim(term, (1 - self.place) * width, width, 3) for term in self.terms]
            )
            self.terms = [lax.dynamic_slice_in_dim(term, self.place * width, width, 3) for term in self.terms]
            self.came = lax.ppermute(away, "seq", SWAP)
        else:
            away = rounded_sum([term[:, 1:] for term in self.terms])
            self.terms = [term[:, :1] for term in self.terms]
            self.came = flipped(away, self.parts, 2)
        return away

    def take(self, mark):
        self.terms.append(pinned(self.came, mark))


def body(block_input, lead_gain, joint_weight, output_weight, tail_gain, up_weight, down_weight, cotangent):
    rows, triple = joint_weight.shape
    dim = block_input.shape[2]
    wide = up_weight.shape[1]
    half = block_input.shape[1]
    length = 2 * half
    parts = dim // rows
    group = triple // 6
    chunk = dim // 2
    place = lax.axis_index("seq")
    me = lax.axis_index("fsdp")
    direct = parts == 16
    base = me if direct else jnp.zeros_like(me)
    spots = jnp.arange(16, dtype=jnp.int32)
    few = jnp.arange(8, dtype=jnp.int32)
    eight = (few % 2) * 8 + (few // 2 % 2) * 4 + few // 4 * 2
    meta = jnp.concatenate(
        [
            place[None],
            spots % 8 // 2 * 4 + ((base % 4) ^ (spots % 2 * 2 + spots // 8)),
            base ^ jnp.concatenate([eight, eight ^ 1]) if direct else spots,
        ]
    ).astype(jnp.int32)

    joint_own = lax.dynamic_index_in_dim(joint_weight.reshape(rows, 3, 2, group), place, 2, keepdims=False)
    joint_own = joint_own.reshape(rows, 3, 3, PAIR).transpose(0, 2, 1, 3).reshape(rows, 3 * group)
    up_turned = up_weight.reshape(rows, parts, 4, rows).transpose(2, 0, 1, 3).reshape(4, rows, dim)
    down_turned = down_weight.reshape(4, rows, dim)
    hidden = [part[k] for k in range(4) for part in (up_turned, down_turned)]

    own = block_input[0]
    upstream = cotangent[0]
    rest = lax.all_gather(jnp.concatenate([output_weight, *hidden], axis=1), "fsdp", axis=0, tiled=True)
    other = lax.ppermute(own, "seq", SWAP)
    both_gains = jnp.pad(jnp.stack([lead_gain, tail_gain], axis=1), ((0, 0), (0, PAIR - 2)))
    first = jnp.concatenate([joint_own, both_gains], axis=1)
    if direct:
        for bit in (8, 4, 2):
            if bit == 2:
                first, other = lax.optimization_barrier((first, other))
            first = jnp.concatenate([first, flipped(first, parts, bit)], axis=0)
        firsts = (first, flipped(first, parts, 1))
    else:
        first = lax.all_gather(first, "fsdp", axis=0, tiled=True)
        firsts = (first[:chunk], first[chunk:])

    (z_one,) = call(first_norm, "first_norm", (shaped(length, dim, dtype=F32),), meta, (own, other), took=3)
    zb, gains = call(
        first_scale,
        "first_scale",
        (shaped(length, dim), shaped(16, dim)),
        meta,
        (z_one, *firsts),
        [pltpu.VMEM((dim, PAIR), BF16)],
        took=2,
        grid=(1,),
        specs=[VMEM] + [column(chunk, PAIR, lambda step: 9)] * 2,
    )
    triples = column(length, 3 * PAIR)
    pair_tokens = column(half, PAIR)
    lse_spec = pl.BlockSpec((1, 8, length), lambda step: (step, 0, 0))
    qkv, o_own, o_other, lse, weight = call(
        attend,
        "attend",
        (
            shaped(length, 9 * PAIR),
            shaped(half, group),
            shaped(half, group),
            shaped(3, 8, length, dtype=F32),
            shaped(dim, 9 * PAIR),
        ),
        meta,
        (zb, *firsts),
        [
            pltpu.VMEM((2, length, PAIR), BF16),
            pltpu.VMEM((PAIR, length), BF16),
            pltpu.VMEM((2, length, BAND), F32),
            pltpu.VMEM((PAIR, BAND), F32),
            pltpu.VMEM((length, PAIR), BF16),
        ],
        took=22,
        grid=(3,),
        specs=[whole(length, dim)] + [column(chunk, 3 * PAIR)] * 2,
        out_specs=[triples, pair_tokens, pair_tokens, lse_spec, column(dim, 3 * PAIR)],
    )
    o_came = lax.ppermute(o_other, "seq", SWAP)
    store = [pltpu.VMEM((dim, length), BF16)]
    (zt,) = call(turn, "turn", (shaped(dim, length),), meta, (zb,), store, took=2, after=[lse])
    mixed, mixed_t = call(
        mix,
        "mix",
        (shaped(half, dim), shaped(dim, half)),
        meta,
        (o_own, o_came),
        [pltpu.VMEM((dim, half), BF16)],
        took=2,
        after=[zt],
    )
    rest_block = column(dim, dim, lambda step: 0)
    total_f32 = shaped(half, dim, dtype=F32)
    resid, zb_two, zt_natural, zt_two = call(
        project_out,
        "project_out",
        (total_f32, shaped(half, dim)) + (shaped(dim, half),) * 2,
        meta,
        (own, mixed, gains, rest),
        grid=(1,),
        specs=[VMEM] * 3 + [rest_block],
    )

    tokens = whole(half, dim)
    turned = whole(dim, half)

    def feed_call(split, before):
        if split:
            grads = (shaped(chunk, 2 * dim),) * 4
            blocks = [column(chunk, dim)] * 4
        else:
            grads = (shaped(dim, 4 * dim),)
            blocks = [column(dim, 2 * dim)]
        return call(
            functools.partial(feed, split),
            "feed",
            (total_f32 if not split else shaped(half, dim), total_f32) + grads,
            meta,
            (zb_two, zt_two if split else zt_natural, rest, rest, upstream, *before),
            [
                pltpu.VMEM((half, dim), F32),
                pltpu.VMEM((half, dim), BF16),
                pltpu.VMEM((half, dim), BF16),
                pltpu.VMEM((dim, half), BF16),
                pltpu.VMEM((dim, half), BF16),
            ],
            took=15,
            grid=(2,),
            specs=[
                tokens,
                turned,
                column(dim, dim, lambda k: 1 + 4 * split + 2 * k),
                column(dim, dim, lambda k: 2 + 4 * split + 2 * k),
            ]
            + [tokens] * (1 + len(before)),
            out_specs=[tokens, tokens] + blocks,
        )

    total, g_two, grad_first = feed_call(0, (resid,))
    out, g_two, up_keep, up_send, down_keep, down_send = feed_call(1, (total, g_two))

    if direct:
        first_sum = lax.psum_scatter(grad_first, "fsdp", scatter_dimension=0, tiled=True)
        up_came = flipped(up_send, parts, 1)
        down_came = flipped(down_send, parts, 1)

    def blocks_of(part):
        return part.reshape(4, 2, rows, -1)

    dresid, db, dm_away, dm_mine = call(
        branch_back,
        "branch_back",
        (total_f32, shaped(half, dim)) + (shaped(half, group),) * 2,
        meta,
        (g_two, resid, upstream, gains, rest),
        grid=(1,),
        specs=[VMEM] * 4 + [rest_block],
    )
    dm_came = lax.ppermute(dm_away, "seq", SWAP)
    marks = []
    if direct:
        up_red = Reduction([blocks_of(part) for part in (up_keep, pinned(up_came, db))], parts, place)
        down_red = Reduction([blocks_of(part) for part in (down_keep, pinned(down_came, dm_came))], parts, place)
        marks = [up_red.go(2)]
    mixed_keep, mixed_send = call(
        output_back, "output_back", (shaped(chunk, dim),) * 2, meta, (mixed_t, db), after=marks
    )
    if direct:
        mixed_came = flipped(mixed_send, parts, 1)
        marks = [down_red.go("seq")]

    def attend_back_call(at, count, width, outs, out_specs, extra, after):
        last = bool(extra)
        shift = lambda step: step + at
        return call(
            functools.partial(attend_back, last),
            "attend_back",
            (shaped(chunk, width), shaped(chunk, width)) + outs,
            meta,
            (qkv, o_own, o_other, dm_mine, dm_came, lse, zt, weight, *extra),
            [
                pltpu.VMEM((2, length, PAIR), BF16),
                pltpu.VMEM((2, length, PAIR), BF16),
                pltpu.VMEM((PAIR, length), BF16),
                pltpu.VMEM((length, PAIR), BF16),
                pltpu.VMEM((8, length), F32),
                pltpu.VMEM((length, PAIR), F32),
                pltpu.VMEM((length, PAIR), F32),
                pltpu.VMEM((PAIR, BAND), F32),
                pltpu.VMEM((length, 3 * PAIR), BF16),
                pltpu.VMEM((length, dim), F32),
                pltpu.VMEM((2, length, BAND), F32),
                pltpu.VMEM((2, length, BAND), F32),
                pltpu.VMEM((2, length, BAND), BF16),
                pltpu.VMEM((2, length, BAND), BF16),
            ],
            took=10 * count,
            after=after,
            grid=(count,),
            specs=[column(length, 3 * PAIR, shift)]
            + [column(half, PAIR, shift)] * 4
            + [
                pl.BlockSpec((1, 8, length), lambda step: (step + at, 0, 0)),
                whole(dim, length),
                column(dim, 3 * PAIR, shift),
            ]
            + [whole(*part.shape) for part in extra],
            out_specs=[column(chunk, width // count)] * 2 + out_specs,
        )

    joint_keep, joint_send, token_total = attend_back_call(
        0, 2, 6 * PAIR, (shaped(length, dim, dtype=F32),), [whole(length, dim)], (), [mixed_keep] + marks
    )
    marks = [token_total]
    if direct:
        up_red.take(token_total)
        down_red.take(token_total)
        mixed_red = Reduction([blocks_of(part) for part in (mixed_keep, pinned(mixed_came, token_total))], parts, place)
        marks = [up_red.go("seq"), down_red.go(2), mixed_red.go(2)]
    joint_keep, joint_send, sent, own_part = attend_back_call(
        2, 1, 9 * PAIR, (shaped(half, dim), total_f32), [tokens] * 2, (joint_keep, joint_send, token_total), marks
    )
    other_part = lax.ppermute(sent, "seq", SWAP)
    marks = []
    if direct:
        joint_came = flipped(joint_send, parts, 1)
        last_sum = []
        for red in (up_red, down_red, mixed_red):
            red.take(sent)
            last_sum.append(rounded_sum(red.terms))
        joint_red = Reduction([blocks_of(part) for part in (joint_keep, joint_came)], parts, place)
        joint_away = joint_red.go(2)
        last_sum = pinned(jnp.concatenate(last_sum, axis=-1).reshape(4, rows, -1), joint_away)
        deep = me // 4
        last_parts = [lax.dynamic_index_in_dim(last_sum, deep, 0, keepdims=False)]
        for far in (1, 2, 3):
            away = lax.dynamic_index_in_dim(last_sum, deep ^ far, 0, keepdims=False)
            last_parts.append(flipped(away, parts, 4 * far))
        joint_red.take(joint_away)
        joint_sum = rounded_sum(joint_red.terms).reshape(4, rows, -1)
        marks = [first_sum, joint_sum]
        joint_sum = exchanged(joint_sum, parts)
    (input_grad,) = call(
        input_back, "input_back", (total_f32,), meta, (own, own_part, other_part, dresid, gains), after=marks
    )

    if direct:
        last_sum = rounded_sum(last_parts)
        joint_sum = jnp.sum(joint_sum.astype(F32), axis=0).astype(BF16)
    else:

        def scattered(keep, send):
            blocks = jnp.stack([keep, send]).reshape(2, 4, 2, dim // 16, -1).transpose(1, 2, 0, 3, 4).reshape(dim, -1)
            return lax.psum_scatter(blocks, "fsdp", scatter_dimension=0, tiled=True)

        first_sum = lax.psum_scatter(grad_first, "fsdp", scatter_dimension=0, tiled=True)
        last_sum = ((up_keep, up_send), (down_keep, down_send), (mixed_keep, mixed_send))
        last_sum = jnp.concatenate([scattered(*pair) for pair in last_sum], axis=1)
        joint_sum = scattered(joint_keep, joint_send)
    first_sum, last_sum, joint_sum = ((part, lax.ppermute(part, "seq", SWAP)) for part in (first_sum, last_sum, joint_sum))
    up_grad, down_grad, output_grad, tail_grad = call(
        functools.partial(feed_out, direct),
        "feed_out",
        (
            shaped(rows, wide, dtype=F32),
            shaped(4 * rows, dim, dtype=F32),
            shaped(rows, dim, dtype=F32),
            shaped(1, rows, dtype=F32),
        ),
        meta,
        (*first_sum, *last_sum, up_weight, tail_gain[None, :]),
    )
    joint_grad, lead_grad = call(
        joint_out,
        "joint_out",
        (shaped(rows, triple, dtype=F32), shaped(1, rows, dtype=F32)),
        meta,
        (*joint_sum, joint_weight, lead_gain[None, :]),
        took=2,
    )
    return (
        out[None],
        input_grad[None],
        lead_grad[0],
        joint_grad,
        output_grad,
        tail_grad[0],
        up_grad,
        down_grad,
    )


def solution(mesh):
    split = P("fsdp", "seq", None)
    placed = (split, P("fsdp"), P("fsdp", None), P("fsdp", None), P("fsdp"), P("fsdp", None), P("fsdp", None), split)
    return jax.shard_map(
        body,
        mesh=mesh,
        in_specs=placed,
        out_specs=(split, split, P("fsdp"), P("fsdp", None), P("fsdp", None), P("fsdp"), P("fsdp", None), P("fsdp", None)),
        check_vma=False,
    )
```

```python
import functools

import jax
import jax.numpy as jnp
from jax import lax
from jax.experimental import pallas as pl
from jax.experimental.pallas import tpu as pltpu
from jax.sharding import PartitionSpec as P

HD = 64
EPS = 1e-05
PAIR = 2 * HD
BAND = 256
LOG2E = 1.4426950408889634
LIMIT = 56 << 20
F32 = jnp.float32
BF16 = jnp.bfloat16

VMEM = pl.BlockSpec(memory_space=pltpu.VMEM)
SMEM = pl.BlockSpec(memory_space=pltpu.SMEM)
ANY = pl.BlockSpec(memory_space=pl.ANY)


def dot(left, right):
    return jnp.dot(left, right, preferred_element_type=F32)


def dot_t(left, right):
    return lax.dot_general(left, right, (((1,), (1,)), ((), ())), preferred_element_type=F32)


def shaped(*dims, dtype=BF16):
    return jax.ShapeDtypeStruct(dims, dtype)


def cost(microseconds):
    return pl.CostEstimate(flops=int(microseconds * 1e7), transcendentals=0, bytes_accessed=int(microseconds * 3e4))


def waiting(kernel, fixed, after):
    def run(*refs):
        kernel(*refs[:fixed], *refs[fixed + after :])

    return run


def whole(*dims):
    return pl.BlockSpec(dims, lambda *_: (0,) * len(dims))


def column(rows, columns, pick=lambda step: step):
    return pl.BlockSpec((rows, columns), lambda *steps: (0, pick(*steps)))


def call(kernel, name, outs, meta, inputs, scratch=(), took=4, after=(), grid=(), specs=None, out_specs=None):
    return pl.pallas_call(
        waiting(kernel, 1 + len(inputs), len(after)),
        name=name,
        grid=grid,
        out_shape=outs,
        in_specs=[SMEM] + list(specs or [VMEM] * len(inputs)) + [ANY] * len(after),
        out_specs=list(out_specs or [VMEM] * len(outs)),
        scratch_shapes=list(scratch),
        compiler_params=pltpu.CompilerParams(vmem_limit_bytes=LIMIT),
        cost_estimate=cost(took),
    )(meta, *inputs, *after)


def standardize(values):
    center = values - jnp.mean(values, axis=-1, keepdims=True)
    spread = jnp.mean(center * center, axis=-1, keepdims=True)
    rstd = lax.rsqrt(spread + EPS)
    return center * rstd, rstd


def norm_back(z, rstd, g):
    return (g - jnp.mean(g, axis=-1, keepdims=True) - z * jnp.mean(g * z, axis=-1, keepdims=True)) * rstd


def half_at(index, size):
    return pl.ds(pl.multiple_of(index * size, size), size)


def rows_in_order(meta, source, target):
    size = source.shape[0] // 16
    for spot in range(16):
        rows = pl.ds(pl.multiple_of(meta[1 + spot] * size, size), size)
        target[spot * size : (spot + 1) * size, :] = source[rows, :]


def placed(meta, near, far, target):
    size = target.shape[0] // 16
    for spot in range(16):
        source = (near, far)[spot // 8]
        rows = pl.ds(pl.multiple_of(meta[17 + spot] * size, size), size)
        target[rows, :] = source[spot % 8 * size : (spot % 8 + 1) * size, :]


def first_norm(meta, own, other, z):
    half = own.shape[0]
    for source, place in ((own, meta[0]), (other, 1 - meta[0])):
        z[half_at(place, half), :] = standardize(source[...].astype(F32))[0]


def first_scale(meta, z, near, far, zb, gains, columns):
    placed(meta, near, far, columns)
    gains[...] = columns[...].T[:16, :]
    zb[...] = (z[...] * gains[0:1, :].astype(F32)).astype(BF16)


def turn(meta, zb, zt, turned):
    turned[...] = zb[...].T
    rows_in_order(meta, turned, zt)


def mix(meta, mine, other, mixed, mt, turned):
    width = mine.shape[1]
    for side, source in ((meta[0], mine), (1 - meta[0], other)):
        mixed[:, half_at(side, width)] = source[...]
    turned[...] = mixed[...].T
    rows_in_order(meta, turned, mt)


def attend(meta, zb, near, far, qkv, o_own, o_other, lse, weight, km, vt, s_sc, ot, o_all):
    length = zb.shape[0]
    half = length // 2
    placed(meta, near, far, weight)
    qkv[...] = dot(zb[...], weight[...]).astype(BF16)
    lane = lax.broadcasted_iota(jnp.int32, (1, PAIR), 1)
    keys = qkv[:, PAIR : 2 * PAIR]
    zero = jnp.zeros_like(keys)
    km[0] = jnp.where(lane < HD, keys, zero)
    km[1] = jnp.where(lane < HD, zero, keys)
    vt[...] = qkv[:, 2 * PAIR :].T
    lse[0] = jnp.zeros(lse.shape[1:], F32)
    allowed = lax.broadcasted_iota(jnp.int32, (BAND, BAND), 0) <= lax.broadcasted_iota(jnp.int32, (BAND, BAND), 1)

    def q_step(q_band, _):
        spots = half_at(q_band, BAND)
        queries = qkv[spots, :PAIR]

        def score(k_band, tops, diagonal):
            rows = half_at(k_band, BAND)
            peaks = []
            for head in range(2):
                s = dot_t(km[head, rows, :], queries) * (HD ** -0.5 * LOG2E)
                if diagonal:
                    s = jnp.where(allowed, s, 0.0)
                s_sc[head, rows, :] = s
                peaks.append(jnp.maximum(tops[head], jnp.max(jnp.abs(s), axis=0, keepdims=True)))
            return tuple(peaks)

        def weigh(k_band, carry, tops, diagonal):
            rows = half_at(k_band, BAND)
            results = []
            for head, (total, out) in enumerate(carry):
                s = s_sc[head, rows, :]
                grow = jnp.exp2(s - tops[head])
                shrink = jnp.exp2(-s - tops[head])
                both = grow + shrink
                if diagonal:
                    both = jnp.where(allowed, both, 0.0)
                part = dot(vt[head * HD : (head + 1) * HD, rows], (grow - shrink).astype(BF16))
                results.append((total + jnp.sum(both, axis=0, keepdims=True), out + part))
            return tuple(results)

        none = jnp.zeros((1, BAND), F32)
        tops = score(q_band, (none, none), True)
        tops = lax.fori_loop(0, q_band, lambda k_band, tops: score(k_band, tops, False), tops)
        start = (none, jnp.zeros((HD, BAND), F32))
        carry = weigh(q_band, (start, start), tops, True)
        carry = lax.fori_loop(0, q_band, lambda k_band, carry: weigh(k_band, carry, tops, False), carry)
        for head, (total, out) in enumerate(carry):
            ot[head * HD : (head + 1) * HD, :] = out / total
            lse[0, head : head + 1, spots] = tops[head] + jnp.log2(0.5 * total)
        o_all[spots, :] = ot[...].T.astype(BF16)
        return 0

    lax.fori_loop(0, length // BAND, q_step, 0)
    o_own[...] = o_all[half_at(meta[0], half), :]
    o_other[...] = o_all[half_at(1 - meta[0], half), :]


def attend_back(pair, meta, qkv, o_own, o_other, d_own, d_other, lse, zt, weight, *refs):
    last = pair == 2
    count = (0, 0, 6)[pair]
    extra, refs = refs[:count], refs[count:]
    keep, send, *outs = refs[: 3 + last]
    km, vm, kt, do, inner, dk, dv, dqt, dqkv, s_sc, w_sc, p_sc, ds_sc = refs[3 + last :]
    length = qkv.shape[0]
    half = length // 2
    lane = lax.broadcasted_iota(jnp.int32, (1, PAIR), 1)
    low = lane < HD
    keys = qkv[:, PAIR : 2 * PAIR]
    values = qkv[:, 2 * PAIR :]
    zero = jnp.zeros_like(keys)
    km[0] = jnp.where(low, keys, zero)
    km[1] = jnp.where(low, zero, keys)
    vm[0] = jnp.where(low, values, zero)
    vm[1] = jnp.where(low, zero, values)
    kt[...] = keys.T
    pick = (
        lax.broadcasted_iota(jnp.int32, (8, PAIR), 1) // HD == lax.broadcasted_iota(jnp.int32, (8, PAIR), 0)
    ).astype(F32)
    for o_part, d_part, place in ((o_own, d_own, meta[0]), (o_other, d_other, 1 - meta[0])):
        do[half_at(place, half), :] = d_part[...]
        product = o_part[...].astype(F32) * d_part[...].astype(F32)
        inner[:, half_at(place, half)] = lax.dot_general(
            pick, product, (((1,), (1,)), ((), ())), preferred_element_type=F32, precision=lax.Precision.HIGHEST
        )
    allowed = lax.broadcasted_iota(jnp.int32, (BAND, BAND), 0) <= lax.broadcasted_iota(jnp.int32, (BAND, BAND), 1)
    for q_band in range(length // BAND):
        spots = slice(q_band * BAND, (q_band + 1) * BAND)
        end = (q_band + 1) * BAND
        queries = qkv[spots, :PAIR]
        upstream = do[spots, :]
        small = jnp.zeros_like(queries)
        for head in range(2):
            mine = slice(head * HD, (head + 1) * HD)
            q_mine = jnp.where(low, queries, small) if head == 0 else jnp.where(low, small, queries)
            d_mine = jnp.where(low, upstream, small) if head == 0 else jnp.where(low, small, upstream)
            base = lse[0, head : head + 1, spots] + 1.0
            mean = inner[head : head + 1, spots]
            s_sc[head, :end, :] = dot_t(km[head, :end, :], queries)
            w_sc[head, :end, :] = dot_t(vm[head, :end, :], upstream)
            for k_band in range(q_band + 1):
                rows = slice(k_band * BAND, (k_band + 1) * BAND)
                s = s_sc[head, rows, :] * (HD ** -0.5 * LOG2E)
                dw = w_sc[head, rows, :]
                if k_band == q_band:
                    s = jnp.where(allowed, s, 0.0)
                    dw = jnp.where(allowed, dw, 0.0)
                grow = jnp.exp2(s - base)
                shrink = jnp.exp2(-s - base)
                p = grow - shrink
                p_sc[head, rows, :] = p.astype(BF16)
                ds_sc[head, rows, :] = ((grow + shrink) * dw - p * mean).astype(BF16)
            dv_part = dot(p_sc[head, :end, :], d_mine)
            dk_part = dot(ds_sc[head, :end, :], q_mine)
            dqt[mine, :] = dot(kt[mine, :end], ds_sc[head, :end, :])
            old = q_band * BAND if head == 0 else end
            if old:
                dv[:old, :] += dv_part[:old]
                dk[:old, :] += dk_part[:old]
            if head == 0:
                dv[old:end, :] = dv_part[old:]
                dk[old:end, :] = dk_part[old:]
        dqkv[spots, :PAIR] = (dqt[...].T * HD ** -0.5).astype(BF16)
    dqkv[:, PAIR : 2 * PAIR] = (dk[...] * HD ** -0.5).astype(BF16)
    dqkv[:, 2 * PAIR :] = dv[...].astype(BF16)
    middle = keep.shape[0]
    start = keep.shape[1] - 3 * PAIR
    send[:, start:] = dot(zt[middle:, :], dqkv[...]).astype(BF16)
    keep[:, start:] = dot(zt[:middle, :], dqkv[...]).astype(BF16)
    if last:
        for spot in range(2):
            columns = slice(spot * 3 * PAIR, (spot + 1) * 3 * PAIR)
            keep[:, columns] = extra[3 * spot][...]
            send[:, columns] = extra[3 * spot + 1][...]
        for side, target in zip((1 - meta[0], meta[0]), outs):
            rows = half_at(side, half)
            part = dot_t(dqkv[rows, :], weight[:, 6 * PAIR :])
            for spot in range(2):
                columns = slice(spot * 3 * PAIR, (spot + 1) * 3 * PAIR)
                part += dot_t(extra[3 * spot + 2][rows, :], weight[:, columns])
            target[...] = part.astype(target.dtype)
    else:
        outs[0][...] = dqkv[...]


def added(step, total, first, part):
    @pl.when(step == 0)
    def _():
        total[...] = part if first is None else first[...] + part

    @pl.when(step > 0)
    def _():
        total[...] += part


def feed(
    meta, own, mixed, gains, weight, up, down, upstream,
    out, first, up_keep, up_send, down_keep, down_send, dresid, db, away, mine_out,
    resid, zb, zt_natural, zt, total, g_total, active, dpre, turned, picked,
):
    step = pl.program_id(0)
    gain = gains[1:2, :].astype(F32)

    @pl.when(step == 0)
    def _():
        summed = own[...].astype(F32) + dot(mixed[...], weight[...])
        resid[...] = summed
        z = (standardize(summed)[0] * gain).astype(BF16)
        zb[...] = z
        zt_natural[...] = z.T
        rows_in_order(meta, zt_natural, zt)

    width = active.shape[1]
    root = 0.7978845608028654
    for part in range(3):
        mine = slice(part * width // 3, (part + 1) * width // 3)
        v = dot(zb[...], up[:, mine])
        slope_in = dot_t(upstream[...], down[mine, :])
        square = v * v
        t = jnp.tanh(root * v * (1.0 + 0.044715 * square))
        cdf = 0.5 * (1.0 + t)
        active[:, mine] = (v * cdf).astype(BF16)
        slope = cdf + v * (0.5 * root) * (1.0 - t * t) * (1.0 + 0.134145 * square)
        dpre[:, mine] = (slope_in * slope).astype(BF16)
        turned[mine, :] = active[:, mine].T
    added(step, total, resid, dot(active[...], down[...]))
    added(step, g_total, None, dot_t(dpre[...], up[...]))

    @pl.when(step < 2)
    def _():
        first[:, :width] = dot(zt_natural[...], dpre[...]).astype(BF16)
        first[:, width:] = dot(turned[...], upstream[...]).astype(BF16)

    @pl.when(step >= 2)
    def _():
        rows_in_order(meta, turned, picked)
        size = width // 2
        for spot, (up_part, down_part) in enumerate(((up_keep, down_keep), (up_send, down_send))):
            mine = slice(spot * size, (spot + 1) * size)
            up_part[...] = dot(zt[mine, :], dpre[...]).astype(BF16)
            down_part[...] = dot(picked[mine, :], upstream[...]).astype(BF16)

    @pl.when(step == pl.num_programs(0) - 1)
    def _():
        z, rstd = standardize(resid[...])
        grad = upstream[...].astype(F32) + norm_back(z, rstd, g_total[...] * gain)
        low = grad.astype(BF16)
        for side, target in ((1 - meta[0], away), (meta[0], mine_out)):
            target[...] = dot_t(low, weight[half_at(side, 3 * PAIR), :]).astype(BF16)
        dresid[...] = grad
        db[...] = low
        out[...] = total[...].astype(out.dtype)


def output_back(meta, mt, db, keep, send):
    middle = keep.shape[0]
    send[...] = dot(mt[middle:, :], db[...]).astype(BF16)
    keep[...] = dot(mt[:middle, :], db[...]).astype(BF16)


def input_back(meta, own, mine, other, dresid, gains, out):
    z, rstd = standardize(own[...].astype(F32))
    g = (mine[...] + other[...].astype(F32)) * gains[0:1, :].astype(F32)
    out[...] = dresid[...] + norm_back(z, rstd, g)


def row_sums(values):
    ones = jnp.ones((8, values.shape[1]), F32)
    sums = lax.dot_general(
        ones, values, (((1,), (1,)), ((), ())), preferred_element_type=F32, precision=lax.Precision.HIGHEST
    )
    return sums[0:1, :]


def joint_out(meta, own, other, weight, gain, grad, gain_grad):
    for side, source in ((meta[0], own), (1 - meta[0], other)):
        for pair in range(3):
            for kind in range(3):
                columns = pl.ds(pl.multiple_of((kind * 6 + side * 3 + pair) * PAIR, PAIR), PAIR)
                at = (pair * 3 + kind) * PAIR
                grad[:, columns] = source[:, at : at + PAIR].astype(F32)
    gain_grad[...] = row_sums(grad[...] * weight[...].astype(F32)) / gain[...].astype(F32)


def feed_out(split, meta, first, first_too, last, last_too, weight, gain, up, down, output, gain_grad):
    rows, dim = output.shape
    output[...] = last[:, -dim:].astype(F32) + last_too[:, -dim:].astype(F32)
    for k in range(4):
        parts = []
        for kind in range(2):
            if k < 2 or not split:
                one, two = (first, first_too) if k < 2 else (last, last_too)
                at = ((2 * k + kind) if k < 2 else (2 * kind + k - 2)) * dim
                parts.append(one[:, at : at + dim].astype(F32) + two[:, at : at + dim].astype(F32))
            else:
                at = kind * dim
                parts.append(jnp.where(meta[0] == k - 2, last[:, at : at + dim], last_too[:, at : at + dim]).astype(F32))
        for owner in range(dim // rows):
            up[:, (4 * owner + k) * rows : (4 * owner + k + 1) * rows] = parts[0][:, owner * rows : (owner + 1) * rows]
        down[k * rows : (k + 1) * rows, :] = parts[1]
    gain_grad[...] = row_sums(up[...] * weight[...].astype(F32)) / gain[...].astype(F32)


SWAP = [(0, 1), (1, 0)]


def flipped(array, parts, bit):
    return lax.ppermute(array, "fsdp", [(spot, spot ^ bit) for spot in range(parts)])


def exchanged(blocks, parts):
    groups = [list(range(side, parts, 4)) for side in range(4)]
    return lax.all_to_all(blocks, "fsdp", 0, 0, axis_index_groups=groups, tiled=True)


def rounded_sum(terms):
    total = terms[0].astype(F32)
    for term in terms[1:]:
        total = total + term.astype(F32)
    return total.astype(BF16)


def pinned(array, mark):
    return lax.optimization_barrier((array, mark))[0]


class Reduction:
    def __init__(self, terms, parts, place):
        self.terms, self.parts, self.place = terms, parts, place

    def go(self, step):
        if step == "seq":
            width = self.terms[0].shape[3] // 2
            away = rounded_sum(
                [lax.dynamic_slice_in_dim(term, (1 - self.place) * width, width, 3) for term in self.terms]
            )
            self.terms = [lax.dynamic_slice_in_dim(term, self.place * width, width, 3) for term in self.terms]
            self.came = lax.ppermute(away, "seq", SWAP)
        else:
            away = rounded_sum([term[:, 1:] for term in self.terms])
            self.terms = [term[:, :1] for term in self.terms]
            self.came = flipped(away, self.parts, 2)
        return away

    def take(self, mark):
        self.terms.append(pinned(self.came, mark))


def body(block_input, lead_gain, joint_weight, output_weight, tail_gain, up_weight, down_weight, cotangent):
    rows, triple = joint_weight.shape
    dim = block_input.shape[2]
    wide = up_weight.shape[1]
    half = block_input.shape[1]
    length = 2 * half
    parts = dim // rows
    group = triple // 6
    chunk = dim // 2
    place = lax.axis_index("seq")
    me = lax.axis_index("fsdp")
    direct = parts == 16
    base = me if direct else jnp.zeros_like(me)
    spots = jnp.arange(16, dtype=jnp.int32)
    few = jnp.arange(8, dtype=jnp.int32)
    eight = (few % 2) * 8 + (few // 2 % 2) * 4 + few // 4 * 2
    meta = jnp.concatenate(
        [
            place[None],
            spots % 8 // 2 * 4 + ((base % 4) ^ (spots % 2 * 2 + spots // 8)),
            base ^ jnp.concatenate([eight, eight ^ 1]) if direct else spots,
        ]
    ).astype(jnp.int32)

    joint_own = lax.dynamic_index_in_dim(joint_weight.reshape(rows, 3, 2, group), place, 2, keepdims=False)
    joint_own = joint_own.reshape(rows, 3, 3, PAIR).transpose(0, 2, 1, 3).reshape(rows, 3 * group)
    up_turned = up_weight.reshape(rows, parts, 4, rows).transpose(2, 0, 1, 3).reshape(4, rows, dim)
    down_turned = down_weight.reshape(4, rows, dim)
    hidden = [part[k] for k in range(4) for part in (up_turned, down_turned)]

    own = block_input[0]
    upstream = cotangent[0]
    rest = lax.all_gather(jnp.concatenate([output_weight, *hidden], axis=1), "fsdp", axis=0, tiled=True)
    other = lax.ppermute(own, "seq", SWAP)
    both_gains = jnp.pad(jnp.stack([lead_gain, tail_gain], axis=1), ((0, 0), (0, PAIR - 2)))
    first = jnp.concatenate([joint_own, both_gains], axis=1)
    if direct:
        for bit in (8, 4, 2):
            if bit == 2:
                first, other = lax.optimization_barrier((first, other))
            first = jnp.concatenate([first, flipped(first, parts, bit)], axis=0)
        firsts = (first, flipped(first, parts, 1))
    else:
        first = lax.all_gather(first, "fsdp", axis=0, tiled=True)
        firsts = (first[:chunk], first[chunk:])

    (z_one,) = call(first_norm, "first_norm", (shaped(length, dim, dtype=F32),), meta, (own, other), took=3)
    zb, gains = call(
        first_scale,
        "first_scale",
        (shaped(length, dim), shaped(16, dim)),
        meta,
        (z_one, *firsts),
        [pltpu.VMEM((dim, PAIR), BF16)],
        took=2,
        grid=(1,),
        specs=[VMEM] + [column(chunk, PAIR, lambda step: 9)] * 2,
    )
    triples = column(length, 3 * PAIR)
    pair_tokens = column(half, PAIR)
    lse_spec = pl.BlockSpec((1, 8, length), lambda step: (step, 0, 0))
    qkv, o_own, o_other, lse, weight = call(
        attend,
        "attend",
        (
            shaped(length, 9 * PAIR),
            shaped(half, group),
            shaped(half, group),
            shaped(3, 8, length, dtype=F32),
            shaped(dim, 9 * PAIR),
        ),
        meta,
        (zb, *firsts),
        [
            pltpu.VMEM((2, length, PAIR), BF16),
            pltpu.VMEM((PAIR, length), BF16),
            pltpu.VMEM((2, length, BAND), F32),
            pltpu.VMEM((PAIR, BAND), F32),
            pltpu.VMEM((length, PAIR), BF16),
        ],
        took=22,
        grid=(3,),
        specs=[whole(length, dim)] + [column(chunk, 3 * PAIR)] * 2,
        out_specs=[triples, pair_tokens, pair_tokens, lse_spec, column(dim, 3 * PAIR)],
    )
    o_came = lax.ppermute(o_other, "seq", SWAP)
    store = [pltpu.VMEM((dim, length), BF16)]
    (zt,) = call(turn, "turn", (shaped(dim, length),), meta, (zb,), store, took=2, after=[lse])
    mixed, mixed_t = call(
        mix,
        "mix",
        (shaped(half, dim), shaped(dim, half)),
        meta,
        (o_own, o_came),
        [pltpu.VMEM((dim, half), BF16)],
        took=2,
        after=[zt],
    )
    rest_block = column(dim, dim, lambda step: 0)
    total_f32 = shaped(half, dim, dtype=F32)
    tokens = whole(half, dim)

    later = column(chunk, dim, lambda k: jnp.maximum(k - 2, 0))
    out, grad_first, up_keep, up_send, down_keep, down_send, dresid, db, dm_away, dm_mine = call(
        feed,
        "feed",
        (shaped(half, dim), shaped(dim, 4 * dim))
        + (shaped(chunk, 2 * dim),) * 4
        + (total_f32, shaped(half, dim), shaped(half, group), shaped(half, group)),
        meta,
        (own, mixed, gains, rest, rest, rest, upstream),
        [
            pltpu.VMEM((half, dim), F32),
            pltpu.VMEM((half, dim), BF16),
            pltpu.VMEM((dim, half), BF16),
            pltpu.VMEM((dim, half), BF16),
            pltpu.VMEM((half, dim), F32),
            pltpu.VMEM((half, dim), F32),
            pltpu.VMEM((half, dim), BF16),
            pltpu.VMEM((half, dim), BF16),
            pltpu.VMEM((dim, half), BF16),
            pltpu.VMEM((dim, half), BF16),
        ],
        took=36,
        grid=(4,),
        specs=[
            tokens,
            tokens,
            whole(16, dim),
            rest_block,
            column(dim, dim, lambda k: 1 + 2 * k),
            column(dim, dim, lambda k: 2 + 2 * k),
            tokens,
        ],
        out_specs=[tokens, column(dim, 2 * dim, lambda k: jnp.minimum(k, 1))]
        + [later] * 4
        + [tokens, tokens, whole(half, group), whole(half, group)],
    )

    if direct:
        first_sum = lax.psum_scatter(grad_first, "fsdp", scatter_dimension=0, tiled=True)
        up_came = flipped(up_send, parts, 1)
        down_came = flipped(down_send, parts, 1)

    def blocks_of(part):
        return part.reshape(4, 2, rows, -1)

    dm_came = lax.ppermute(dm_away, "seq", SWAP)
    mixed_keep, mixed_send = call(output_back, "output_back", (shaped(chunk, dim),) * 2, meta, (mixed_t, db))
    dm_came = pinned(dm_came, mixed_keep)
    marks = [[mixed_keep], [], []]
    if direct:
        mixed_came = flipped(mixed_send, parts, 1)
        up_red = Reduction([blocks_of(part) for part in (up_keep, pinned(up_came, db))], parts, place)
        marks[0].append(up_red.go(2))
        down_red = Reduction([blocks_of(part) for part in (down_keep, pinned(down_came, dm_came))], parts, place)
        marks[0].append(down_red.go("seq"))
        mixed_red = Reduction([blocks_of(part) for part in (mixed_keep, pinned(mixed_came, dm_came))], parts, place)
        marks[0].append(mixed_red.go(2))
        marks[0].append(up_red.came)

    def attend_back_call(pair, outs, out_specs, extra, after):
        width = (9 if pair == 2 else 3) * PAIR
        pick = lambda step: pair
        return call(
            functools.partial(attend_back, pair),
            "attend_back",
            (shaped(chunk, width), shaped(chunk, width)) + outs,
            meta,
            (qkv, o_own, o_other, dm_mine, dm_came, lse, zt, weight, *extra),
            [
                pltpu.VMEM((2, length, PAIR), BF16),
                pltpu.VMEM((2, length, PAIR), BF16),
                pltpu.VMEM((PAIR, length), BF16),
                pltpu.VMEM((length, PAIR), BF16),
                pltpu.VMEM((8, length), F32),
                pltpu.VMEM((length, PAIR), F32),
                pltpu.VMEM((length, PAIR), F32),
                pltpu.VMEM((PAIR, BAND), F32),
                pltpu.VMEM((length, 3 * PAIR), BF16),
                pltpu.VMEM((2, length, BAND), F32),
                pltpu.VMEM((2, length, BAND), F32),
                pltpu.VMEM((2, length, BAND), BF16),
                pltpu.VMEM((2, length, BAND), BF16),
            ],
            took=10,
            after=after,
            grid=(1,),
            specs=[column(length, 3 * PAIR, pick)]
            + [column(half, PAIR, pick)] * 4
            + [
                pl.BlockSpec((1, 8, length), lambda step: (pair, 0, 0)),
                whole(dim, length),
                whole(dim, 9 * PAIR) if pair == 2 else column(dim, 3 * PAIR, pick),
            ]
            + [whole(*part.shape) for part in extra],
            out_specs=[whole(chunk, width)] * 2 + out_specs,
        )

    one = (shaped(length, 3 * PAIR),)
    keep_0, send_0, token_0 = attend_back_call(0, one, [whole(length, 3 * PAIR)], (), marks[0])
    if direct:
        up_red.take(token_0)
        down_red.take(token_0)
        marks[1] = [up_red.go("seq"), down_red.go(2)]
    keep_1, send_1, token_1 = attend_back_call(1, one, [whole(length, 3 * PAIR)], (), marks[1] + [token_0])
    if direct:
        last_sum = []
        for red in (up_red, down_red, mixed_red):
            red.take(token_1)
            last_sum.append(rounded_sum(red.terms))
        last_sum = jnp.concatenate(last_sum, axis=-1).reshape(4, rows, -1)
        deep = me // 4
        last_parts = [lax.dynamic_index_in_dim(last_sum, deep, 0, keepdims=False)]
        for far in (1, 2, 3):
            away = lax.dynamic_index_in_dim(last_sum, deep ^ far, 0, keepdims=False)
            marks[2].append(away)
            last_parts.append(flipped(away, parts, 4 * far))
    joint_keep, joint_send, sent, own_part = attend_back_call(
        2,
        (shaped(half, dim), total_f32),
        [tokens] * 2,
        (keep_0, send_0, token_0, keep_1, send_1, token_1),
        marks[2],
    )
    other_part = lax.ppermute(sent, "seq", SWAP)
    marks = []
    marks = []
    if direct:
        joint_came = flipped(joint_send, parts, 1)
        joint_red = Reduction([blocks_of(part) for part in (joint_keep, joint_came)], parts, place)
        joint_red.go(2)
        joint_red.take(joint_keep)
        joint_sum = rounded_sum(joint_red.terms).reshape(4, rows, -1)
        marks = [first_sum, joint_sum]
        joint_sum = exchanged(joint_sum, parts)
    (input_grad,) = call(
        input_back, "input_back", (total_f32,), meta, (own, own_part, other_part, dresid, gains), after=marks
    )

    if direct:
        last_sum = rounded_sum(last_parts)
        joint_sum = jnp.sum(pinned(joint_sum, input_grad).astype(F32), axis=0).astype(BF16)
    else:

        def scattered(keep, send):
            blocks = jnp.stack([keep, send]).reshape(2, 4, 2, dim // 16, -1).transpose(1, 2, 0, 3, 4).reshape(dim, -1)
            return lax.psum_scatter(blocks, "fsdp", scatter_dimension=0, tiled=True)

        first_sum = lax.psum_scatter(grad_first, "fsdp", scatter_dimension=0, tiled=True)
        last_sum = ((up_keep, up_send), (down_keep, down_send), (mixed_keep, mixed_send))
        last_sum = jnp.concatenate([scattered(*pair) for pair in last_sum], axis=1)
        joint_sum = scattered(joint_keep, joint_send)
    first_sum, last_sum, joint_sum = ((part, lax.ppermute(part, "seq", SWAP)) for part in (first_sum, last_sum, joint_sum))
    up_grad, down_grad, output_grad, tail_grad = call(
        functools.partial(feed_out, direct),
        "feed_out",
        (
            shaped(rows, wide, dtype=F32),
            shaped(4 * rows, dim, dtype=F32),
            shaped(rows, dim, dtype=F32),
            shaped(1, rows, dtype=F32),
        ),
        meta,
        (*first_sum, *last_sum, up_weight, tail_gain[None, :]),
    )
    joint_grad, lead_grad = call(
        joint_out,
        "joint_out",
        (shaped(rows, triple, dtype=F32), shaped(1, rows, dtype=F32)),
        meta,
        (*joint_sum, joint_weight, lead_gain[None, :]),
        took=2,
        after=[up_grad],
    )
    return (
        out[None],
        input_grad[None],
        lead_grad[0],
        joint_grad,
        output_grad,
        tail_grad[0],
        up_grad,
        down_grad,
    )


def solution(mesh):
    split = P("fsdp", "seq", None)
    placed = (split, P("fsdp"), P("fsdp", None), P("fsdp", None), P("fsdp"), P("fsdp", None), P("fsdp", None), split)
    return jax.shard_map(
        body,
        mesh=mesh,
        in_specs=placed,
        out_specs=(split, split, P("fsdp"), P("fsdp", None), P("fsdp", None), P("fsdp"), P("fsdp", None), P("fsdp", None)),
        check_vma=False,
    )
```

```python
import functools

import jax
import jax.numpy as jnp
from jax import lax
from jax.experimental import pallas as pl
from jax.experimental.pallas import tpu as pltpu
from jax.sharding import PartitionSpec as P

HD = 64
EPS = 1e-05
PAIR = 2 * HD
BAND = 256
LOG2E = 1.4426950408889634
LIMIT = 56 << 20
F32 = jnp.float32
BF16 = jnp.bfloat16

VMEM = pl.BlockSpec(memory_space=pltpu.VMEM)
SMEM = pl.BlockSpec(memory_space=pltpu.SMEM)
ANY = pl.BlockSpec(memory_space=pl.ANY)


def dot(left, right):
    return jnp.dot(left, right, preferred_element_type=F32)


def dot_t(left, right):
    return lax.dot_general(left, right, (((1,), (1,)), ((), ())), preferred_element_type=F32)


def shaped(*dims, dtype=BF16):
    return jax.ShapeDtypeStruct(dims, dtype)


def cost(microseconds):
    return pl.CostEstimate(flops=int(microseconds * 1e7), transcendentals=0, bytes_accessed=int(microseconds * 3e4))


def waiting(kernel, fixed, after):
    def run(*refs):
        kernel(*refs[:fixed], *refs[fixed + after :])

    return run


def whole(*dims):
    return pl.BlockSpec(dims, lambda *_: (0,) * len(dims))


def column(rows, columns, pick=lambda step: step):
    return pl.BlockSpec((rows, columns), lambda *steps: (0, pick(*steps)))


def call(kernel, name, outs, meta, inputs, scratch=(), took=4, after=(), grid=(), specs=None, out_specs=None):
    return pl.pallas_call(
        waiting(kernel, 1 + len(inputs), len(after)),
        name=name,
        grid=grid,
        out_shape=outs,
        in_specs=[SMEM] + list(specs or [VMEM] * len(inputs)) + [ANY] * len(after),
        out_specs=list(out_specs or [VMEM] * len(outs)),
        scratch_shapes=list(scratch),
        compiler_params=pltpu.CompilerParams(vmem_limit_bytes=LIMIT),
        cost_estimate=cost(took),
    )(meta, *inputs, *after)


def standardize(values):
    center = values - jnp.mean(values, axis=-1, keepdims=True)
    spread = jnp.mean(center * center, axis=-1, keepdims=True)
    rstd = lax.rsqrt(spread + EPS)
    return center * rstd, rstd


def norm_back(z, rstd, g):
    return (g - jnp.mean(g, axis=-1, keepdims=True) - z * jnp.mean(g * z, axis=-1, keepdims=True)) * rstd


def half_at(index, size):
    return pl.ds(pl.multiple_of(index * size, size), size)


def rows_in_order(meta, source, target):
    size = source.shape[0] // 16
    for spot in range(16):
        rows = pl.ds(pl.multiple_of(meta[1 + spot] * size, size), size)
        target[spot * size : (spot + 1) * size, :] = source[rows, :]


def placed(meta, near, far, target):
    size = target.shape[0] // 16
    for spot in range(16):
        source = (near, far)[spot // 8]
        rows = pl.ds(pl.multiple_of(meta[17 + spot] * size, size), size)
        target[rows, :] = source[spot % 8 * size : (spot % 8 + 1) * size, :]


def first_norm(meta, own, other, z):
    half = own.shape[0]
    for source, place in ((own, meta[0]), (other, 1 - meta[0])):
        z[half_at(place, half), :] = standardize(source[...].astype(F32))[0]


def first_scale(meta, z, near, far, zb, gains, columns):
    placed(meta, near, far, columns)
    gains[...] = columns[...].T[:16, :]
    zb[...] = (z[...] * gains[0:1, :].astype(F32)).astype(BF16)


def turn(meta, zb, zt, turned):
    turned[...] = zb[...].T
    rows_in_order(meta, turned, zt)


def mix(meta, mine, other, mixed, mt, turned):
    width = mine.shape[1]
    for side, source in ((meta[0], mine), (1 - meta[0], other)):
        mixed[:, half_at(side, width)] = source[...]
    turned[...] = mixed[...].T
    rows_in_order(meta, turned, mt)


def attend(meta, zb, near, far, qkv, o_own, o_other, lse, weight, km, vt, s_sc, ot, o_all):
    length = zb.shape[0]
    half = length // 2
    placed(meta, near, far, weight)
    qkv[...] = dot(zb[...], weight[...]).astype(BF16)
    lane = lax.broadcasted_iota(jnp.int32, (1, PAIR), 1)
    keys = qkv[:, PAIR : 2 * PAIR]
    zero = jnp.zeros_like(keys)
    km[0] = jnp.where(lane < HD, keys, zero)
    km[1] = jnp.where(lane < HD, zero, keys)
    vt[...] = qkv[:, 2 * PAIR :].T
    lse[0] = jnp.zeros(lse.shape[1:], F32)
    allowed = lax.broadcasted_iota(jnp.int32, (BAND, BAND), 0) <= lax.broadcasted_iota(jnp.int32, (BAND, BAND), 1)

    def q_step(q_band, _):
        spots = half_at(q_band, BAND)
        queries = qkv[spots, :PAIR]

        def score(k_band, tops, diagonal):
            rows = half_at(k_band, BAND)
            peaks = []
            for head in range(2):
                s = dot_t(km[head, rows, :], queries) * (HD ** -0.5 * LOG2E)
                if diagonal:
                    s = jnp.where(allowed, s, 0.0)
                s_sc[head, rows, :] = s
                peaks.append(jnp.maximum(tops[head], jnp.max(jnp.abs(s), axis=0, keepdims=True)))
            return tuple(peaks)

        def weigh(k_band, carry, tops, diagonal):
            rows = half_at(k_band, BAND)
            results = []
            for head, (total, out) in enumerate(carry):
                s = s_sc[head, rows, :]
                grow = jnp.exp2(s - tops[head])
                shrink = jnp.exp2(-s - tops[head])
                both = grow + shrink
                if diagonal:
                    both = jnp.where(allowed, both, 0.0)
                part = dot(vt[head * HD : (head + 1) * HD, rows], (grow - shrink).astype(BF16))
                results.append((total + jnp.sum(both, axis=0, keepdims=True), out + part))
            return tuple(results)

        none = jnp.zeros((1, BAND), F32)
        tops = score(q_band, (none, none), True)
        tops = lax.fori_loop(0, q_band, lambda k_band, tops: score(k_band, tops, False), tops)
        start = (none, jnp.zeros((HD, BAND), F32))
        carry = weigh(q_band, (start, start), tops, True)
        carry = lax.fori_loop(0, q_band, lambda k_band, carry: weigh(k_band, carry, tops, False), carry)
        for head, (total, out) in enumerate(carry):
            ot[head * HD : (head + 1) * HD, :] = out / total
            lse[0, head : head + 1, spots] = tops[head] + jnp.log2(0.5 * total)
        o_all[spots, :] = ot[...].T.astype(BF16)
        return 0

    lax.fori_loop(0, length // BAND, q_step, 0)
    o_own[...] = o_all[half_at(meta[0], half), :]
    o_other[...] = o_all[half_at(1 - meta[0], half), :]


def attend_back(pair, meta, qkv, o_own, o_other, d_own, d_other, lse, zt, weight, *refs):
    last = pair == 2
    count = (0, 0, 4)[pair]
    extra, refs = refs[:count], refs[count:]
    keep, send, *outs = refs[:3]
    km, vm, kt, do, inner, dk, dv, dqt, dqkv, s_sc, w_sc, p_sc, ds_sc = refs[3:]
    length = qkv.shape[0]
    half = length // 2
    lane = lax.broadcasted_iota(jnp.int32, (1, PAIR), 1)
    low = lane < HD
    keys = qkv[:, PAIR : 2 * PAIR]
    values = qkv[:, 2 * PAIR :]
    zero = jnp.zeros_like(keys)
    km[0] = jnp.where(low, keys, zero)
    km[1] = jnp.where(low, zero, keys)
    vm[0] = jnp.where(low, values, zero)
    vm[1] = jnp.where(low, zero, values)
    kt[...] = keys.T
    pick = (
        lax.broadcasted_iota(jnp.int32, (8, PAIR), 1) // HD == lax.broadcasted_iota(jnp.int32, (8, PAIR), 0)
    ).astype(F32)
    for o_part, d_part, place in ((o_own, d_own, meta[0]), (o_other, d_other, 1 - meta[0])):
        do[half_at(place, half), :] = d_part[...]
        product = o_part[...].astype(F32) * d_part[...].astype(F32)
        inner[:, half_at(place, half)] = lax.dot_general(
            pick, product, (((1,), (1,)), ((), ())), preferred_element_type=F32, precision=lax.Precision.HIGHEST
        )
    allowed = lax.broadcasted_iota(jnp.int32, (BAND, BAND), 0) <= lax.broadcasted_iota(jnp.int32, (BAND, BAND), 1)
    for q_band in range(length // BAND):
        spots = slice(q_band * BAND, (q_band + 1) * BAND)
        end = (q_band + 1) * BAND
        queries = qkv[spots, :PAIR]
        upstream = do[spots, :]
        small = jnp.zeros_like(queries)
        for head in range(2):
            mine = slice(head * HD, (head + 1) * HD)
            q_mine = jnp.where(low, queries, small) if head == 0 else jnp.where(low, small, queries)
            d_mine = jnp.where(low, upstream, small) if head == 0 else jnp.where(low, small, upstream)
            base = lse[0, head : head + 1, spots] + 1.0
            mean = inner[head : head + 1, spots]
            s_sc[head, :end, :] = dot_t(km[head, :end, :], queries)
            w_sc[head, :end, :] = dot_t(vm[head, :end, :], upstream)
            for k_band in range(q_band + 1):
                rows = slice(k_band * BAND, (k_band + 1) * BAND)
                s = s_sc[head, rows, :] * (HD ** -0.5 * LOG2E)
                dw = w_sc[head, rows, :]
                if k_band == q_band:
                    s = jnp.where(allowed, s, 0.0)
                    dw = jnp.where(allowed, dw, 0.0)
                grow = jnp.exp2(s - base)
                shrink = jnp.exp2(-s - base)
                p = grow - shrink
                p_sc[head, rows, :] = p.astype(BF16)
                ds_sc[head, rows, :] = ((grow + shrink) * dw - p * mean).astype(BF16)
            dv_part = dot(p_sc[head, :end, :], d_mine)
            dk_part = dot(ds_sc[head, :end, :], q_mine)
            dqt[mine, :] = dot(kt[mine, :end], ds_sc[head, :end, :])
            old = q_band * BAND if head == 0 else end
            if old:
                dv[:old, :] += dv_part[:old]
                dk[:old, :] += dk_part[:old]
            if head == 0:
                dv[old:end, :] = dv_part[old:]
                dk[old:end, :] = dk_part[old:]
        dqkv[spots, :PAIR] = (dqt[...].T * HD ** -0.5).astype(BF16)
    dqkv[:, PAIR : 2 * PAIR] = (dk[...] * HD ** -0.5).astype(BF16)
    dqkv[:, 2 * PAIR :] = dv[...].astype(BF16)
    middle = keep.shape[0]
    start = keep.shape[1] - 3 * PAIR
    send[:, start:] = dot(zt[middle:, :], dqkv[...]).astype(BF16)
    keep[:, start:] = dot(zt[:middle, :], dqkv[...]).astype(BF16)
    if last:
        for spot in range(2):
            columns = slice(spot * 3 * PAIR, (spot + 1) * 3 * PAIR)
            keep[:, columns] = extra[2 * spot][...]
            send[:, columns] = extra[2 * spot + 1][...]
    outs[0][...] = dqkv[...]


def token_back(meta, t0, t1, t2, weight, away, mine_out):
    half = away.shape[0]
    for side, target in ((1 - meta[0], away), (meta[0], mine_out)):
        part = None
        for spot, token in enumerate((t0, t1, t2)):
            columns = slice(spot * 3 * PAIR, (spot + 1) * 3 * PAIR)
            new = dot_t(token[half_at(side, half), :], weight[:, columns])
            part = new if part is None else part + new
        target[...] = part.astype(target.dtype)


def added(step, total, first, part):
    @pl.when(step == 0)
    def _():
        total[...] = part if first is None else first[...] + part

    @pl.when(step > 0)
    def _():
        total[...] += part


def feed(
    meta, own, mixed, gains, weight, up, down, upstream,
    active, dpre, zt_natural, zt, resid, dresid, db, away, mine_out, zb, g_total,
):
    step = pl.program_id(0)
    gain = gains[1:2, :].astype(F32)

    @pl.when(step == 0)
    def _():
        summed = own[...].astype(F32) + dot(mixed[...], weight[...])
        resid[...] = summed
        z = (standardize(summed)[0] * gain).astype(BF16)
        zb[...] = z
        zt_natural[...] = z.T
        rows_in_order(meta, zt_natural, zt)

    width = active.shape[1]
    root = 0.7978845608028654
    for part in range(3):
        mine = slice(part * width // 3, (part + 1) * width // 3)
        v = dot(zb[...], up[:, mine])
        slope_in = dot_t(upstream[...], down[mine, :])
        square = v * v
        t = jnp.tanh(root * v * (1.0 + 0.044715 * square))
        cdf = 0.5 * (1.0 + t)
        active[:, mine] = (v * cdf).astype(BF16)
        slope = cdf + v * (0.5 * root) * (1.0 - t * t) * (1.0 + 0.134145 * square)
        dpre[:, mine] = (slope_in * slope).astype(BF16)
    added(step, g_total, None, dot_t(dpre[...], up[...]))

    @pl.when(step == pl.num_programs(0) - 1)
    def _():
        z, rstd = standardize(resid[...])
        grad = upstream[...].astype(F32) + norm_back(z, rstd, g_total[...] * gain)
        low = grad.astype(BF16)
        for side, target in ((1 - meta[0], away), (meta[0], mine_out)):
            target[...] = dot_t(low, weight[half_at(side, 3 * PAIR), :]).astype(BF16)
        dresid[...] = grad
        db[...] = low


def hidden_back(
    meta, zt_natural, zt, active, dpre, upstream, mt, db,
    first, up_keep, up_send, down_keep, down_send, mixed_keep, mixed_send, turned, picked,
):
    step = pl.program_id(0)
    width = active.shape[1]
    turned[...] = active[...].T

    @pl.when(step < 2)
    def _():
        first[:, :width] = dot(zt_natural[...], dpre[...]).astype(BF16)
        first[:, width:] = dot(turned[...], upstream[...]).astype(BF16)

    @pl.when(step >= 2)
    def _():
        rows_in_order(meta, turned, picked)
        size = width // 2
        for spot, (up_part, down_part) in enumerate(((up_keep, down_keep), (up_send, down_send))):
            mine = slice(spot * size, (spot + 1) * size)
            up_part[...] = dot(zt[mine, :], dpre[...]).astype(BF16)
            down_part[...] = dot(picked[mine, :], upstream[...]).astype(BF16)

    @pl.when(step == pl.num_programs(0) - 1)
    def _():
        size = width // 2
        mixed_send[...] = dot(mt[size:, :], db[...]).astype(BF16)
        mixed_keep[...] = dot(mt[:size, :], db[...]).astype(BF16)


def forward_out(meta, before, active, down, out, total):
    step = pl.program_id(0)
    added(step, total, before, dot(active[...], down[...]))

    @pl.when(step == pl.num_programs(0) - 1)
    def _():
        out[...] = total[...].astype(out.dtype)


def input_back(meta, own, mine, other, dresid, gains, out):
    z, rstd = standardize(own[...].astype(F32))
    g = (mine[...] + other[...].astype(F32)) * gains[0:1, :].astype(F32)
    out[...] = dresid[...] + norm_back(z, rstd, g)


def row_sums(values):
    ones = jnp.ones((8, values.shape[1]), F32)
    sums = lax.dot_general(
        ones, values, (((1,), (1,)), ((), ())), preferred_element_type=F32, precision=lax.Precision.HIGHEST
    )
    return sums[0:1, :]


def joint_out(meta, own, other, weight, gain, grad, gain_grad):
    for side, source in ((meta[0], own), (1 - meta[0], other)):
        for pair in range(3):
            for kind in range(3):
                columns = pl.ds(pl.multiple_of((kind * 6 + side * 3 + pair) * PAIR, PAIR), PAIR)
                at = (pair * 3 + kind) * PAIR
                grad[:, columns] = source[:, at : at + PAIR].astype(F32)
    gain_grad[...] = row_sums(grad[...] * weight[...].astype(F32)) / gain[...].astype(F32)


def feed_out(split, meta, first, first_too, last, last_too, weight, gain, up, down, output, gain_grad):
    rows, dim = output.shape
    if split:
        width = dim // 2
        for side, source in ((meta[0], last), (1 - meta[0], last_too)):
            output[:, half_at(side, width)] = source[:, 2 * dim :].astype(F32)
    else:
        output[...] = last[:, -dim:].astype(F32) + last_too[:, -dim:].astype(F32)
    for k in range(4):
        parts = []
        for kind in range(2):
            if k < 2 or not split:
                one, two = (first, first_too) if k < 2 else (last, last_too)
                at = ((2 * k + kind) if k < 2 else (2 * kind + k - 2)) * dim
                parts.append(one[:, at : at + dim].astype(F32) + two[:, at : at + dim].astype(F32))
            else:
                at = kind * dim
                parts.append(jnp.where(meta[0] == k - 2, last[:, at : at + dim], last_too[:, at : at + dim]).astype(F32))
        for owner in range(dim // rows):
            up[:, (4 * owner + k) * rows : (4 * owner + k + 1) * rows] = parts[0][:, owner * rows : (owner + 1) * rows]
        down[k * rows : (k + 1) * rows, :] = parts[1]
    gain_grad[...] = row_sums(up[...] * weight[...].astype(F32)) / gain[...].astype(F32)


SWAP = [(0, 1), (1, 0)]


def flipped(array, parts, bit):
    return lax.ppermute(array, "fsdp", [(spot, spot ^ bit) for spot in range(parts)])


def exchanged(blocks, parts):
    groups = [list(range(side, parts, 4)) for side in range(4)]
    return lax.all_to_all(blocks, "fsdp", 0, 0, axis_index_groups=groups, tiled=True)


def rounded_sum(terms):
    total = terms[0].astype(F32)
    for term in terms[1:]:
        total = total + term.astype(F32)
    return total.astype(BF16)


def pinned(array, mark):
    return lax.optimization_barrier((array, mark))[0]


class Reduction:
    def __init__(self, terms, parts, place):
        self.terms, self.parts, self.place = terms, parts, place

    def go(self, step):
        if step == "seq":
            width = self.terms[0].shape[3] // 2
            away = rounded_sum(
                [lax.dynamic_slice_in_dim(term, (1 - self.place) * width, width, 3) for term in self.terms]
            )
            self.terms = [lax.dynamic_slice_in_dim(term, self.place * width, width, 3) for term in self.terms]
            self.came = lax.ppermute(away, "seq", SWAP)
        else:
            away = rounded_sum([term[:, 1:] for term in self.terms])
            self.terms = [term[:, :1] for term in self.terms]
            self.came = flipped(away, self.parts, 2)
        return away

    def take(self, mark):
        self.terms.append(pinned(self.came, mark))


def body(block_input, lead_gain, joint_weight, output_weight, tail_gain, up_weight, down_weight, cotangent):
    rows, triple = joint_weight.shape
    dim = block_input.shape[2]
    wide = up_weight.shape[1]
    half = block_input.shape[1]
    length = 2 * half
    parts = dim // rows
    group = triple // 6
    chunk = dim // 2
    place = lax.axis_index("seq")
    me = lax.axis_index("fsdp")
    direct = parts == 16
    base = me if direct else jnp.zeros_like(me)
    spots = jnp.arange(16, dtype=jnp.int32)
    few = jnp.arange(8, dtype=jnp.int32)
    eight = (few % 2) * 8 + (few // 2 % 2) * 4 + few // 4 * 2
    meta = jnp.concatenate(
        [
            place[None],
            spots % 8 // 2 * 4 + ((base % 4) ^ (spots % 2 * 2 + spots // 8)),
            base ^ jnp.concatenate([eight, eight ^ 1]) if direct else spots,
        ]
    ).astype(jnp.int32)

    joint_own = lax.dynamic_index_in_dim(joint_weight.reshape(rows, 3, 2, group), place, 2, keepdims=False)
    joint_own = joint_own.reshape(rows, 3, 3, PAIR).transpose(0, 2, 1, 3).reshape(rows, 3 * group)
    up_turned = up_weight.reshape(rows, parts, 4, rows).transpose(2, 0, 1, 3).reshape(4, rows, dim)
    down_turned = down_weight.reshape(4, rows, dim)
    hidden = [part[k] for k in range(4) for part in (up_turned, down_turned)]

    own = block_input[0]
    upstream = cotangent[0]
    rest = lax.all_gather(jnp.concatenate([output_weight, *hidden], axis=1), "fsdp", axis=0, tiled=True)
    other = lax.ppermute(own, "seq", SWAP)
    both_gains = jnp.pad(jnp.stack([lead_gain, tail_gain], axis=1), ((0, 0), (0, PAIR - 2)))
    first = jnp.concatenate([joint_own, both_gains], axis=1)
    if direct:
        for bit in (8, 4, 2):
            if bit == 2:
                first, other = lax.optimization_barrier((first, other))
            first = jnp.concatenate([first, flipped(first, parts, bit)], axis=0)
        firsts = (first, flipped(first, parts, 1))
    else:
        first = lax.all_gather(first, "fsdp", axis=0, tiled=True)
        firsts = (first[:chunk], first[chunk:])

    (z_one,) = call(first_norm, "first_norm", (shaped(length, dim, dtype=F32),), meta, (own, other), took=3)
    zb, gains = call(
        first_scale,
        "first_scale",
        (shaped(length, dim), shaped(16, dim)),
        meta,
        (z_one, *firsts),
        [pltpu.VMEM((dim, PAIR), BF16)],
        took=2,
        grid=(1,),
        specs=[VMEM] + [column(chunk, PAIR, lambda step: 9)] * 2,
    )
    triples = column(length, 3 * PAIR)
    pair_tokens = column(half, PAIR)
    lse_spec = pl.BlockSpec((1, 8, length), lambda step: (step, 0, 0))
    qkv, o_own, o_other, lse, weight = call(
        attend,
        "attend",
        (
            shaped(length, 9 * PAIR),
            shaped(half, group),
            shaped(half, group),
            shaped(3, 8, length, dtype=F32),
            shaped(dim, 9 * PAIR),
        ),
        meta,
        (zb, *firsts),
        [
            pltpu.VMEM((2, length, PAIR), BF16),
            pltpu.VMEM((PAIR, length), BF16),
            pltpu.VMEM((2, length, BAND), F32),
            pltpu.VMEM((PAIR, BAND), F32),
            pltpu.VMEM((length, PAIR), BF16),
        ],
        took=22,
        grid=(3,),
        specs=[whole(length, dim)] + [column(chunk, 3 * PAIR)] * 2,
        out_specs=[triples, pair_tokens, pair_tokens, lse_spec, column(dim, 3 * PAIR)],
    )
    o_came = lax.ppermute(o_other, "seq", SWAP)
    store = [pltpu.VMEM((dim, length), BF16)]
    (zt,) = call(turn, "turn", (shaped(dim, length),), meta, (zb,), store, took=2, after=[lse])
    mixed, mixed_t = call(
        mix,
        "mix",
        (shaped(half, dim), shaped(dim, half)),
        meta,
        (o_own, o_came),
        [pltpu.VMEM((dim, half), BF16)],
        took=2,
        after=[zt],
    )
    rest_block = column(dim, dim, lambda step: 0)
    total_f32 = shaped(half, dim, dtype=F32)
    tokens = whole(half, dim)

    later = column(chunk, dim, lambda k: jnp.maximum(k - 2, 0))
    turned = whole(dim, half)
    active, dpre, zt_natural, zt_two, resid, dresid, db, dm_away, dm_mine = call(
        feed,
        "feed",
        (shaped(half, wide),) * 2
        + (shaped(dim, half),) * 2
        + (total_f32, total_f32, shaped(half, dim), shaped(half, group), shaped(half, group)),
        meta,
        (own, mixed, gains, rest, rest, rest, upstream),
        [pltpu.VMEM((half, dim), BF16), pltpu.VMEM((half, dim), F32)],
        took=20,
        grid=(4,),
        specs=[
            tokens,
            tokens,
            whole(16, dim),
            rest_block,
            column(dim, dim, lambda k: 1 + 2 * k),
            column(dim, dim, lambda k: 2 + 2 * k),
            tokens,
        ],
        out_specs=[column(half, dim)] * 2 + [turned] * 2 + [tokens] * 3 + [whole(half, group)] * 2,
    )
    dm_came = lax.ppermute(dm_away, "seq", SWAP)
    grad_first, up_keep, up_send, down_keep, down_send, mixed_keep, mixed_send = call(
        hidden_back,
        "hidden_back",
        (shaped(dim, 4 * dim),) + (shaped(chunk, 2 * dim),) * 4 + (shaped(chunk, dim),) * 2,
        meta,
        (zt_natural, zt_two, active, dpre, upstream, mixed_t, db),
        [pltpu.VMEM((dim, half), BF16), pltpu.VMEM((dim, half), BF16)],
        took=12,
        grid=(4,),
        specs=[turned, turned, column(half, dim), column(half, dim), tokens, turned, tokens],
        out_specs=[column(dim, 2 * dim, lambda k: jnp.minimum(k, 1))] + [later] * 4 + [whole(chunk, dim)] * 2,
    )
    dm_came = pinned(dm_came, up_keep)

    def blocks_of(part):
        return part.reshape(4, 2, rows, -1)

    marks = [[], [], []]
    if direct:
        first_sum = lax.psum_scatter(pinned(grad_first, dm_came), "fsdp", scatter_dimension=0, tiled=True)
        up_came, down_came, mixed_came = (
            flipped(pinned(part, dm_came), parts, 1) for part in (up_send, down_send, mixed_send)
        )
    def attend_back_call(pair, outs, out_specs, extra, after):
        width = (9 if pair == 2 else 3) * PAIR
        pick = lambda step: pair
        return call(
            functools.partial(attend_back, pair),
            "attend_back",
            (shaped(chunk, width), shaped(chunk, width)) + outs,
            meta,
            (qkv, o_own, o_other, dm_mine, dm_came, lse, zt, weight, *extra),
            [
                pltpu.VMEM((2, length, PAIR), BF16),
                pltpu.VMEM((2, length, PAIR), BF16),
                pltpu.VMEM((PAIR, length), BF16),
                pltpu.VMEM((length, PAIR), BF16),
                pltpu.VMEM((8, length), F32),
                pltpu.VMEM((length, PAIR), F32),
                pltpu.VMEM((length, PAIR), F32),
                pltpu.VMEM((PAIR, BAND), F32),
                pltpu.VMEM((length, 3 * PAIR), BF16),
                pltpu.VMEM((2, length, BAND), F32),
                pltpu.VMEM((2, length, BAND), F32),
                pltpu.VMEM((2, length, BAND), BF16),
                pltpu.VMEM((2, length, BAND), BF16),
            ],
            took=10,
            after=after,
            grid=(1,),
            specs=[column(length, 3 * PAIR, pick)]
            + [column(half, PAIR, pick)] * 4
            + [
                pl.BlockSpec((1, 8, length), lambda step: (pair, 0, 0)),
                whole(dim, length),
                column(dim, 3 * PAIR, pick),
            ]
            + [whole(*part.shape) for part in extra],
            out_specs=[whole(chunk, width)] * 2 + out_specs,
        )

    one = (shaped(length, 3 * PAIR),)
    keep_0, send_0, token_0 = attend_back_call(0, one, [whole(length, 3 * PAIR)], (), marks[0])
    if direct:
        pairs = ((up_keep, up_came), (down_keep, down_came), (mixed_keep, mixed_came))
        up_red, down_red, mixed_red = (
            Reduction([blocks_of(part) for part in (keep, pinned(came, token_0))], parts, place) for keep, came in pairs
        )
        marks[1] += [up_red.go(2), down_red.go("seq"), mixed_red.go("seq")]
    keep_1, send_1, token_1 = attend_back_call(1, one, [whole(length, 3 * PAIR)], (), marks[1] + [token_0])
    marks[2].append(token_1)
    joint_keep, joint_send, token_2 = attend_back_call(
        2, one, [whole(length, 3 * PAIR)], (keep_0, send_0, keep_1, send_1), marks[2]
    )
    if direct:
        reds = (up_red, down_red, mixed_red)
        joint_send, *cames = lax.optimization_barrier((joint_send, *(red.came for red in reds)))
        for red, came in zip(reds, cames):
            red.terms.append(came)
    marks = []
    marks = []
    if direct:
        joint_came = flipped(joint_send, parts, 1)
        joint_red = Reduction([blocks_of(part) for part in (joint_keep, joint_came)], parts, place)
        marks = [up_red.go("seq"), down_red.go(2), mixed_red.go(2), joint_red.go(2)]
    sent, own_part = call(
        token_back,
        "token_back",
        (shaped(half, dim), total_f32),
        meta,
        (token_0, token_1, token_2, weight),
        took=5,
        after=marks,
    )
    other_part = lax.ppermute(sent, "seq", SWAP)

    def forward_call(late, before, after):
        at = 2 * late
        return call(
            forward_out,
            "forward_out",
            (shaped(half, dim) if late else total_f32,),
            meta,
            (before, active, rest),
            [pltpu.VMEM((half, dim), F32)],
            took=3,
            after=after,
            grid=(2,),
            specs=[tokens, column(half, dim, lambda k: at + k), column(dim, dim, lambda k: 2 + 2 * (at + k))],
            out_specs=[tokens],
        )

    marks = [own_part]
    if direct:
        joint_red.take(own_part)
        joint_sum = rounded_sum(joint_red.terms).reshape(4, rows, -1)
        marks.append(joint_sum)
    (out,) = forward_call(0, resid, marks)
    marks = []
    if direct:
        last_sum = []
        for red in (up_red, down_red, mixed_red):
            red.take(out)
            last_sum.append(rounded_sum(red.terms))
        last_sum = jnp.concatenate(last_sum, axis=-1).reshape(4, rows, -1)
        deep = me // 4
        last_parts = [lax.dynamic_index_in_dim(last_sum, deep, 0, keepdims=False)]
        for far in (1, 2, 3):
            away = lax.dynamic_index_in_dim(last_sum, deep ^ far, 0, keepdims=False)
            last_parts.append(flipped(away, parts, 4 * far))
            marks.append(away)
        joint_sum = exchanged(joint_sum, parts)
    (out,) = forward_call(1, out, marks)
    marks = [out]
    (input_grad,) = call(
        input_back, "input_back", (total_f32,), meta, (own, own_part, other_part, dresid, gains), after=marks
    )

    if direct:
        last_sum = rounded_sum(last_parts)
        joint_sum = jnp.sum(pinned(joint_sum, out).astype(F32), axis=0).astype(BF16)
    else:

        def scattered(keep, send):
            blocks = jnp.stack([keep, send]).reshape(2, 4, 2, dim // 16, -1).transpose(1, 2, 0, 3, 4).reshape(dim, -1)
            return lax.psum_scatter(blocks, "fsdp", scatter_dimension=0, tiled=True)

        first_sum = lax.psum_scatter(grad_first, "fsdp", scatter_dimension=0, tiled=True)
        last_sum = ((up_keep, up_send), (down_keep, down_send), (mixed_keep, mixed_send))
        last_sum = jnp.concatenate([scattered(*pair) for pair in last_sum], axis=1)
        joint_sum = scattered(joint_keep, joint_send)
    first_sum = pinned(first_sum, input_grad)
    first_sum, last_sum, joint_sum = ((part, lax.ppermute(part, "seq", SWAP)) for part in (first_sum, last_sum, joint_sum))
    joint_grad, lead_grad = call(
        joint_out,
        "joint_out",
        (shaped(rows, triple, dtype=F32), shaped(1, rows, dtype=F32)),
        meta,
        (*joint_sum, joint_weight, lead_gain[None, :]),
        took=2,
    )
    up_grad, down_grad, output_grad, tail_grad = call(
        functools.partial(feed_out, direct),
        "feed_out",
        (
            shaped(rows, wide, dtype=F32),
            shaped(4 * rows, dim, dtype=F32),
            shaped(rows, dim, dtype=F32),
            shaped(1, rows, dtype=F32),
        ),
        meta,
        (*first_sum, *last_sum, up_weight, tail_gain[None, :]),
        after=[joint_grad],
    )
    return (
        out[None],
        input_grad[None],
        lead_grad[0],
        joint_grad,
        output_grad,
        tail_grad[0],
        up_grad,
        down_grad,
    )


def solution(mesh):
    split = P("fsdp", "seq", None)
    placed = (split, P("fsdp"), P("fsdp", None), P("fsdp", None), P("fsdp"), P("fsdp", None), P("fsdp", None), split)
    return jax.shard_map(
        body,
        mesh=mesh,
        in_specs=placed,
        out_specs=(split, split, P("fsdp"), P("fsdp", None), P("fsdp", None), P("fsdp"), P("fsdp", None), P("fsdp", None)),
        check_vma=False,
    )
```

```python
import functools

import jax
import jax.numpy as jnp
from jax import lax
from jax.experimental import pallas as pl
from jax.experimental.pallas import tpu as pltpu
from jax.sharding import PartitionSpec as P

HD = 64
EPS = 1e-05
PAIR = 2 * HD
BAND = 256
LOG2E = 1.4426950408889634
LIMIT = 56 << 20
F32 = jnp.float32
BF16 = jnp.bfloat16

VMEM = pl.BlockSpec(memory_space=pltpu.VMEM)
SMEM = pl.BlockSpec(memory_space=pltpu.SMEM)
ANY = pl.BlockSpec(memory_space=pl.ANY)


def dot(left, right):
    return jnp.dot(left, right, preferred_element_type=F32)


def dot_t(left, right):
    return lax.dot_general(left, right, (((1,), (1,)), ((), ())), preferred_element_type=F32)


def shaped(*dims, dtype=BF16):
    return jax.ShapeDtypeStruct(dims, dtype)


def cost(microseconds):
    return pl.CostEstimate(flops=int(microseconds * 1e7), transcendentals=0, bytes_accessed=int(microseconds * 3e4))


def waiting(kernel, fixed, after):
    def run(*refs):
        kernel(*refs[:fixed], *refs[fixed + after :])

    return run


def whole(*dims):
    return pl.BlockSpec(dims, lambda *_: (0,) * len(dims))


def column(rows, columns, pick=lambda step: step):
    return pl.BlockSpec((rows, columns), lambda *steps: (0, pick(*steps)))


def call(kernel, name, outs, meta, inputs, scratch=(), took=4, after=(), grid=(), specs=None, out_specs=None):
    return pl.pallas_call(
        waiting(kernel, 1 + len(inputs), len(after)),
        name=name,
        grid=grid,
        out_shape=outs,
        in_specs=[SMEM] + list(specs or [VMEM] * len(inputs)) + [ANY] * len(after),
        out_specs=list(out_specs or [VMEM] * len(outs)),
        scratch_shapes=list(scratch),
        compiler_params=pltpu.CompilerParams(vmem_limit_bytes=LIMIT),
        cost_estimate=cost(took),
    )(meta, *inputs, *after)


def standardize(values):
    center = values - jnp.mean(values, axis=-1, keepdims=True)
    spread = jnp.mean(center * center, axis=-1, keepdims=True)
    rstd = lax.rsqrt(spread + EPS)
    return center * rstd, rstd


def norm_back(z, rstd, g):
    return (g - jnp.mean(g, axis=-1, keepdims=True) - z * jnp.mean(g * z, axis=-1, keepdims=True)) * rstd


def half_at(index, size):
    return pl.ds(pl.multiple_of(index * size, size), size)


def rows_in_order(meta, source, target):
    size = source.shape[0] // 16
    for spot in range(16):
        rows = pl.ds(pl.multiple_of(meta[1 + spot] * size, size), size)
        target[spot * size : (spot + 1) * size, :] = source[rows, :]


def placed(meta, near, far, target):
    size = target.shape[0] // 16
    for spot in range(16):
        source = (near, far)[spot // 8]
        rows = pl.ds(pl.multiple_of(meta[17 + spot] * size, size), size)
        target[rows, :] = source[spot % 8 * size : (spot % 8 + 1) * size, :]


def first_norm(meta, own, other, z):
    half = own.shape[0]
    for source, place in ((own, meta[0]), (other, 1 - meta[0])):
        z[half_at(place, half), :] = standardize(source[...].astype(F32))[0]


def first_scale(meta, z, near, far, zb, gains, columns):
    placed(meta, near, far, columns)
    gains[...] = columns[...].T[:16, :]
    zb[...] = (z[...] * gains[0:1, :].astype(F32)).astype(BF16)


def turn(meta, zb, zt, turned):
    turned[...] = zb[...].T
    rows_in_order(meta, turned, zt)


def mix(meta, mine, other, mixed, mt, turned):
    width = mine.shape[1]
    for side, source in ((meta[0], mine), (1 - meta[0], other)):
        mixed[:, half_at(side, width)] = source[...]
    turned[...] = mixed[...].T
    rows_in_order(meta, turned, mt)


def attend(meta, zb, near, far, qkv, o_own, o_other, lse, weight, km, vt, s_sc, ot, o_all):
    length = zb.shape[0]
    half = length // 2
    placed(meta, near, far, weight)
    qkv[...] = dot(zb[...], weight[...]).astype(BF16)
    lane = lax.broadcasted_iota(jnp.int32, (1, PAIR), 1)
    keys = qkv[:, PAIR : 2 * PAIR]
    zero = jnp.zeros_like(keys)
    km[0] = jnp.where(lane < HD, keys, zero)
    km[1] = jnp.where(lane < HD, zero, keys)
    vt[...] = qkv[:, 2 * PAIR :].T
    lse[0] = jnp.zeros(lse.shape[1:], F32)
    allowed = lax.broadcasted_iota(jnp.int32, (BAND, BAND), 0) <= lax.broadcasted_iota(jnp.int32, (BAND, BAND), 1)

    def q_step(q_band, _):
        spots = half_at(q_band, BAND)
        queries = qkv[spots, :PAIR]

        def score(k_band, tops, diagonal):
            rows = half_at(k_band, BAND)
            peaks = []
            for head in range(2):
                s = dot_t(km[head, rows, :], queries) * (HD ** -0.5 * LOG2E)
                if diagonal:
                    s = jnp.where(allowed, s, 0.0)
                s_sc[head, rows, :] = s
                peaks.append(jnp.maximum(tops[head], jnp.max(jnp.abs(s), axis=0, keepdims=True)))
            return tuple(peaks)

        def weigh(k_band, carry, tops, diagonal):
            rows = half_at(k_band, BAND)
            results = []
            for head, (total, out) in enumerate(carry):
                s = s_sc[head, rows, :]
                grow = jnp.exp2(s - tops[head])
                shrink = jnp.exp2(-s - tops[head])
                both = grow + shrink
                if diagonal:
                    both = jnp.where(allowed, both, 0.0)
                part = dot(vt[head * HD : (head + 1) * HD, rows], (grow - shrink).astype(BF16))
                results.append((total + jnp.sum(both, axis=0, keepdims=True), out + part))
            return tuple(results)

        none = jnp.zeros((1, BAND), F32)
        tops = score(q_band, (none, none), True)
        tops = lax.fori_loop(0, q_band, lambda k_band, tops: score(k_band, tops, False), tops)
        start = (none, jnp.zeros((HD, BAND), F32))
        carry = weigh(q_band, (start, start), tops, True)
        carry = lax.fori_loop(0, q_band, lambda k_band, carry: weigh(k_band, carry, tops, False), carry)
        for head, (total, out) in enumerate(carry):
            ot[head * HD : (head + 1) * HD, :] = out / total
            lse[0, head : head + 1, spots] = tops[head] + jnp.log2(0.5 * total)
        o_all[spots, :] = ot[...].T.astype(BF16)
        return 0

    lax.fori_loop(0, length // BAND, q_step, 0)
    o_own[...] = o_all[half_at(meta[0], half), :]
    o_other[...] = o_all[half_at(1 - meta[0], half), :]


def attend_back(pair, meta, qkv, o_own, o_other, d_own, d_other, lse, zt, weight, *refs):
    last = pair == 2
    count = (0, 0, 4)[pair]
    extra, refs = refs[:count], refs[count:]
    keep, send, *outs = refs[:3]
    km, vm, kt, do, inner, dk, dv, dqt, dqkv, s_sc, w_sc, p_sc, ds_sc = refs[3:]
    length = qkv.shape[0]
    half = length // 2
    lane = lax.broadcasted_iota(jnp.int32, (1, PAIR), 1)
    low = lane < HD
    keys = qkv[:, PAIR : 2 * PAIR]
    values = qkv[:, 2 * PAIR :]
    zero = jnp.zeros_like(keys)
    km[0] = jnp.where(low, keys, zero)
    km[1] = jnp.where(low, zero, keys)
    vm[0] = jnp.where(low, values, zero)
    vm[1] = jnp.where(low, zero, values)
    kt[...] = keys.T
    pick = (
        lax.broadcasted_iota(jnp.int32, (8, PAIR), 1) // HD == lax.broadcasted_iota(jnp.int32, (8, PAIR), 0)
    ).astype(F32)
    for o_part, d_part, place in ((o_own, d_own, meta[0]), (o_other, d_other, 1 - meta[0])):
        do[half_at(place, half), :] = d_part[...]
        product = o_part[...].astype(F32) * d_part[...].astype(F32)
        inner[:, half_at(place, half)] = lax.dot_general(
            pick, product, (((1,), (1,)), ((), ())), preferred_element_type=F32, precision=lax.Precision.HIGHEST
        )
    allowed = lax.broadcasted_iota(jnp.int32, (BAND, BAND), 0) <= lax.broadcasted_iota(jnp.int32, (BAND, BAND), 1)
    for q_band in range(length // BAND):
        spots = slice(q_band * BAND, (q_band + 1) * BAND)
        end = (q_band + 1) * BAND
        queries = qkv[spots, :PAIR]
        upstream = do[spots, :]
        small = jnp.zeros_like(queries)
        for head in range(2):
            mine = slice(head * HD, (head + 1) * HD)
            q_mine = jnp.where(low, queries, small) if head == 0 else jnp.where(low, small, queries)
            d_mine = jnp.where(low, upstream, small) if head == 0 else jnp.where(low, small, upstream)
            base = lse[0, head : head + 1, spots] + 1.0
            mean = inner[head : head + 1, spots]
            s_sc[head, :end, :] = dot_t(km[head, :end, :], queries)
            w_sc[head, :end, :] = dot_t(vm[head, :end, :], upstream)
            for k_band in range(q_band + 1):
                rows = slice(k_band * BAND, (k_band + 1) * BAND)
                s = s_sc[head, rows, :] * (HD ** -0.5 * LOG2E)
                dw = w_sc[head, rows, :]
                if k_band == q_band:
                    s = jnp.where(allowed, s, 0.0)
                    dw = jnp.where(allowed, dw, 0.0)
                grow = jnp.exp2(s - base)
                shrink = jnp.exp2(-s - base)
                p = grow - shrink
                p_sc[head, rows, :] = p.astype(BF16)
                ds_sc[head, rows, :] = ((grow + shrink) * dw - p * mean).astype(BF16)
            dv_part = dot(p_sc[head, :end, :], d_mine)
            dk_part = dot(ds_sc[head, :end, :], q_mine)
            dqt[mine, :] = dot(kt[mine, :end], ds_sc[head, :end, :])
            old = q_band * BAND if head == 0 else end
            if old:
                dv[:old, :] += dv_part[:old]
                dk[:old, :] += dk_part[:old]
            if head == 0:
                dv[old:end, :] = dv_part[old:]
                dk[old:end, :] = dk_part[old:]
        dqkv[spots, :PAIR] = (dqt[...].T * HD ** -0.5).astype(BF16)
    dqkv[:, PAIR : 2 * PAIR] = (dk[...] * HD ** -0.5).astype(BF16)
    dqkv[:, 2 * PAIR :] = dv[...].astype(BF16)
    middle = keep.shape[0]
    start = keep.shape[1] - 3 * PAIR
    send[:, start:] = dot(zt[middle:, :], dqkv[...]).astype(BF16)
    keep[:, start:] = dot(zt[:middle, :], dqkv[...]).astype(BF16)
    if last:
        for spot in range(2):
            columns = slice(spot * 3 * PAIR, (spot + 1) * 3 * PAIR)
            keep[:, columns] = extra[2 * spot][...]
            send[:, columns] = extra[2 * spot + 1][...]
    outs[0][...] = dqkv[...]


def token_back(meta, t0, t1, t2, weight, away, mine_out):
    half = away.shape[0]
    for side, target in ((1 - meta[0], away), (meta[0], mine_out)):
        part = None
        for spot, token in enumerate((t0, t1, t2)):
            columns = slice(spot * 3 * PAIR, (spot + 1) * 3 * PAIR)
            new = dot_t(token[half_at(side, half), :], weight[:, columns])
            part = new if part is None else part + new
        target[...] = part.astype(target.dtype)


def added(step, total, first, part):
    @pl.when(step == 0)
    def _():
        total[...] = part if first is None else first[...] + part

    @pl.when(step > 0)
    def _():
        total[...] += part


def feed(
    meta, own, mixed, gains, weight, up, down, upstream,
    active, dpre, first, zt, resid, dresid, db, away, mine_out, zb, zt_natural, g_total, turned,
):
    step = pl.program_id(0)
    gain = gains[1:2, :].astype(F32)

    @pl.when(step == 0)
    def _():
        summed = own[...].astype(F32) + dot(mixed[...], weight[...])
        resid[...] = summed
        z = (standardize(summed)[0] * gain).astype(BF16)
        zb[...] = z
        zt_natural[...] = z.T
        rows_in_order(meta, zt_natural, zt)

    width = active.shape[1]
    root = 0.7978845608028654
    for part in range(3):
        mine = slice(part * width // 3, (part + 1) * width // 3)
        v = dot(zb[...], up[:, mine])
        slope_in = dot_t(upstream[...], down[mine, :])
        square = v * v
        t = jnp.tanh(root * v * (1.0 + 0.044715 * square))
        cdf = 0.5 * (1.0 + t)
        active[:, mine] = (v * cdf).astype(BF16)
        slope = cdf + v * (0.5 * root) * (1.0 - t * t) * (1.0 + 0.134145 * square)
        dpre[:, mine] = (slope_in * slope).astype(BF16)
    added(step, g_total, None, dot_t(dpre[...], up[...]))

    @pl.when(step < 2)
    def _():
        turned[...] = active[...].T
        first[:, :width] = dot(zt_natural[...], dpre[...]).astype(BF16)
        first[:, width:] = dot(turned[...], upstream[...]).astype(BF16)

    @pl.when(step == pl.num_programs(0) - 1)
    def _():
        z, rstd = standardize(resid[...])
        grad = upstream[...].astype(F32) + norm_back(z, rstd, g_total[...] * gain)
        low = grad.astype(BF16)
        for side, target in ((1 - meta[0], away), (meta[0], mine_out)):
            target[...] = dot_t(low, weight[half_at(side, 3 * PAIR), :]).astype(BF16)
        dresid[...] = grad
        db[...] = low


def hidden_back(
    meta, zt, active, dpre, upstream, mt, db,
    up_keep, up_send, down_keep, down_send, mixed_keep, mixed_send, turned, picked,
):
    step = pl.program_id(0)
    width = active.shape[1]
    turned[...] = active[...].T
    rows_in_order(meta, turned, picked)
    size = width // 2
    for spot, (up_part, down_part) in enumerate(((up_keep, down_keep), (up_send, down_send))):
        mine = slice(spot * size, (spot + 1) * size)
        up_part[...] = dot(zt[mine, :], dpre[...]).astype(BF16)
        down_part[...] = dot(picked[mine, :], upstream[...]).astype(BF16)

    @pl.when(step == pl.num_programs(0) - 1)
    def _():
        mixed_send[...] = dot(mt[size:, :], db[...]).astype(BF16)
        mixed_keep[...] = dot(mt[:size, :], db[...]).astype(BF16)


def forward_out(meta, before, active, down, out, total):
    step = pl.program_id(0)
    added(step, total, before, dot(active[...], down[...]))

    @pl.when(step == pl.num_programs(0) - 1)
    def _():
        out[...] = total[...].astype(out.dtype)


def input_back(meta, own, mine, other, dresid, gains, out):
    z, rstd = standardize(own[...].astype(F32))
    g = (mine[...] + other[...].astype(F32)) * gains[0:1, :].astype(F32)
    out[...] = dresid[...] + norm_back(z, rstd, g)


def row_sums(values):
    ones = jnp.ones((8, values.shape[1]), F32)
    sums = lax.dot_general(
        ones, values, (((1,), (1,)), ((), ())), preferred_element_type=F32, precision=lax.Precision.HIGHEST
    )
    return sums[0:1, :]


def joint_out(meta, own, other, weight, gain, grad, gain_grad):
    for side, source in ((meta[0], own), (1 - meta[0], other)):
        for pair in range(3):
            for kind in range(3):
                columns = pl.ds(pl.multiple_of((kind * 6 + side * 3 + pair) * PAIR, PAIR), PAIR)
                at = (pair * 3 + kind) * PAIR
                grad[:, columns] = source[:, at : at + PAIR].astype(F32)
    gain_grad[...] = row_sums(grad[...] * weight[...].astype(F32)) / gain[...].astype(F32)


def feed_out(split, meta, first, first_too, last, last_too, weight, gain, up, down, output, gain_grad):
    rows, dim = output.shape
    if split:
        width = dim // 2
        for side, source in ((meta[0], last), (1 - meta[0], last_too)):
            output[:, half_at(side, width)] = source[:, 2 * dim :].astype(F32)
    else:
        output[...] = last[:, -dim:].astype(F32) + last_too[:, -dim:].astype(F32)
    for k in range(4):
        parts = []
        for kind in range(2):
            if k < 2 or not split:
                one, two = (first, first_too) if k < 2 else (last, last_too)
                at = ((2 * k + kind) if k < 2 else (2 * kind + k - 2)) * dim
                parts.append(one[:, at : at + dim].astype(F32) + two[:, at : at + dim].astype(F32))
            else:
                at = kind * dim
                parts.append(jnp.where(meta[0] == k - 2, last[:, at : at + dim], last_too[:, at : at + dim]).astype(F32))
        for owner in range(dim // rows):
            up[:, (4 * owner + k) * rows : (4 * owner + k + 1) * rows] = parts[0][:, owner * rows : (owner + 1) * rows]
        down[k * rows : (k + 1) * rows, :] = parts[1]
    gain_grad[...] = row_sums(up[...] * weight[...].astype(F32)) / gain[...].astype(F32)


SWAP = [(0, 1), (1, 0)]


def flipped(array, parts, bit):
    return lax.ppermute(array, "fsdp", [(spot, spot ^ bit) for spot in range(parts)])


def exchanged(blocks, parts):
    groups = [list(range(side, parts, 4)) for side in range(4)]
    return lax.all_to_all(blocks, "fsdp", 0, 0, axis_index_groups=groups, tiled=True)


def rounded_sum(terms):
    total = terms[0].astype(F32)
    for term in terms[1:]:
        total = total + term.astype(F32)
    return total.astype(BF16)


def pinned(array, mark):
    return lax.optimization_barrier((array, mark))[0]


class Reduction:
    def __init__(self, terms, parts, place):
        self.terms, self.parts, self.place = terms, parts, place

    def go(self, step):
        if step == "seq":
            width = self.terms[0].shape[3] // 2
            away = rounded_sum(
                [lax.dynamic_slice_in_dim(term, (1 - self.place) * width, width, 3) for term in self.terms]
            )
            self.terms = [lax.dynamic_slice_in_dim(term, self.place * width, width, 3) for term in self.terms]
            self.came = lax.ppermute(away, "seq", SWAP)
        else:
            away = rounded_sum([term[:, 1:] for term in self.terms])
            self.terms = [term[:, :1] for term in self.terms]
            self.came = flipped(away, self.parts, 2)
        return away

    def take(self, mark):
        self.terms.append(pinned(self.came, mark))


def body(block_input, lead_gain, joint_weight, output_weight, tail_gain, up_weight, down_weight, cotangent):
    rows, triple = joint_weight.shape
    dim = block_input.shape[2]
    wide = up_weight.shape[1]
    half = block_input.shape[1]
    length = 2 * half
    parts = dim // rows
    group = triple // 6
    chunk = dim // 2
    place = lax.axis_index("seq")
    me = lax.axis_index("fsdp")
    direct = parts == 16
    base = me if direct else jnp.zeros_like(me)
    spots = jnp.arange(16, dtype=jnp.int32)
    few = jnp.arange(8, dtype=jnp.int32)
    eight = (few % 2) * 8 + (few // 2 % 2) * 4 + few // 4 * 2
    meta = jnp.concatenate(
        [
            place[None],
            spots % 8 // 2 * 4 + ((base % 4) ^ (spots % 2 * 2 + spots // 8)),
            base ^ jnp.concatenate([eight, eight ^ 1]) if direct else spots,
        ]
    ).astype(jnp.int32)

    joint_own = lax.dynamic_index_in_dim(joint_weight.reshape(rows, 3, 2, group), place, 2, keepdims=False)
    joint_own = joint_own.reshape(rows, 3, 3, PAIR).transpose(0, 2, 1, 3).reshape(rows, 3 * group)
    up_turned = up_weight.reshape(rows, parts, 4, rows).transpose(2, 0, 1, 3).reshape(4, rows, dim)
    down_turned = down_weight.reshape(4, rows, dim)
    hidden = [part[k] for k in range(4) for part in (up_turned, down_turned)]

    own = block_input[0]
    upstream = cotangent[0]
    rest = lax.all_gather(jnp.concatenate([output_weight, *hidden], axis=1), "fsdp", axis=0, tiled=True)
    other = lax.ppermute(own, "seq", SWAP)
    both_gains = jnp.pad(jnp.stack([lead_gain, tail_gain], axis=1), ((0, 0), (0, PAIR - 2)))
    first = jnp.concatenate([joint_own, both_gains], axis=1)
    if direct:
        for bit in (8, 4, 2):
            if bit == 2:
                first, other = lax.optimization_barrier((first, other))
            first = jnp.concatenate([first, flipped(first, parts, bit)], axis=0)
        firsts = (first, flipped(first, parts, 1))
    else:
        first = lax.all_gather(first, "fsdp", axis=0, tiled=True)
        firsts = (first[:chunk], first[chunk:])

    (z_one,) = call(first_norm, "first_norm", (shaped(length, dim, dtype=F32),), meta, (own, other), took=3)
    zb, gains = call(
        first_scale,
        "first_scale",
        (shaped(length, dim), shaped(16, dim)),
        meta,
        (z_one, *firsts),
        [pltpu.VMEM((dim, PAIR), BF16)],
        took=2,
        grid=(1,),
        specs=[VMEM] + [column(chunk, PAIR, lambda step: 9)] * 2,
    )
    triples = column(length, 3 * PAIR)
    pair_tokens = column(half, PAIR)
    lse_spec = pl.BlockSpec((1, 8, length), lambda step: (step, 0, 0))
    qkv, o_own, o_other, lse, weight = call(
        attend,
        "attend",
        (
            shaped(length, 9 * PAIR),
            shaped(half, group),
            shaped(half, group),
            shaped(3, 8, length, dtype=F32),
            shaped(dim, 9 * PAIR),
        ),
        meta,
        (zb, *firsts),
        [
            pltpu.VMEM((2, length, PAIR), BF16),
            pltpu.VMEM((PAIR, length), BF16),
            pltpu.VMEM((2, length, BAND), F32),
            pltpu.VMEM((PAIR, BAND), F32),
            pltpu.VMEM((length, PAIR), BF16),
        ],
        took=22,
        grid=(3,),
        specs=[whole(length, dim)] + [column(chunk, 3 * PAIR)] * 2,
        out_specs=[triples, pair_tokens, pair_tokens, lse_spec, column(dim, 3 * PAIR)],
    )
    o_came = lax.ppermute(o_other, "seq", SWAP)
    store = [pltpu.VMEM((dim, length), BF16)]
    (zt,) = call(turn, "turn", (shaped(dim, length),), meta, (zb,), store, took=2, after=[lse])
    mixed, mixed_t = call(
        mix,
        "mix",
        (shaped(half, dim), shaped(dim, half)),
        meta,
        (o_own, o_came),
        [pltpu.VMEM((dim, half), BF16)],
        took=2,
        after=[zt],
    )
    rest_block = column(dim, dim, lambda step: 0)
    total_f32 = shaped(half, dim, dtype=F32)
    tokens = whole(half, dim)

    turned = whole(dim, half)
    active, dpre, grad_first, zt_two, resid, dresid, db, dm_away, dm_mine = call(
        feed,
        "feed",
        (shaped(half, wide),) * 2
        + (shaped(dim, 4 * dim), shaped(dim, half))
        + (total_f32, total_f32, shaped(half, dim), shaped(half, group), shaped(half, group)),
        meta,
        (own, mixed, gains, rest, rest, rest, upstream),
        [
            pltpu.VMEM((half, dim), BF16),
            pltpu.VMEM((dim, half), BF16),
            pltpu.VMEM((half, dim), F32),
            pltpu.VMEM((dim, half), BF16),
        ],
        took=20,
        grid=(4,),
        specs=[
            tokens,
            tokens,
            whole(16, dim),
            rest_block,
            column(dim, dim, lambda k: 1 + 2 * k),
            column(dim, dim, lambda k: 2 + 2 * k),
            tokens,
        ],
        out_specs=[column(half, dim)] * 2
        + [column(dim, 2 * dim, lambda k: jnp.minimum(k, 1)), turned]
        + [tokens] * 3 + [whole(half, group)] * 2,
    )
    dm_came = lax.ppermute(dm_away, "seq", SWAP)
    up_keep, up_send, down_keep, down_send, mixed_keep, mixed_send = call(
        hidden_back,
        "hidden_back",
        (shaped(chunk, 2 * dim),) * 4 + (shaped(chunk, dim),) * 2,
        meta,
        (zt_two, active, dpre, upstream, mixed_t, db),
        [pltpu.VMEM((dim, half), BF16), pltpu.VMEM((dim, half), BF16)],
        took=7,
        grid=(2,),
        specs=[turned] + [column(half, dim, lambda k: k + 2)] * 2 + [tokens, turned, tokens],
        out_specs=[column(chunk, dim)] * 4 + [whole(chunk, dim)] * 2,
    )
    dm_came = pinned(dm_came, up_keep)

    def blocks_of(part):
        return part.reshape(4, 2, rows, -1)

    marks = [[], [], []]
    if direct:
        first_sum = lax.psum_scatter(grad_first, "fsdp", scatter_dimension=0, tiled=True)
        up_came, down_came, mixed_came = (
            flipped(pinned(part, dm_came), parts, 1) for part in (up_send, down_send, mixed_send)
        )
    def attend_back_call(pair, outs, out_specs, extra, after):
        width = (9 if pair == 2 else 3) * PAIR
        pick = lambda step: pair
        return call(
            functools.partial(attend_back, pair),
            "attend_back",
            (shaped(chunk, width), shaped(chunk, width)) + outs,
            meta,
            (qkv, o_own, o_other, dm_mine, dm_came, lse, zt, weight, *extra),
            [
                pltpu.VMEM((2, length, PAIR), BF16),
                pltpu.VMEM((2, length, PAIR), BF16),
                pltpu.VMEM((PAIR, length), BF16),
                pltpu.VMEM((length, PAIR), BF16),
                pltpu.VMEM((8, length), F32),
                pltpu.VMEM((length, PAIR), F32),
                pltpu.VMEM((length, PAIR), F32),
                pltpu.VMEM((PAIR, BAND), F32),
                pltpu.VMEM((length, 3 * PAIR), BF16),
                pltpu.VMEM((2, length, BAND), F32),
                pltpu.VMEM((2, length, BAND), F32),
                pltpu.VMEM((2, length, BAND), BF16),
                pltpu.VMEM((2, length, BAND), BF16),
            ],
            took=10,
            after=after,
            grid=(1,),
            specs=[column(length, 3 * PAIR, pick)]
            + [column(half, PAIR, pick)] * 4
            + [
                pl.BlockSpec((1, 8, length), lambda step: (pair, 0, 0)),
                whole(dim, length),
                column(dim, 3 * PAIR, pick),
            ]
            + [whole(*part.shape) for part in extra],
            out_specs=[whole(chunk, width)] * 2 + out_specs,
        )

    one = (shaped(length, 3 * PAIR),)
    keep_0, send_0, token_0 = attend_back_call(0, one, [whole(length, 3 * PAIR)], (), marks[0])
    if direct:
        pairs = ((up_keep, up_came), (down_keep, down_came), (mixed_keep, mixed_came))
        up_red, down_red, mixed_red = (
            Reduction([blocks_of(part) for part in (keep, pinned(came, token_0))], parts, place) for keep, came in pairs
        )
        marks[1] += [up_red.go(2), down_red.go("seq"), mixed_red.go("seq")]
    keep_1, send_1, token_1 = attend_back_call(1, one, [whole(length, 3 * PAIR)], (), marks[1] + [token_0])
    marks[2].append(token_1)
    joint_keep, joint_send, token_2 = attend_back_call(
        2, one, [whole(length, 3 * PAIR)], (keep_0, send_0, keep_1, send_1), marks[2]
    )
    if direct:
        reds = (up_red, down_red, mixed_red)
        joint_send, *cames = lax.optimization_barrier((joint_send, *(red.came for red in reds)))
        for red, came in zip(reds, cames):
            red.terms.append(came)
    marks = []
    marks = []
    if direct:
        joint_came = flipped(joint_send, parts, 1)
        joint_red = Reduction([blocks_of(part) for part in (joint_keep, joint_came)], parts, place)
        marks = [up_red.go("seq"), down_red.go(2), mixed_red.go(2), joint_red.go(2)]
    sent, own_part = call(
        token_back,
        "token_back",
        (shaped(half, dim), total_f32),
        meta,
        (token_0, token_1, token_2, weight),
        took=5,
        after=marks,
    )
    other_part = lax.ppermute(sent, "seq", SWAP)

    def forward_call(late, before, after):
        at = 2 * late
        return call(
            forward_out,
            "forward_out",
            (shaped(half, dim) if late else total_f32,),
            meta,
            (before, active, rest),
            [pltpu.VMEM((half, dim), F32)],
            took=3,
            after=after,
            grid=(2,),
            specs=[tokens, column(half, dim, lambda k: at + k), column(dim, dim, lambda k: 2 + 2 * (at + k))],
            out_specs=[tokens],
        )

    marks = [own_part]
    if direct:
        joint_red.take(own_part)
        joint_sum = rounded_sum(joint_red.terms).reshape(4, rows, -1)
        marks.append(joint_sum)
    (out,) = forward_call(0, resid, marks)
    marks = []
    if direct:
        last_sum = []
        for red in (up_red, down_red, mixed_red):
            red.take(out)
            last_sum.append(rounded_sum(red.terms))
        last_sum = jnp.concatenate(last_sum, axis=-1).reshape(4, rows, -1)
        deep = me // 4
        last_parts = [lax.dynamic_index_in_dim(last_sum, deep, 0, keepdims=False)]
        for far in (1, 2, 3):
            away = lax.dynamic_index_in_dim(last_sum, deep ^ far, 0, keepdims=False)
            last_parts.append(flipped(away, parts, 4 * far))
            marks.append(away)
        joint_sum = exchanged(joint_sum, parts)
    (out,) = forward_call(1, out, marks)
    marks = [out]
    (input_grad,) = call(
        input_back, "input_back", (total_f32,), meta, (own, own_part, other_part, dresid, gains), after=marks
    )

    if direct:
        last_sum = rounded_sum(last_parts)
        joint_sum = jnp.sum(pinned(joint_sum, out).astype(F32), axis=0).astype(BF16)
    else:

        def scattered(keep, send):
            blocks = jnp.stack([keep, send]).reshape(2, 4, 2, dim // 16, -1).transpose(1, 2, 0, 3, 4).reshape(dim, -1)
            return lax.psum_scatter(blocks, "fsdp", scatter_dimension=0, tiled=True)

        first_sum = lax.psum_scatter(grad_first, "fsdp", scatter_dimension=0, tiled=True)
        last_sum = ((up_keep, up_send), (down_keep, down_send), (mixed_keep, mixed_send))
        last_sum = jnp.concatenate([scattered(*pair) for pair in last_sum], axis=1)
        joint_sum = scattered(joint_keep, joint_send)
    first_sum = pinned(first_sum, input_grad)
    first_sum, last_sum, joint_sum = ((part, lax.ppermute(part, "seq", SWAP)) for part in (first_sum, last_sum, joint_sum))
    joint_grad, lead_grad = call(
        joint_out,
        "joint_out",
        (shaped(rows, triple, dtype=F32), shaped(1, rows, dtype=F32)),
        meta,
        (*joint_sum, joint_weight, lead_gain[None, :]),
        took=2,
    )
    up_grad, down_grad, output_grad, tail_grad = call(
        functools.partial(feed_out, direct),
        "feed_out",
        (
            shaped(rows, wide, dtype=F32),
            shaped(4 * rows, dim, dtype=F32),
            shaped(rows, dim, dtype=F32),
            shaped(1, rows, dtype=F32),
        ),
        meta,
        (*first_sum, *last_sum, up_weight, tail_gain[None, :]),
        after=[joint_grad],
    )
    return (
        out[None],
        input_grad[None],
        lead_grad[0],
        joint_grad,
        output_grad,
        tail_grad[0],
        up_grad,
        down_grad,
    )


def solution(mesh):
    split = P("fsdp", "seq", None)
    placed = (split, P("fsdp"), P("fsdp", None), P("fsdp", None), P("fsdp"), P("fsdp", None), P("fsdp", None), split)
    return jax.shard_map(
        body,
        mesh=mesh,
        in_specs=placed,
        out_specs=(split, split, P("fsdp"), P("fsdp", None), P("fsdp", None), P("fsdp"), P("fsdp", None), P("fsdp", None)),
        check_vma=False,
    )
```

```python
import functools

import jax
import jax.numpy as jnp
from jax import lax
from jax.experimental import pallas as pl
from jax.experimental.pallas import tpu as pltpu
from jax.sharding import PartitionSpec as P

HD = 64
EPS = 1e-05
PAIR = 2 * HD
BAND = 256
LOG2E = 1.4426950408889634
LIMIT = 56 << 20
F32 = jnp.float32
BF16 = jnp.bfloat16

VMEM = pl.BlockSpec(memory_space=pltpu.VMEM)
SMEM = pl.BlockSpec(memory_space=pltpu.SMEM)
ANY = pl.BlockSpec(memory_space=pl.ANY)


def dot(left, right):
    return jnp.dot(left, right, preferred_element_type=F32)


def dot_t(left, right):
    return lax.dot_general(left, right, (((1,), (1,)), ((), ())), preferred_element_type=F32)


def shaped(*dims, dtype=BF16):
    return jax.ShapeDtypeStruct(dims, dtype)


def cost(microseconds):
    return pl.CostEstimate(flops=int(microseconds * 1e7), transcendentals=0, bytes_accessed=int(microseconds * 3e4))


def waiting(kernel, fixed, after):
    def run(*refs):
        kernel(*refs[:fixed], *refs[fixed + after :])

    return run


def whole(*dims):
    return pl.BlockSpec(dims, lambda *_: (0,) * len(dims))


def column(rows, columns, pick=lambda step: step):
    return pl.BlockSpec((rows, columns), lambda *steps: (0, pick(*steps)))


def call(kernel, name, outs, meta, inputs, scratch=(), took=4, after=(), grid=(), specs=None, out_specs=None):
    return pl.pallas_call(
        waiting(kernel, 1 + len(inputs), len(after)),
        name=name,
        grid=grid,
        out_shape=outs,
        in_specs=[SMEM] + list(specs or [VMEM] * len(inputs)) + [ANY] * len(after),
        out_specs=list(out_specs or [VMEM] * len(outs)),
        scratch_shapes=list(scratch),
        compiler_params=pltpu.CompilerParams(vmem_limit_bytes=LIMIT),
        cost_estimate=cost(took),
    )(meta, *inputs, *after)


def standardize(values):
    center = values - jnp.mean(values, axis=-1, keepdims=True)
    spread = jnp.mean(center * center, axis=-1, keepdims=True)
    rstd = lax.rsqrt(spread + EPS)
    return center * rstd, rstd


def norm_back(z, rstd, g):
    return (g - jnp.mean(g, axis=-1, keepdims=True) - z * jnp.mean(g * z, axis=-1, keepdims=True)) * rstd


def half_at(index, size):
    return pl.ds(pl.multiple_of(index * size, size), size)


def rows_in_order(meta, source, target):
    size = source.shape[0] // 16
    for spot in range(16):
        rows = pl.ds(pl.multiple_of(meta[1 + spot] * size, size), size)
        target[spot * size : (spot + 1) * size, :] = source[rows, :]


def placed(meta, near, far, target):
    size = target.shape[0] // 16
    for spot in range(16):
        source = (near, far)[spot // 8]
        rows = pl.ds(pl.multiple_of(meta[17 + spot] * size, size), size)
        target[rows, :] = source[spot % 8 * size : (spot % 8 + 1) * size, :]


def first_norm(meta, own, other, z):
    half = own.shape[0]
    for source, place in ((own, meta[0]), (other, 1 - meta[0])):
        z[half_at(place, half), :] = standardize(source[...].astype(F32))[0]


def first_scale(meta, z, near, far, zb, gains, columns):
    placed(meta, near, far, columns)
    gains[...] = columns[...].T[:16, :]
    zb[...] = (z[...] * gains[0:1, :].astype(F32)).astype(BF16)


def turn(meta, zb, zt, turned):
    turned[...] = zb[...].T
    rows_in_order(meta, turned, zt)


def mix(meta, mine, other, mixed, mt, turned):
    width = mine.shape[1]
    for side, source in ((meta[0], mine), (1 - meta[0], other)):
        mixed[:, half_at(side, width)] = source[...]
    turned[...] = mixed[...].T
    rows_in_order(meta, turned, mt)


def attend(meta, zb, near, far, qkv, o_own, o_other, lse, weight, km, vt, s_sc, ot, o_all):
    length = zb.shape[0]
    half = length // 2
    placed(meta, near, far, weight)
    qkv[...] = dot(zb[...], weight[...]).astype(BF16)
    lane = lax.broadcasted_iota(jnp.int32, (1, PAIR), 1)
    keys = qkv[:, PAIR : 2 * PAIR]
    zero = jnp.zeros_like(keys)
    km[0] = jnp.where(lane < HD, keys, zero)
    km[1] = jnp.where(lane < HD, zero, keys)
    vt[...] = qkv[:, 2 * PAIR :].T
    lse[0] = jnp.zeros(lse.shape[1:], F32)
    allowed = lax.broadcasted_iota(jnp.int32, (BAND, BAND), 0) <= lax.broadcasted_iota(jnp.int32, (BAND, BAND), 1)

    def q_step(q_band, _):
        spots = half_at(q_band, BAND)
        queries = qkv[spots, :PAIR]

        def score(k_band, tops, diagonal):
            rows = half_at(k_band, BAND)
            peaks = []
            for head in range(2):
                s = dot_t(km[head, rows, :], queries) * (HD ** -0.5 * LOG2E)
                if diagonal:
                    s = jnp.where(allowed, s, 0.0)
                s_sc[head, rows, :] = s
                peaks.append(jnp.maximum(tops[head], jnp.max(jnp.abs(s), axis=0, keepdims=True)))
            return tuple(peaks)

        def weigh(k_band, carry, tops, diagonal):
            rows = half_at(k_band, BAND)
            results = []
            for head, (total, out) in enumerate(carry):
                s = s_sc[head, rows, :]
                grow = jnp.exp2(s - tops[head])
                shrink = jnp.exp2(-s - tops[head])
                both = grow + shrink
                if diagonal:
                    both = jnp.where(allowed, both, 0.0)
                part = dot(vt[head * HD : (head + 1) * HD, rows], (grow - shrink).astype(BF16))
                results.append((total + jnp.sum(both, axis=0, keepdims=True), out + part))
            return tuple(results)

        none = jnp.zeros((1, BAND), F32)
        tops = score(q_band, (none, none), True)
        tops = lax.fori_loop(0, q_band, lambda k_band, tops: score(k_band, tops, False), tops)
        start = (none, jnp.zeros((HD, BAND), F32))
        carry = weigh(q_band, (start, start), tops, True)
        carry = lax.fori_loop(0, q_band, lambda k_band, carry: weigh(k_band, carry, tops, False), carry)
        for head, (total, out) in enumerate(carry):
            ot[head * HD : (head + 1) * HD, :] = out / total
            lse[0, head : head + 1, spots] = tops[head] + jnp.log2(0.5 * total)
        o_all[spots, :] = ot[...].T.astype(BF16)
        return 0

    lax.fori_loop(0, length // BAND, q_step, 0)
    o_own[...] = o_all[half_at(meta[0], half), :]
    o_other[...] = o_all[half_at(1 - meta[0], half), :]


def attend_back(pair, meta, qkv, o_own, o_other, d_own, d_other, lse, zt, weight, *refs):
    last = pair == 2
    count = (0, 0, 4)[pair]
    extra, refs = refs[:count], refs[count:]
    keep, send, *outs = refs[:3]
    km, vm, kt, do, inner, dk, dv, dqt, dqkv, s_sc, w_sc, p_sc, ds_sc = refs[3:]
    length = qkv.shape[0]
    half = length // 2
    lane = lax.broadcasted_iota(jnp.int32, (1, PAIR), 1)
    low = lane < HD
    keys = qkv[:, PAIR : 2 * PAIR]
    values = qkv[:, 2 * PAIR :]
    zero = jnp.zeros_like(keys)
    km[0] = jnp.where(low, keys, zero)
    km[1] = jnp.where(low, zero, keys)
    vm[0] = jnp.where(low, values, zero)
    vm[1] = jnp.where(low, zero, values)
    kt[...] = keys.T
    pick = (
        lax.broadcasted_iota(jnp.int32, (8, PAIR), 1) // HD == lax.broadcasted_iota(jnp.int32, (8, PAIR), 0)
    ).astype(F32)
    for o_part, d_part, place in ((o_own, d_own, meta[0]), (o_other, d_other, 1 - meta[0])):
        do[half_at(place, half), :] = d_part[...]
        product = o_part[...].astype(F32) * d_part[...].astype(F32)
        inner[:, half_at(place, half)] = lax.dot_general(
            pick, product, (((1,), (1,)), ((), ())), preferred_element_type=F32, precision=lax.Precision.HIGHEST
        )
    allowed = lax.broadcasted_iota(jnp.int32, (BAND, BAND), 0) <= lax.broadcasted_iota(jnp.int32, (BAND, BAND), 1)
    for q_band in range(length // BAND):
        spots = slice(q_band * BAND, (q_band + 1) * BAND)
        end = (q_band + 1) * BAND
        queries = qkv[spots, :PAIR]
        upstream = do[spots, :]
        small = jnp.zeros_like(queries)
        for head in range(2):
            mine = slice(head * HD, (head + 1) * HD)
            q_mine = jnp.where(low, queries, small) if head == 0 else jnp.where(low, small, queries)
            d_mine = jnp.where(low, upstream, small) if head == 0 else jnp.where(low, small, upstream)
            base = lse[0, head : head + 1, spots] + 1.0
            mean = inner[head : head + 1, spots]
            s_sc[head, :end, :] = dot_t(km[head, :end, :], queries)
            w_sc[head, :end, :] = dot_t(vm[head, :end, :], upstream)
            for k_band in range(q_band + 1):
                rows = slice(k_band * BAND, (k_band + 1) * BAND)
                s = s_sc[head, rows, :] * (HD ** -0.5 * LOG2E)
                dw = w_sc[head, rows, :]
                if k_band == q_band:
                    s = jnp.where(allowed, s, 0.0)
                    dw = jnp.where(allowed, dw, 0.0)
                grow = jnp.exp2(s - base)
                shrink = jnp.exp2(-s - base)
                p = grow - shrink
                p_sc[head, rows, :] = p.astype(BF16)
                ds_sc[head, rows, :] = ((grow + shrink) * dw - p * mean).astype(BF16)
            dv_part = dot(p_sc[head, :end, :], d_mine)
            dk_part = dot(ds_sc[head, :end, :], q_mine)
            dqt[mine, :] = dot(kt[mine, :end], ds_sc[head, :end, :])
            old = q_band * BAND if head == 0 else end
            if old:
                dv[:old, :] += dv_part[:old]
                dk[:old, :] += dk_part[:old]
            if head == 0:
                dv[old:end, :] = dv_part[old:]
                dk[old:end, :] = dk_part[old:]
        dqkv[spots, :PAIR] = (dqt[...].T * HD ** -0.5).astype(BF16)
    dqkv[:, PAIR : 2 * PAIR] = (dk[...] * HD ** -0.5).astype(BF16)
    dqkv[:, 2 * PAIR :] = dv[...].astype(BF16)
    middle = keep.shape[0]
    start = keep.shape[1] - 3 * PAIR
    send[:, start:] = dot(zt[middle:, :], dqkv[...]).astype(BF16)
    keep[:, start:] = dot(zt[:middle, :], dqkv[...]).astype(BF16)
    if last:
        for spot in range(2):
            columns = slice(spot * 3 * PAIR, (spot + 1) * 3 * PAIR)
            keep[:, columns] = extra[2 * spot][...]
            send[:, columns] = extra[2 * spot + 1][...]
    outs[0][...] = dqkv[...]


def token_back(meta, t0, t1, t2, weight, away, mine_out):
    half = away.shape[0]
    for side, target in ((1 - meta[0], away), (meta[0], mine_out)):
        part = None
        for spot, token in enumerate((t0, t1, t2)):
            columns = slice(spot * 3 * PAIR, (spot + 1) * 3 * PAIR)
            new = dot_t(token[half_at(side, half), :], weight[:, columns])
            part = new if part is None else part + new
        target[...] = part.astype(target.dtype)


def added(step, total, first, part):
    @pl.when(step == 0)
    def _():
        total[...] = part if first is None else first[...] + part

    @pl.when(step > 0)
    def _():
        total[...] += part


def feed(
    meta, own, mixed, gains, weight, up, down, upstream,
    active, dpre, first, zt, resid, dresid, db, away, mine_out, zb, zt_natural, g_total, turned,
):
    step = pl.program_id(0)
    gain = gains[1:2, :].astype(F32)

    @pl.when(step == 0)
    def _():
        summed = own[...].astype(F32) + dot(mixed[...], weight[...])
        resid[...] = summed
        z = (standardize(summed)[0] * gain).astype(BF16)
        zb[...] = z
        zt_natural[...] = z.T
        rows_in_order(meta, zt_natural, zt)

    width = active.shape[1]
    root = 0.7978845608028654
    for part in range(3):
        mine = slice(part * width // 3, (part + 1) * width // 3)
        v = dot(zb[...], up[:, mine])
        slope_in = dot_t(upstream[...], down[mine, :])
        square = v * v
        t = jnp.tanh(root * v * (1.0 + 0.044715 * square))
        cdf = 0.5 * (1.0 + t)
        active[:, mine] = (v * cdf).astype(BF16)
        slope = cdf + v * (0.5 * root) * (1.0 - t * t) * (1.0 + 0.134145 * square)
        dpre[:, mine] = (slope_in * slope).astype(BF16)
    added(step, g_total, None, dot_t(dpre[...], up[...]))

    @pl.when(step < 2)
    def _():
        turned[...] = active[...].T
        first[:, :width] = dot(zt_natural[...], dpre[...]).astype(BF16)
        first[:, width:] = dot(turned[...], upstream[...]).astype(BF16)

    @pl.when(step == pl.num_programs(0) - 1)
    def _():
        z, rstd = standardize(resid[...])
        grad = upstream[...].astype(F32) + norm_back(z, rstd, g_total[...] * gain)
        low = grad.astype(BF16)
        for side, target in ((1 - meta[0], away), (meta[0], mine_out)):
            target[...] = dot_t(low, weight[half_at(side, 3 * PAIR), :]).astype(BF16)
        dresid[...] = grad
        db[...] = low


def hidden_back(
    meta, zt, active, dpre, upstream, mt, db,
    up_keep, up_send, down_keep, down_send, mixed_keep, mixed_send, turned, picked,
):
    step = pl.program_id(0)
    width = active.shape[1]
    turned[...] = active[...].T
    rows_in_order(meta, turned, picked)
    size = width // 2
    for spot, (up_part, down_part) in enumerate(((up_keep, down_keep), (up_send, down_send))):
        mine = slice(spot * size, (spot + 1) * size)
        up_part[...] = dot(zt[mine, :], dpre[...]).astype(BF16)
        down_part[...] = dot(picked[mine, :], upstream[...]).astype(BF16)

    @pl.when(step == pl.num_programs(0) - 1)
    def _():
        mixed_send[...] = dot(mt[size:, :], db[...]).astype(BF16)
        mixed_keep[...] = dot(mt[:size, :], db[...]).astype(BF16)


def forward_out(meta, before, active, down, out, total):
    step = pl.program_id(0)
    added(step, total, before, dot(active[...], down[...]))

    @pl.when(step == pl.num_programs(0) - 1)
    def _():
        out[...] = total[...].astype(out.dtype)


def input_back(meta, own, mine, other, dresid, gains, out):
    z, rstd = standardize(own[...].astype(F32))
    g = (mine[...] + other[...].astype(F32)) * gains[0:1, :].astype(F32)
    out[...] = dresid[...] + norm_back(z, rstd, g)


def row_sums(values):
    ones = jnp.ones((8, values.shape[1]), F32)
    sums = lax.dot_general(
        ones, values, (((1,), (1,)), ((), ())), preferred_element_type=F32, precision=lax.Precision.HIGHEST
    )
    return sums[0:1, :]


def joint_out(meta, own, other, weight, gain, grad, gain_grad):
    for side, source in ((meta[0], own), (1 - meta[0], other)):
        for pair in range(3):
            for kind in range(3):
                columns = pl.ds(pl.multiple_of((kind * 6 + side * 3 + pair) * PAIR, PAIR), PAIR)
                at = (pair * 3 + kind) * PAIR
                grad[:, columns] = source[:, at : at + PAIR].astype(F32)
    gain_grad[...] = row_sums(grad[...] * weight[...].astype(F32)) / gain[...].astype(F32)


def feed_out(split, meta, first, first_too, last, last_too, weight, gain, up, down, output, gain_grad):
    rows, dim = output.shape
    if split:
        width = dim // 2
        for side, source in ((meta[0], last), (1 - meta[0], last_too)):
            output[:, half_at(side, width)] = source[:, 2 * dim :].astype(F32)
    else:
        output[...] = last[:, -dim:].astype(F32) + last_too[:, -dim:].astype(F32)
    for k in range(4):
        parts = []
        for kind in range(2):
            if k < 2 or not split:
                one, two = (first, first_too) if k < 2 else (last, last_too)
                at = ((2 * k + kind) if k < 2 else (2 * kind + k - 2)) * dim
                parts.append(one[:, at : at + dim].astype(F32) + two[:, at : at + dim].astype(F32))
            else:
                at = kind * dim
                parts.append(jnp.where(meta[0] == k - 2, last[:, at : at + dim], last_too[:, at : at + dim]).astype(F32))
        for owner in range(dim // rows):
            up[:, (4 * owner + k) * rows : (4 * owner + k + 1) * rows] = parts[0][:, owner * rows : (owner + 1) * rows]
        down[k * rows : (k + 1) * rows, :] = parts[1]
    gain_grad[...] = row_sums(up[...] * weight[...].astype(F32)) / gain[...].astype(F32)


SWAP = [(0, 1), (1, 0)]


def flipped(array, parts, bit):
    return lax.ppermute(array, "fsdp", [(spot, spot ^ bit) for spot in range(parts)])


def exchanged(blocks, parts):
    groups = [list(range(side, parts, 4)) for side in range(4)]
    return lax.all_to_all(blocks, "fsdp", 0, 0, axis_index_groups=groups, tiled=True)


def rounded_sum(terms):
    total = terms[0].astype(F32)
    for term in terms[1:]:
        total = total + term.astype(F32)
    return total.astype(BF16)


def pinned(array, mark):
    return lax.optimization_barrier((array, mark))[0]


class Reduction:
    def __init__(self, terms, parts, place):
        self.terms, self.parts, self.place = terms, parts, place

    def go(self, step):
        if step == "seq":
            width = self.terms[0].shape[3] // 2
            away = rounded_sum(
                [lax.dynamic_slice_in_dim(term, (1 - self.place) * width, width, 3) for term in self.terms]
            )
            self.terms = [lax.dynamic_slice_in_dim(term, self.place * width, width, 3) for term in self.terms]
            self.came = lax.ppermute(away, "seq", SWAP)
        else:
            away = rounded_sum([term[:, 1:] for term in self.terms])
            self.terms = [term[:, :1] for term in self.terms]
            self.came = flipped(away, self.parts, 2)
        return away

    def take(self, mark):
        self.terms.append(pinned(self.came, mark))


def body(block_input, lead_gain, joint_weight, output_weight, tail_gain, up_weight, down_weight, cotangent):
    rows, triple = joint_weight.shape
    dim = block_input.shape[2]
    wide = up_weight.shape[1]
    half = block_input.shape[1]
    length = 2 * half
    parts = dim // rows
    group = triple // 6
    chunk = dim // 2
    place = lax.axis_index("seq")
    me = lax.axis_index("fsdp")
    direct = parts == 16
    base = me if direct else jnp.zeros_like(me)
    spots = jnp.arange(16, dtype=jnp.int32)
    few = jnp.arange(8, dtype=jnp.int32)
    eight = (few % 2) * 8 + (few // 2 % 2) * 4 + few // 4 * 2
    meta = jnp.concatenate(
        [
            place[None],
            spots % 8 // 2 * 4 + ((base % 4) ^ (spots % 2 * 2 + spots // 8)),
            base ^ jnp.concatenate([eight, eight ^ 1]) if direct else spots,
        ]
    ).astype(jnp.int32)

    joint_own = lax.dynamic_index_in_dim(joint_weight.reshape(rows, 3, 2, group), place, 2, keepdims=False)
    joint_own = joint_own.reshape(rows, 3, 3, PAIR).transpose(0, 2, 1, 3).reshape(rows, 3 * group)
    up_turned = up_weight.reshape(rows, parts, 4, rows).transpose(2, 0, 1, 3).reshape(4, rows, dim)
    down_turned = down_weight.reshape(4, rows, dim)
    hidden = [part[k] for k in range(4) for part in (up_turned, down_turned)]

    own = block_input[0]
    upstream = cotangent[0]
    rest = lax.all_gather(jnp.concatenate([output_weight, *hidden], axis=1), "fsdp", axis=0, tiled=True)
    other = lax.ppermute(own, "seq", SWAP)
    both_gains = jnp.pad(jnp.stack([lead_gain, tail_gain], axis=1), ((0, 0), (0, PAIR - 2)))
    first = jnp.concatenate([joint_own, both_gains], axis=1)
    if direct:
        for bit in (8, 4, 2):
            if bit == 2:
                first, other = lax.optimization_barrier((first, other))
            first = jnp.concatenate([first, flipped(first, parts, bit)], axis=0)
        firsts = (first, flipped(first, parts, 1))
    else:
        first = lax.all_gather(first, "fsdp", axis=0, tiled=True)
        firsts = (first[:chunk], first[chunk:])

    (z_one,) = call(first_norm, "first_norm", (shaped(length, dim, dtype=F32),), meta, (own, other), took=3)
    zb, gains = call(
        first_scale,
        "first_scale",
        (shaped(length, dim), shaped(16, dim)),
        meta,
        (z_one, *firsts),
        [pltpu.VMEM((dim, PAIR), BF16)],
        took=2,
        grid=(1,),
        specs=[VMEM] + [column(chunk, PAIR, lambda step: 9)] * 2,
    )
    triples = column(length, 3 * PAIR)
    pair_tokens = column(half, PAIR)
    lse_spec = pl.BlockSpec((1, 8, length), lambda step: (step, 0, 0))
    qkv, o_own, o_other, lse, weight = call(
        attend,
        "attend",
        (
            shaped(length, 9 * PAIR),
            shaped(half, group),
            shaped(half, group),
            shaped(3, 8, length, dtype=F32),
            shaped(dim, 9 * PAIR),
        ),
        meta,
        (zb, *firsts),
        [
            pltpu.VMEM((2, length, PAIR), BF16),
            pltpu.VMEM((PAIR, length), BF16),
            pltpu.VMEM((2, length, BAND), F32),
            pltpu.VMEM((PAIR, BAND), F32),
            pltpu.VMEM((length, PAIR), BF16),
        ],
        took=22,
        grid=(3,),
        specs=[whole(length, dim)] + [column(chunk, 3 * PAIR)] * 2,
        out_specs=[triples, pair_tokens, pair_tokens, lse_spec, column(dim, 3 * PAIR)],
    )
    o_came = lax.ppermute(o_other, "seq", SWAP)
    store = [pltpu.VMEM((dim, length), BF16)]
    (zt,) = call(turn, "turn", (shaped(dim, length),), meta, (zb,), store, took=2, after=[lse])
    mixed, mixed_t = call(
        mix,
        "mix",
        (shaped(half, dim), shaped(dim, half)),
        meta,
        (o_own, o_came),
        [pltpu.VMEM((dim, half), BF16)],
        took=2,
        after=[zt],
    )
    rest_block = column(dim, dim, lambda step: 0)
    total_f32 = shaped(half, dim, dtype=F32)
    tokens = whole(half, dim)

    turned = whole(dim, half)
    active, dpre, grad_first, zt_two, resid, dresid, db, dm_away, dm_mine = call(
        feed,
        "feed",
        (shaped(half, wide),) * 2
        + (shaped(dim, 4 * dim), shaped(dim, half))
        + (total_f32, total_f32, shaped(half, dim), shaped(half, group), shaped(half, group)),
        meta,
        (own, mixed, gains, rest, rest, rest, upstream),
        [
            pltpu.VMEM((half, dim), BF16),
            pltpu.VMEM((dim, half), BF16),
            pltpu.VMEM((half, dim), F32),
            pltpu.VMEM((dim, half), BF16),
        ],
        took=20,
        grid=(4,),
        specs=[
            tokens,
            tokens,
            whole(16, dim),
            rest_block,
            column(dim, dim, lambda k: 1 + 2 * k),
            column(dim, dim, lambda k: 2 + 2 * k),
            tokens,
        ],
        out_specs=[column(half, dim)] * 2
        + [column(dim, 2 * dim, lambda k: jnp.minimum(k, 1)), turned]
        + [tokens] * 3 + [whole(half, group)] * 2,
    )
    dm_came = lax.ppermute(dm_away, "seq", SWAP)
    up_keep, up_send, down_keep, down_send, mixed_keep, mixed_send = call(
        hidden_back,
        "hidden_back",
        (shaped(chunk, 2 * dim),) * 4 + (shaped(chunk, dim),) * 2,
        meta,
        (zt_two, active, dpre, upstream, mixed_t, db),
        [pltpu.VMEM((dim, half), BF16), pltpu.VMEM((dim, half), BF16)],
        took=7,
        grid=(2,),
        specs=[turned] + [column(half, dim, lambda k: k + 2)] * 2 + [tokens, turned, tokens],
        out_specs=[column(chunk, dim)] * 4 + [whole(chunk, dim)] * 2,
    )
    dm_came = pinned(dm_came, up_keep)

    def blocks_of(part):
        return part.reshape(4, 2, rows, -1)

    marks = [[], [], []]
    if direct:
        first_sum = lax.psum_scatter(grad_first, "fsdp", scatter_dimension=0, tiled=True)
        up_came, down_came, mixed_came = (
            flipped(pinned(part, dm_came), parts, 1) for part in (up_send, down_send, mixed_send)
        )
    def attend_back_call(pair, outs, out_specs, extra, after):
        width = (9 if pair == 2 else 3) * PAIR
        pick = lambda step: pair
        return call(
            functools.partial(attend_back, pair),
            "attend_back",
            (shaped(chunk, width), shaped(chunk, width)) + outs,
            meta,
            (qkv, o_own, o_other, dm_mine, dm_came, lse, zt, weight, *extra),
            [
                pltpu.VMEM((2, length, PAIR), BF16),
                pltpu.VMEM((2, length, PAIR), BF16),
                pltpu.VMEM((PAIR, length), BF16),
                pltpu.VMEM((length, PAIR), BF16),
                pltpu.VMEM((8, length), F32),
                pltpu.VMEM((length, PAIR), F32),
                pltpu.VMEM((length, PAIR), F32),
                pltpu.VMEM((PAIR, BAND), F32),
                pltpu.VMEM((length, 3 * PAIR), BF16),
                pltpu.VMEM((2, length, BAND), F32),
                pltpu.VMEM((2, length, BAND), F32),
                pltpu.VMEM((2, length, BAND), BF16),
                pltpu.VMEM((2, length, BAND), BF16),
            ],
            took=10,
            after=after,
            grid=(1,),
            specs=[column(length, 3 * PAIR, pick)]
            + [column(half, PAIR, pick)] * 4
            + [
                pl.BlockSpec((1, 8, length), lambda step: (pair, 0, 0)),
                whole(dim, length),
                column(dim, 3 * PAIR, pick),
            ]
            + [whole(*part.shape) for part in extra],
            out_specs=[whole(chunk, width)] * 2 + out_specs,
        )

    one = (shaped(length, 3 * PAIR),)
    keep_0, send_0, token_0 = attend_back_call(0, one, [whole(length, 3 * PAIR)], (), marks[0])
    if direct:
        pairs = ((up_keep, up_came), (down_keep, down_came), (mixed_keep, mixed_came))
        up_red, down_red, mixed_red = (
            Reduction([blocks_of(part) for part in (keep, pinned(came, token_0))], parts, place) for keep, came in pairs
        )
        marks[1] += [up_red.go(2), down_red.go("seq"), mixed_red.go("seq")]
    keep_1, send_1, token_1 = attend_back_call(1, one, [whole(length, 3 * PAIR)], (), marks[1] + [token_0])
    marks[2].append(token_1)
    joint_keep, joint_send, token_2 = attend_back_call(
        2, one, [whole(length, 3 * PAIR)], (keep_0, send_0, keep_1, send_1), marks[2]
    )
    if direct:
        reds = (up_red, down_red, mixed_red)
        joint_send, *cames = lax.optimization_barrier((joint_send, *(red.came for red in reds)))
        for red, came in zip(reds, cames):
            red.terms.append(came)
    marks = []
    marks = []
    if direct:
        joint_came = flipped(joint_send, parts, 1)
        joint_red = Reduction([blocks_of(part) for part in (joint_keep, joint_came)], parts, place)
        marks = [up_red.go("seq"), down_red.go(2), mixed_red.go(2)]
        joint_red.terms = list(pinned(joint_red.terms, marks))
        marks.append(joint_red.go(2))
    sent, own_part = call(
        token_back,
        "token_back",
        (shaped(half, dim), total_f32),
        meta,
        (token_0, token_1, token_2, weight),
        took=5,
        after=marks,
    )
    other_part = lax.ppermute(sent, "seq", SWAP)

    def forward_call(late, before, after):
        at = 2 * late
        return call(
            forward_out,
            "forward_out",
            (shaped(half, dim) if late else total_f32,),
            meta,
            (before, active, rest),
            [pltpu.VMEM((half, dim), F32)],
            took=3,
            after=after,
            grid=(2,),
            specs=[tokens, column(half, dim, lambda k: at + k), column(dim, dim, lambda k: 2 + 2 * (at + k))],
            out_specs=[tokens],
        )

    marks = [own_part]
    if direct:
        marks = [own_part]
        last_sum = []
        for red in (up_red, down_red, mixed_red):
            red.take(own_part)
            last_sum.append(rounded_sum(red.terms))
        last_sum = jnp.concatenate(last_sum, axis=-1).reshape(4, rows, -1)
        deep = me // 4
        last_parts = [lax.dynamic_index_in_dim(last_sum, deep, 0, keepdims=False)]
        for far in (1, 2, 3):
            away = lax.dynamic_index_in_dim(last_sum, deep ^ far, 0, keepdims=False)
            last_parts.append(flipped(away, parts, 4 * far))
            marks.append(away)
        joint_red.take(marks)
        joint_sum = rounded_sum(joint_red.terms).reshape(4, rows, -1)
        marks.append(joint_sum)
    (out,) = forward_call(0, resid, marks)
    marks = []
    if direct:
        joint_sum = exchanged(joint_sum, parts)
    (out,) = forward_call(1, out, marks)
    marks = [out]
    (input_grad,) = call(
        input_back, "input_back", (total_f32,), meta, (own, own_part, other_part, dresid, gains), after=marks
    )

    if direct:
        last_sum = rounded_sum(last_parts)
        joint_sum = jnp.sum(pinned(joint_sum, out).astype(F32), axis=0).astype(BF16)
    else:

        def scattered(keep, send):
            blocks = jnp.stack([keep, send]).reshape(2, 4, 2, dim // 16, -1).transpose(1, 2, 0, 3, 4).reshape(dim, -1)
            return lax.psum_scatter(blocks, "fsdp", scatter_dimension=0, tiled=True)

        first_sum = lax.psum_scatter(grad_first, "fsdp", scatter_dimension=0, tiled=True)
        last_sum = ((up_keep, up_send), (down_keep, down_send), (mixed_keep, mixed_send))
        last_sum = jnp.concatenate([scattered(*pair) for pair in last_sum], axis=1)
        joint_sum = scattered(joint_keep, joint_send)
    first_sum = pinned(first_sum, input_grad)
    first_sum, last_sum, joint_sum = ((part, lax.ppermute(part, "seq", SWAP)) for part in (first_sum, last_sum, joint_sum))
    up_grad, down_grad, output_grad, tail_grad = call(
        functools.partial(feed_out, direct),
        "feed_out",
        (
            shaped(rows, wide, dtype=F32),
            shaped(4 * rows, dim, dtype=F32),
            shaped(rows, dim, dtype=F32),
            shaped(1, rows, dtype=F32),
        ),
        meta,
        (*first_sum, *last_sum, up_weight, tail_gain[None, :]),
        after=[input_grad],
    )
    joint_grad, lead_grad = call(
        joint_out,
        "joint_out",
        (shaped(rows, triple, dtype=F32), shaped(1, rows, dtype=F32)),
        meta,
        (*joint_sum, joint_weight, lead_gain[None, :]),
        took=2,
        after=[up_grad],
    )
    return (
        out[None],
        input_grad[None],
        lead_grad[0],
        joint_grad,
        output_grad,
        tail_grad[0],
        up_grad,
        down_grad,
    )


def solution(mesh):
    split = P("fsdp", "seq", None)
    placed = (split, P("fsdp"), P("fsdp", None), P("fsdp", None), P("fsdp"), P("fsdp", None), P("fsdp", None), split)
    return jax.shard_map(
        body,
        mesh=mesh,
        in_specs=placed,
        out_specs=(split, split, P("fsdp"), P("fsdp", None), P("fsdp", None), P("fsdp"), P("fsdp", None), P("fsdp", None)),
        check_vma=False,
    )
```

```python
import functools

import jax
import jax.numpy as jnp
from jax import lax
from jax.experimental import pallas as pl
from jax.experimental.pallas import tpu as pltpu
from jax.sharding import PartitionSpec as P

HD = 64
EPS = 1e-05
PAIR = 2 * HD
BAND = 256
LOG2E = 1.4426950408889634
LIMIT = 56 << 20
F32 = jnp.float32
BF16 = jnp.bfloat16

VMEM = pl.BlockSpec(memory_space=pltpu.VMEM)
SMEM = pl.BlockSpec(memory_space=pltpu.SMEM)
ANY = pl.BlockSpec(memory_space=pl.ANY)


def dot(left, right):
    return jnp.dot(left, right, preferred_element_type=F32)


def dot_t(left, right):
    return lax.dot_general(left, right, (((1,), (1,)), ((), ())), preferred_element_type=F32)


def shaped(*dims, dtype=BF16):
    return jax.ShapeDtypeStruct(dims, dtype)


def cost(microseconds):
    return pl.CostEstimate(flops=int(microseconds * 1e7), transcendentals=0, bytes_accessed=int(microseconds * 3e4))


def waiting(kernel, fixed, after):
    def run(*refs):
        kernel(*refs[:fixed], *refs[fixed + after :])

    return run


def whole(*dims):
    return pl.BlockSpec(dims, lambda *_: (0,) * len(dims))


def column(rows, columns, pick=lambda step: step):
    return pl.BlockSpec((rows, columns), lambda *steps: (0, pick(*steps)))


def call(kernel, name, outs, meta, inputs, scratch=(), took=4, after=(), grid=(), specs=None, out_specs=None):
    return pl.pallas_call(
        waiting(kernel, 1 + len(inputs), len(after)),
        name=name,
        grid=grid,
        out_shape=outs,
        in_specs=[SMEM] + list(specs or [VMEM] * len(inputs)) + [ANY] * len(after),
        out_specs=list(out_specs or [VMEM] * len(outs)),
        scratch_shapes=list(scratch),
        compiler_params=pltpu.CompilerParams(vmem_limit_bytes=LIMIT),
        cost_estimate=cost(took),
    )(meta, *inputs, *after)


def standardize(values):
    center = values - jnp.mean(values, axis=-1, keepdims=True)
    spread = jnp.mean(center * center, axis=-1, keepdims=True)
    rstd = lax.rsqrt(spread + EPS)
    return center * rstd, rstd


def norm_back(z, rstd, g):
    return (g - jnp.mean(g, axis=-1, keepdims=True) - z * jnp.mean(g * z, axis=-1, keepdims=True)) * rstd


def half_at(index, size):
    return pl.ds(pl.multiple_of(index * size, size), size)


def rows_in_order(meta, source, target):
    size = source.shape[0] // 16
    for spot in range(16):
        rows = pl.ds(pl.multiple_of(meta[1 + spot] * size, size), size)
        target[spot * size : (spot + 1) * size, :] = source[rows, :]


def placed(meta, near, far, target):
    size = target.shape[0] // 16
    for spot in range(16):
        source = (near, far)[spot // 8]
        rows = pl.ds(pl.multiple_of(meta[17 + spot] * size, size), size)
        target[rows, :] = source[spot % 8 * size : (spot % 8 + 1) * size, :]


def pack(output, up, down, packed):
    rows, dim = output.shape
    packed[:, :dim] = output[...]
    for k in range(4):
        at = (1 + 2 * k) * dim
        for owner in range(dim // rows):
            source = (4 * owner + k) * rows
            packed[:, at + owner * rows : at + (owner + 1) * rows] = up[:, source : source + rows]
        packed[:, at + dim : at + 2 * dim] = down[k * rows : (k + 1) * rows, :]


def first_norm(meta, own, other, z):
    half = own.shape[0]
    for source, place in ((own, meta[0]), (other, 1 - meta[0])):
        z[half_at(place, half), :] = standardize(source[...].astype(F32))[0]


def first_scale(meta, z, near, far, zb, gains, columns):
    placed(meta, near, far, columns)
    gains[...] = columns[...].T[:16, :]
    zb[...] = (z[...] * gains[0:1, :].astype(F32)).astype(BF16)


def turn(meta, zb, zt, turned):
    turned[...] = zb[...].T
    rows_in_order(meta, turned, zt)


def mix(meta, mine, other, mixed, mt, turned):
    width = mine.shape[1]
    for side, source in ((meta[0], mine), (1 - meta[0], other)):
        mixed[:, half_at(side, width)] = source[...]
    turned[...] = mixed[...].T
    rows_in_order(meta, turned, mt)


def attend(meta, zb, near, far, qkv, o_own, o_other, lse, weight, km, vt, s_sc, ot, o_all):
    length = zb.shape[0]
    half = length // 2
    placed(meta, near, far, weight)
    qkv[...] = dot(zb[...], weight[...]).astype(BF16)
    lane = lax.broadcasted_iota(jnp.int32, (1, PAIR), 1)
    keys = qkv[:, PAIR : 2 * PAIR]
    zero = jnp.zeros_like(keys)
    km[0] = jnp.where(lane < HD, keys, zero)
    km[1] = jnp.where(lane < HD, zero, keys)
    vt[...] = qkv[:, 2 * PAIR :].T
    lse[0] = jnp.zeros(lse.shape[1:], F32)
    allowed = lax.broadcasted_iota(jnp.int32, (BAND, BAND), 0) <= lax.broadcasted_iota(jnp.int32, (BAND, BAND), 1)

    def q_step(q_band, _):
        spots = half_at(q_band, BAND)
        queries = qkv[spots, :PAIR]

        def score(k_band, tops, diagonal):
            rows = half_at(k_band, BAND)
            peaks = []
            for head in range(2):
                s = dot_t(km[head, rows, :], queries) * (HD ** -0.5 * LOG2E)
                if diagonal:
                    s = jnp.where(allowed, s, 0.0)
                s_sc[head, rows, :] = s
                peaks.append(jnp.maximum(tops[head], jnp.max(jnp.abs(s), axis=0, keepdims=True)))
            return tuple(peaks)

        def weigh(k_band, carry, tops, diagonal):
            rows = half_at(k_band, BAND)
            results = []
            for head, (total, out) in enumerate(carry):
                s = s_sc[head, rows, :]
                grow = jnp.exp2(s - tops[head])
                shrink = jnp.exp2(-s - tops[head])
                both = grow + shrink
                if diagonal:
                    both = jnp.where(allowed, both, 0.0)
                part = dot(vt[head * HD : (head + 1) * HD, rows], (grow - shrink).astype(BF16))
                results.append((total + jnp.sum(both, axis=0, keepdims=True), out + part))
            return tuple(results)

        none = jnp.zeros((1, BAND), F32)
        tops = score(q_band, (none, none), True)
        tops = lax.fori_loop(0, q_band, lambda k_band, tops: score(k_band, tops, False), tops)
        start = (none, jnp.zeros((HD, BAND), F32))
        carry = weigh(q_band, (start, start), tops, True)
        carry = lax.fori_loop(0, q_band, lambda k_band, carry: weigh(k_band, carry, tops, False), carry)
        for head, (total, out) in enumerate(carry):
            ot[head * HD : (head + 1) * HD, :] = out / total
            lse[0, head : head + 1, spots] = tops[head] + jnp.log2(0.5 * total)
        o_all[spots, :] = ot[...].T.astype(BF16)
        return 0

    lax.fori_loop(0, length // BAND, q_step, 0)
    o_own[...] = o_all[half_at(meta[0], half), :]
    o_other[...] = o_all[half_at(1 - meta[0], half), :]


def attend_back(pair, meta, qkv, o_own, o_other, d_own, d_other, lse, zt, weight, *refs):
    last = pair == 2
    count = (0, 0, 4)[pair]
    extra, refs = refs[:count], refs[count:]
    keep, send, *outs = refs[:3]
    km, vm, kt, do, inner, dk, dv, dqt, dqkv, s_sc, w_sc, p_sc, ds_sc = refs[3:]
    length = qkv.shape[0]
    half = length // 2
    lane = lax.broadcasted_iota(jnp.int32, (1, PAIR), 1)
    low = lane < HD
    keys = qkv[:, PAIR : 2 * PAIR]
    values = qkv[:, 2 * PAIR :]
    zero = jnp.zeros_like(keys)
    km[0] = jnp.where(low, keys, zero)
    km[1] = jnp.where(low, zero, keys)
    vm[0] = jnp.where(low, values, zero)
    vm[1] = jnp.where(low, zero, values)
    kt[...] = keys.T
    pick = (
        lax.broadcasted_iota(jnp.int32, (8, PAIR), 1) // HD == lax.broadcasted_iota(jnp.int32, (8, PAIR), 0)
    ).astype(F32)
    for o_part, d_part, place in ((o_own, d_own, meta[0]), (o_other, d_other, 1 - meta[0])):
        do[half_at(place, half), :] = d_part[...]
        product = o_part[...].astype(F32) * d_part[...].astype(F32)
        inner[:, half_at(place, half)] = lax.dot_general(
            pick, product, (((1,), (1,)), ((), ())), preferred_element_type=F32, precision=lax.Precision.HIGHEST
        )
    allowed = lax.broadcasted_iota(jnp.int32, (BAND, BAND), 0) <= lax.broadcasted_iota(jnp.int32, (BAND, BAND), 1)
    for q_band in range(length // BAND):
        spots = slice(q_band * BAND, (q_band + 1) * BAND)
        end = (q_band + 1) * BAND
        queries = qkv[spots, :PAIR]
        upstream = do[spots, :]
        small = jnp.zeros_like(queries)
        for head in range(2):
            mine = slice(head * HD, (head + 1) * HD)
            q_mine = jnp.where(low, queries, small) if head == 0 else jnp.where(low, small, queries)
            d_mine = jnp.where(low, upstream, small) if head == 0 else jnp.where(low, small, upstream)
            base = lse[0, head : head + 1, spots] + 1.0
            mean = inner[head : head + 1, spots]
            s_sc[head, :end, :] = dot_t(km[head, :end, :], queries)
            w_sc[head, :end, :] = dot_t(vm[head, :end, :], upstream)
            for k_band in range(q_band + 1):
                rows = slice(k_band * BAND, (k_band + 1) * BAND)
                s = s_sc[head, rows, :] * (HD ** -0.5 * LOG2E)
                dw = w_sc[head, rows, :]
                if k_band == q_band:
                    s = jnp.where(allowed, s, 0.0)
                    dw = jnp.where(allowed, dw, 0.0)
                grow = jnp.exp2(s - base)
                shrink = jnp.exp2(-s - base)
                p = grow - shrink
                p_sc[head, rows, :] = p.astype(BF16)
                ds_sc[head, rows, :] = ((grow + shrink) * dw - p * mean).astype(BF16)
            dv_part = dot(p_sc[head, :end, :], d_mine)
            dk_part = dot(ds_sc[head, :end, :], q_mine)
            dqt[mine, :] = dot(kt[mine, :end], ds_sc[head, :end, :])
            old = q_band * BAND if head == 0 else end
            if old:
                dv[:old, :] += dv_part[:old]
                dk[:old, :] += dk_part[:old]
            if head == 0:
                dv[old:end, :] = dv_part[old:]
                dk[old:end, :] = dk_part[old:]
        dqkv[spots, :PAIR] = (dqt[...].T * HD ** -0.5).astype(BF16)
    dqkv[:, PAIR : 2 * PAIR] = (dk[...] * HD ** -0.5).astype(BF16)
    dqkv[:, 2 * PAIR :] = dv[...].astype(BF16)
    middle = keep.shape[0]
    start = keep.shape[1] - 3 * PAIR
    send[:, start:] = dot(zt[middle:, :], dqkv[...]).astype(BF16)
    keep[:, start:] = dot(zt[:middle, :], dqkv[...]).astype(BF16)
    if last:
        for spot in range(2):
            columns = slice(spot * 3 * PAIR, (spot + 1) * 3 * PAIR)
            keep[:, columns] = extra[2 * spot][...]
            send[:, columns] = extra[2 * spot + 1][...]
    outs[0][...] = dqkv[...]


def token_back(meta, t0, t1, t2, weight, away, mine_out):
    half = away.shape[0]
    for side, target in ((1 - meta[0], away), (meta[0], mine_out)):
        part = None
        for spot, token in enumerate((t0, t1, t2)):
            columns = slice(spot * 3 * PAIR, (spot + 1) * 3 * PAIR)
            new = dot_t(token[half_at(side, half), :], weight[:, columns])
            part = new if part is None else part + new
        target[...] = part.astype(target.dtype)


def added(step, total, first, part):
    @pl.when(step == 0)
    def _():
        total[...] = part if first is None else first[...] + part

    @pl.when(step > 0)
    def _():
        total[...] += part


def feed(
    meta, own, mixed, gains, weight, up, down, upstream,
    active, dpre, first, zt, resid, dresid, db, away, mine_out, zb, zt_natural, g_total, turned,
):
    step = pl.program_id(0)
    gain = gains[1:2, :].astype(F32)

    @pl.when(step == 0)
    def _():
        summed = own[...].astype(F32) + dot(mixed[...], weight[...])
        resid[...] = summed
        z = (standardize(summed)[0] * gain).astype(BF16)
        zb[...] = z
        zt_natural[...] = z.T
        rows_in_order(meta, zt_natural, zt)

    width = active.shape[1]
    root = 0.7978845608028654
    for part in range(3):
        mine = slice(part * width // 3, (part + 1) * width // 3)
        v = dot(zb[...], up[:, mine])
        slope_in = dot_t(upstream[...], down[mine, :])
        square = v * v
        t = jnp.tanh(root * v * (1.0 + 0.044715 * square))
        cdf = 0.5 * (1.0 + t)
        active[:, mine] = (v * cdf).astype(BF16)
        slope = cdf + v * (0.5 * root) * (1.0 - t * t) * (1.0 + 0.134145 * square)
        dpre[:, mine] = (slope_in * slope).astype(BF16)
    added(step, g_total, None, dot_t(dpre[...], up[...]))

    @pl.when(step < 2)
    def _():
        turned[...] = active[...].T
        first[:, :width] = dot(zt_natural[...], dpre[...]).astype(BF16)
        first[:, width:] = dot(turned[...], upstream[...]).astype(BF16)

    @pl.when(step == pl.num_programs(0) - 1)
    def _():
        z, rstd = standardize(resid[...])
        grad = upstream[...].astype(F32) + norm_back(z, rstd, g_total[...] * gain)
        low = grad.astype(BF16)
        for side, target in ((1 - meta[0], away), (meta[0], mine_out)):
            target[...] = dot_t(low, weight[half_at(side, 3 * PAIR), :]).astype(BF16)
        dresid[...] = grad
        db[...] = low


def hidden_back(
    meta, zt, active, dpre, upstream, mt, db,
    up_keep, up_send, down_keep, down_send, mixed_keep, mixed_send, turned, picked,
):
    step = pl.program_id(0)
    width = active.shape[1]
    turned[...] = active[...].T
    rows_in_order(meta, turned, picked)
    size = width // 2
    for spot, (up_part, down_part) in enumerate(((up_keep, down_keep), (up_send, down_send))):
        mine = slice(spot * size, (spot + 1) * size)
        up_part[...] = dot(zt[mine, :], dpre[...]).astype(BF16)
        down_part[...] = dot(picked[mine, :], upstream[...]).astype(BF16)

    @pl.when(step == pl.num_programs(0) - 1)
    def _():
        mixed_send[...] = dot(mt[size:, :], db[...]).astype(BF16)
        mixed_keep[...] = dot(mt[:size, :], db[...]).astype(BF16)


def forward_out(meta, before, active, down, out, total):
    step = pl.program_id(0)
    added(step, total, before, dot(active[...], down[...]))

    @pl.when(step == pl.num_programs(0) - 1)
    def _():
        out[...] = total[...].astype(out.dtype)


def input_back(meta, own, mine, other, dresid, gains, out):
    z, rstd = standardize(own[...].astype(F32))
    g = (mine[...] + other[...].astype(F32)) * gains[0:1, :].astype(F32)
    out[...] = dresid[...] + norm_back(z, rstd, g)


def row_sums(values):
    ones = jnp.ones((8, values.shape[1]), F32)
    sums = lax.dot_general(
        ones, values, (((1,), (1,)), ((), ())), preferred_element_type=F32, precision=lax.Precision.HIGHEST
    )
    return sums[0:1, :]


def joint_out(meta, own, other, weight, gain, grad, gain_grad):
    for side, source in ((meta[0], own), (1 - meta[0], other)):
        for pair in range(3):
            for kind in range(3):
                columns = pl.ds(pl.multiple_of((kind * 6 + side * 3 + pair) * PAIR, PAIR), PAIR)
                at = (pair * 3 + kind) * PAIR
                grad[:, columns] = source[:, at : at + PAIR].astype(F32)
    gain_grad[...] = row_sums(grad[...] * weight[...].astype(F32)) / gain[...].astype(F32)


def feed_out(split, meta, first, first_too, last, last_too, weight, gain, up, down, output, gain_grad):
    rows, dim = output.shape
    if split:
        width = dim // 2
        for side, source in ((meta[0], last), (1 - meta[0], last_too)):
            output[:, half_at(side, width)] = source[:, 2 * dim :].astype(F32)
    else:
        output[...] = last[:, -dim:].astype(F32) + last_too[:, -dim:].astype(F32)
    for k in range(4):
        parts = []
        for kind in range(2):
            if k < 2 or not split:
                one, two = (first, first_too) if k < 2 else (last, last_too)
                at = ((2 * k + kind) if k < 2 else (2 * kind + k - 2)) * dim
                parts.append(one[:, at : at + dim].astype(F32) + two[:, at : at + dim].astype(F32))
            else:
                at = kind * dim
                parts.append(jnp.where(meta[0] == k - 2, last[:, at : at + dim], last_too[:, at : at + dim]).astype(F32))
        for owner in range(dim // rows):
            up[:, (4 * owner + k) * rows : (4 * owner + k + 1) * rows] = parts[0][:, owner * rows : (owner + 1) * rows]
        down[k * rows : (k + 1) * rows, :] = parts[1]
    gain_grad[...] = row_sums(up[...] * weight[...].astype(F32)) / gain[...].astype(F32)


SWAP = [(0, 1), (1, 0)]


def flipped(array, parts, bit):
    return lax.ppermute(array, "fsdp", [(spot, spot ^ bit) for spot in range(parts)])


def exchanged(blocks, parts):
    groups = [list(range(side, parts, 4)) for side in range(4)]
    return lax.all_to_all(blocks, "fsdp", 0, 0, axis_index_groups=groups, tiled=True)


def rounded_sum(terms):
    total = terms[0].astype(F32)
    for term in terms[1:]:
        total = total + term.astype(F32)
    return total.astype(BF16)


def pinned(array, mark):
    return lax.optimization_barrier((array, mark))[0]


class Reduction:
    def __init__(self, terms, parts, place):
        self.terms, self.parts, self.place = terms, parts, place

    def go(self, step):
        if step == "seq":
            width = self.terms[0].shape[3] // 2
            away = rounded_sum(
                [lax.dynamic_slice_in_dim(term, (1 - self.place) * width, width, 3) for term in self.terms]
            )
            self.terms = [lax.dynamic_slice_in_dim(term, self.place * width, width, 3) for term in self.terms]
            self.came = lax.ppermute(away, "seq", SWAP)
        else:
            away = rounded_sum([term[:, 1:] for term in self.terms])
            self.terms = [term[:, :1] for term in self.terms]
            self.came = flipped(away, self.parts, 2)
        return away

    def take(self, mark):
        self.terms.append(pinned(self.came, mark))


def body(block_input, lead_gain, joint_weight, output_weight, tail_gain, up_weight, down_weight, cotangent):
    rows, triple = joint_weight.shape
    dim = block_input.shape[2]
    wide = up_weight.shape[1]
    half = block_input.shape[1]
    length = 2 * half
    parts = dim // rows
    group = triple // 6
    chunk = dim // 2
    place = lax.axis_index("seq")
    me = lax.axis_index("fsdp")
    direct = parts == 16
    base = me if direct else jnp.zeros_like(me)
    spots = jnp.arange(16, dtype=jnp.int32)
    few = jnp.arange(8, dtype=jnp.int32)
    eight = (few % 2) * 8 + (few // 2 % 2) * 4 + few // 4 * 2
    meta = jnp.concatenate(
        [
            place[None],
            spots % 8 // 2 * 4 + ((base % 4) ^ (spots % 2 * 2 + spots // 8)),
            base ^ jnp.concatenate([eight, eight ^ 1]) if direct else spots,
        ]
    ).astype(jnp.int32)

    joint_own = lax.dynamic_index_in_dim(joint_weight.reshape(rows, 3, 2, group), place, 2, keepdims=False)
    joint_own = joint_own.reshape(rows, 3, 3, PAIR).transpose(0, 2, 1, 3).reshape(rows, 3 * group)
    packed = pl.pallas_call(
        pack,
        name="pack",
        out_shape=shaped(rows, 9 * dim),
        compiler_params=pltpu.CompilerParams(vmem_limit_bytes=LIMIT),
        cost_estimate=cost(2),
    )(output_weight, up_weight, down_weight)

    own = block_input[0]
    upstream = cotangent[0]
    rest = lax.all_gather(packed, "fsdp", axis=0, tiled=True)
    other = lax.ppermute(own, "seq", SWAP)
    both_gains = jnp.pad(jnp.stack([lead_gain, tail_gain], axis=1), ((0, 0), (0, PAIR - 2)))
    first = jnp.concatenate([joint_own, both_gains], axis=1)
    if direct:
        for bit in (8, 4, 2):
            if bit == 2:
                first, other = lax.optimization_barrier((first, other))
            first = jnp.concatenate([first, flipped(first, parts, bit)], axis=0)
        firsts = (first, flipped(first, parts, 1))
    else:
        first = lax.all_gather(first, "fsdp", axis=0, tiled=True)
        firsts = (first[:chunk], first[chunk:])

    (z_one,) = call(first_norm, "first_norm", (shaped(length, dim, dtype=F32),), meta, (own, other), took=3)
    zb, gains = call(
        first_scale,
        "first_scale",
        (shaped(length, dim), shaped(16, dim)),
        meta,
        (z_one, *firsts),
        [pltpu.VMEM((dim, PAIR), BF16)],
        took=2,
        grid=(1,),
        specs=[VMEM] + [column(chunk, PAIR, lambda step: 9)] * 2,
    )
    triples = column(length, 3 * PAIR)
    pair_tokens = column(half, PAIR)
    lse_spec = pl.BlockSpec((1, 8, length), lambda step: (step, 0, 0))
    qkv, o_own, o_other, lse, weight = call(
        attend,
        "attend",
        (
            shaped(length, 9 * PAIR),
            shaped(half, group),
            shaped(half, group),
            shaped(3, 8, length, dtype=F32),
            shaped(dim, 9 * PAIR),
        ),
        meta,
        (zb, *firsts),
        [
            pltpu.VMEM((2, length, PAIR), BF16),
            pltpu.VMEM((PAIR, length), BF16),
            pltpu.VMEM((2, length, BAND), F32),
            pltpu.VMEM((PAIR, BAND), F32),
            pltpu.VMEM((length, PAIR), BF16),
        ],
        took=22,
        grid=(3,),
        specs=[whole(length, dim)] + [column(chunk, 3 * PAIR)] * 2,
        out_specs=[triples, pair_tokens, pair_tokens, lse_spec, column(dim, 3 * PAIR)],
    )
    o_came = lax.ppermute(o_other, "seq", SWAP)
    store = [pltpu.VMEM((dim, length), BF16)]
    (zt,) = call(turn, "turn", (shaped(dim, length),), meta, (zb,), store, took=2, after=[lse])
    mixed, mixed_t = call(
        mix,
        "mix",
        (shaped(half, dim), shaped(dim, half)),
        meta,
        (o_own, o_came),
        [pltpu.VMEM((dim, half), BF16)],
        took=2,
        after=[zt],
    )
    rest_block = column(dim, dim, lambda step: 0)
    total_f32 = shaped(half, dim, dtype=F32)
    tokens = whole(half, dim)

    turned = whole(dim, half)
    active, dpre, grad_first, zt_two, resid, dresid, db, dm_away, dm_mine = call(
        feed,
        "feed",
        (shaped(half, wide),) * 2
        + (shaped(dim, 4 * dim), shaped(dim, half))
        + (total_f32, total_f32, shaped(half, dim), shaped(half, group), shaped(half, group)),
        meta,
        (own, mixed, gains, rest, rest, rest, upstream),
        [
            pltpu.VMEM((half, dim), BF16),
            pltpu.VMEM((dim, half), BF16),
            pltpu.VMEM((half, dim), F32),
            pltpu.VMEM((dim, half), BF16),
        ],
        took=20,
        grid=(4,),
        specs=[
            tokens,
            tokens,
            whole(16, dim),
            rest_block,
            column(dim, dim, lambda k: 1 + 2 * k),
            column(dim, dim, lambda k: 2 + 2 * k),
            tokens,
        ],
        out_specs=[column(half, dim)] * 2
        + [column(dim, 2 * dim, lambda k: jnp.minimum(k, 1)), turned]
        + [tokens] * 3 + [whole(half, group)] * 2,
    )
    dm_came = lax.ppermute(dm_away, "seq", SWAP)
    up_keep, up_send, down_keep, down_send, mixed_keep, mixed_send = call(
        hidden_back,
        "hidden_back",
        (shaped(chunk, 2 * dim),) * 4 + (shaped(chunk, dim),) * 2,
        meta,
        (zt_two, active, dpre, upstream, mixed_t, db),
        [pltpu.VMEM((dim, half), BF16), pltpu.VMEM((dim, half), BF16)],
        took=7,
        grid=(2,),
        specs=[turned] + [column(half, dim, lambda k: k + 2)] * 2 + [tokens, turned, tokens],
        out_specs=[column(chunk, dim)] * 4 + [whole(chunk, dim)] * 2,
    )
    dm_came = pinned(dm_came, up_keep)

    def blocks_of(part):
        return part.reshape(4, 2, rows, -1)

    marks = [[], [], []]
    if direct:
        first_sum = lax.psum_scatter(grad_first, "fsdp", scatter_dimension=0, tiled=True)
        up_came, down_came, mixed_came = (
            flipped(pinned(part, dm_came), parts, 1) for part in (up_send, down_send, mixed_send)
        )
    def attend_back_call(pair, outs, out_specs, extra, after):
        width = (9 if pair == 2 else 3) * PAIR
        pick = lambda step: pair
        return call(
            functools.partial(attend_back, pair),
            "attend_back",
            (shaped(chunk, width), shaped(chunk, width)) + outs,
            meta,
            (qkv, o_own, o_other, dm_mine, dm_came, lse, zt, weight, *extra),
            [
                pltpu.VMEM((2, length, PAIR), BF16),
                pltpu.VMEM((2, length, PAIR), BF16),
                pltpu.VMEM((PAIR, length), BF16),
                pltpu.VMEM((length, PAIR), BF16),
                pltpu.VMEM((8, length), F32),
                pltpu.VMEM((length, PAIR), F32),
                pltpu.VMEM((length, PAIR), F32),
                pltpu.VMEM((PAIR, BAND), F32),
                pltpu.VMEM((length, 3 * PAIR), BF16),
                pltpu.VMEM((2, length, BAND), F32),
                pltpu.VMEM((2, length, BAND), F32),
                pltpu.VMEM((2, length, BAND), BF16),
                pltpu.VMEM((2, length, BAND), BF16),
            ],
            took=10,
            after=after,
            grid=(1,),
            specs=[column(length, 3 * PAIR, pick)]
            + [column(half, PAIR, pick)] * 4
            + [
                pl.BlockSpec((1, 8, length), lambda step: (pair, 0, 0)),
                whole(dim, length),
                column(dim, 3 * PAIR, pick),
            ]
            + [whole(*part.shape) for part in extra],
            out_specs=[whole(chunk, width)] * 2 + out_specs,
        )

    one = (shaped(length, 3 * PAIR),)
    keep_0, send_0, token_0 = attend_back_call(0, one, [whole(length, 3 * PAIR)], (), marks[0])
    if direct:
        pairs = ((up_keep, up_came), (down_keep, down_came), (mixed_keep, mixed_came))
        up_red, down_red, mixed_red = (
            Reduction([blocks_of(part) for part in (keep, pinned(came, token_0))], parts, place) for keep, came in pairs
        )
        marks[1] += [up_red.go(2), down_red.go("seq"), mixed_red.go("seq")]
    keep_1, send_1, token_1 = attend_back_call(1, one, [whole(length, 3 * PAIR)], (), marks[1] + [token_0])
    marks[2].append(token_1)
    joint_keep, joint_send, token_2 = attend_back_call(
        2, one, [whole(length, 3 * PAIR)], (keep_0, send_0, keep_1, send_1), marks[2]
    )
    if direct:
        reds = (up_red, down_red, mixed_red)
        joint_send, *cames = lax.optimization_barrier((joint_send, *(red.came for red in reds)))
        for red, came in zip(reds, cames):
            red.terms.append(came)
    marks = []
    marks = []
    if direct:
        joint_came = flipped(joint_send, parts, 1)
        joint_red = Reduction([blocks_of(part) for part in (joint_keep, joint_came)], parts, place)
        marks = [up_red.go("seq"), down_red.go(2), mixed_red.go(2)]
        joint_red.terms = list(pinned(joint_red.terms, marks))
        marks.append(joint_red.go(2))
    sent, own_part = call(
        token_back,
        "token_back",
        (shaped(half, dim), total_f32),
        meta,
        (token_0, token_1, token_2, weight),
        took=5,
        after=marks,
    )
    other_part = lax.ppermute(sent, "seq", SWAP)

    def forward_call(late, before, after):
        at = 2 * late
        return call(
            forward_out,
            "forward_out",
            (shaped(half, dim) if late else total_f32,),
            meta,
            (before, active, rest),
            [pltpu.VMEM((half, dim), F32)],
            took=3,
            after=after,
            grid=(2,),
            specs=[tokens, column(half, dim, lambda k: at + k), column(dim, dim, lambda k: 2 + 2 * (at + k))],
            out_specs=[tokens],
        )

    marks = [own_part]
    if direct:
        marks = [own_part]
        last_sum = []
        for red in (up_red, down_red, mixed_red):
            red.take(own_part)
            last_sum.append(rounded_sum(red.terms))
        last_sum = jnp.concatenate(last_sum, axis=-1).reshape(4, rows, -1)
        deep = me // 4
        last_parts = [lax.dynamic_index_in_dim(last_sum, deep, 0, keepdims=False)]
        for far in (1, 2, 3):
            away = lax.dynamic_index_in_dim(last_sum, deep ^ far, 0, keepdims=False)
            last_parts.append(flipped(away, parts, 4 * far))
            marks.append(away)
        joint_red.take(marks)
        joint_sum = rounded_sum(joint_red.terms).reshape(4, rows, -1)
        marks.append(joint_sum)
    (out,) = forward_call(0, resid, marks)
    marks = []
    if direct:
        joint_sum = exchanged(joint_sum, parts)
    (out,) = forward_call(1, out, marks)
    marks = [out]
    (input_grad,) = call(
        input_back, "input_back", (total_f32,), meta, (own, own_part, other_part, dresid, gains), after=marks
    )

    if direct:
        last_sum = rounded_sum(last_parts)
        joint_sum = jnp.sum(pinned(joint_sum, out).astype(F32), axis=0).astype(BF16)
    else:

        def scattered(keep, send):
            blocks = jnp.stack([keep, send]).reshape(2, 4, 2, dim // 16, -1).transpose(1, 2, 0, 3, 4).reshape(dim, -1)
            return lax.psum_scatter(blocks, "fsdp", scatter_dimension=0, tiled=True)

        first_sum = lax.psum_scatter(grad_first, "fsdp", scatter_dimension=0, tiled=True)
        last_sum = ((up_keep, up_send), (down_keep, down_send), (mixed_keep, mixed_send))
        last_sum = jnp.concatenate([scattered(*pair) for pair in last_sum], axis=1)
        joint_sum = scattered(joint_keep, joint_send)
    first_sum = pinned(first_sum, input_grad)
    first_sum, last_sum, joint_sum = ((part, lax.ppermute(part, "seq", SWAP)) for part in (first_sum, last_sum, joint_sum))
    up_grad, down_grad, output_grad, tail_grad = call(
        functools.partial(feed_out, direct),
        "feed_out",
        (
            shaped(rows, wide, dtype=F32),
            shaped(4 * rows, dim, dtype=F32),
            shaped(rows, dim, dtype=F32),
            shaped(1, rows, dtype=F32),
        ),
        meta,
        (*first_sum, *last_sum, up_weight, tail_gain[None, :]),
        after=[input_grad],
    )
    joint_grad, lead_grad = call(
        joint_out,
        "joint_out",
        (shaped(rows, triple, dtype=F32), shaped(1, rows, dtype=F32)),
        meta,
        (*joint_sum, joint_weight, lead_gain[None, :]),
        took=2,
        after=[up_grad],
    )
    return (
        out[None],
        input_grad[None],
        lead_grad[0],
        joint_grad,
        output_grad,
        tail_grad[0],
        up_grad,
        down_grad,
    )


def solution(mesh):
    split = P("fsdp", "seq", None)
    placed = (split, P("fsdp"), P("fsdp", None), P("fsdp", None), P("fsdp"), P("fsdp", None), P("fsdp", None), split)
    return jax.shard_map(
        body,
        mesh=mesh,
        in_specs=placed,
        out_specs=(split, split, P("fsdp"), P("fsdp", None), P("fsdp", None), P("fsdp"), P("fsdp", None), P("fsdp", None)),
        check_vma=False,
    )
```

```python
import functools

import jax
import jax.numpy as jnp
from jax import lax
from jax.experimental import pallas as pl
from jax.experimental.pallas import tpu as pltpu
from jax.sharding import PartitionSpec as P

HD = 64
EPS = 1e-05
PAIR = 2 * HD
BAND = 256
LOG2E = 1.4426950408889634
LIMIT = 56 << 20
F32 = jnp.float32
BF16 = jnp.bfloat16

VMEM = pl.BlockSpec(memory_space=pltpu.VMEM)
SMEM = pl.BlockSpec(memory_space=pltpu.SMEM)
ANY = pl.BlockSpec(memory_space=pl.ANY)


def dot(left, right):
    return jnp.dot(left, right, preferred_element_type=F32)


def dot_t(left, right):
    return lax.dot_general(left, right, (((1,), (1,)), ((), ())), preferred_element_type=F32)


def shaped(*dims, dtype=BF16):
    return jax.ShapeDtypeStruct(dims, dtype)


def cost(microseconds):
    return pl.CostEstimate(flops=int(microseconds * 1e7), transcendentals=0, bytes_accessed=int(microseconds * 3e4))


def waiting(kernel, fixed, after):
    def run(*refs):
        kernel(*refs[:fixed], *refs[fixed + after :])

    return run


def whole(*dims):
    return pl.BlockSpec(dims, lambda *_: (0,) * len(dims))


def column(rows, columns, pick=lambda step: step):
    return pl.BlockSpec((rows, columns), lambda *steps: (0, pick(*steps)))


def call(kernel, name, outs, meta, inputs, scratch=(), took=4, after=(), grid=(), specs=None, out_specs=None):
    return pl.pallas_call(
        waiting(kernel, 1 + len(inputs), len(after)),
        name=name,
        grid=grid,
        out_shape=outs,
        in_specs=[SMEM] + list(specs or [VMEM] * len(inputs)) + [ANY] * len(after),
        out_specs=list(out_specs or [VMEM] * len(outs)),
        scratch_shapes=list(scratch),
        compiler_params=pltpu.CompilerParams(vmem_limit_bytes=LIMIT),
        cost_estimate=cost(took),
    )(meta, *inputs, *after)


def standardize(values):
    center = values - jnp.mean(values, axis=-1, keepdims=True)
    spread = jnp.mean(center * center, axis=-1, keepdims=True)
    rstd = lax.rsqrt(spread + EPS)
    return center * rstd, rstd


def norm_back(z, rstd, g):
    return (g - jnp.mean(g, axis=-1, keepdims=True) - z * jnp.mean(g * z, axis=-1, keepdims=True)) * rstd


def half_at(index, size):
    return pl.ds(pl.multiple_of(index * size, size), size)


def rows_in_order(meta, source, target):
    size = source.shape[0] // 16
    for spot in range(16):
        rows = pl.ds(pl.multiple_of(meta[1 + spot] * size, size), size)
        target[spot * size : (spot + 1) * size, :] = source[rows, :]


def placed(meta, near, far, target):
    size = target.shape[0] // 16
    for spot in range(16):
        source = (near, far)[spot // 8]
        rows = pl.ds(pl.multiple_of(meta[17 + spot] * size, size), size)
        target[rows, :] = source[spot % 8 * size : (spot % 8 + 1) * size, :]


def pack(output, up, down, packed):
    rows, dim = output.shape
    packed[:, :dim] = output[...]
    for k in range(4):
        at = (1 + 2 * k) * dim
        for owner in range(dim // rows):
            source = (4 * owner + k) * rows
            packed[:, at + owner * rows : at + (owner + 1) * rows] = up[:, source : source + rows]
        packed[:, at + dim : at + 2 * dim] = down[k * rows : (k + 1) * rows, :]


def first_norm(meta, own, other, z):
    half = own.shape[0]
    for source, place in ((own, meta[0]), (other, 1 - meta[0])):
        z[half_at(place, half), :] = standardize(source[...].astype(F32))[0]


def first_scale(meta, z, near, far, zb, gains, columns):
    placed(meta, near, far, columns)
    gains[...] = columns[...].T[:16, :]
    zb[...] = (z[...] * gains[0:1, :].astype(F32)).astype(BF16)


def turn(meta, zb, zt, turned):
    turned[...] = zb[...].T
    rows_in_order(meta, turned, zt)


def mix(meta, mine, other, mixed, mt, turned):
    width = mine.shape[1]
    for side, source in ((meta[0], mine), (1 - meta[0], other)):
        mixed[:, half_at(side, width)] = source[...]
    turned[...] = mixed[...].T
    rows_in_order(meta, turned, mt)


def attend(meta, zb, near, far, qkv, o_own, o_other, lse, weight, km, vt, s_sc, ot, o_all):
    length = zb.shape[0]
    half = length // 2
    placed(meta, near, far, weight)
    qkv[...] = dot(zb[...], weight[...]).astype(BF16)
    lane = lax.broadcasted_iota(jnp.int32, (1, PAIR), 1)
    keys = qkv[:, PAIR : 2 * PAIR]
    zero = jnp.zeros_like(keys)
    km[0] = jnp.where(lane < HD, keys, zero)
    km[1] = jnp.where(lane < HD, zero, keys)
    vt[...] = qkv[:, 2 * PAIR :].T
    lse[0] = jnp.zeros(lse.shape[1:], F32)
    allowed = lax.broadcasted_iota(jnp.int32, (BAND, BAND), 0) <= lax.broadcasted_iota(jnp.int32, (BAND, BAND), 1)

    def q_step(q_band, _):
        spots = half_at(q_band, BAND)
        queries = qkv[spots, :PAIR]

        def score(k_band, tops, diagonal):
            rows = half_at(k_band, BAND)
            peaks = []
            for head in range(2):
                s = dot_t(km[head, rows, :], queries) * (HD ** -0.5 * LOG2E)
                if diagonal:
                    s = jnp.where(allowed, s, 0.0)
                s_sc[head, rows, :] = s
                peaks.append(jnp.maximum(tops[head], jnp.max(jnp.abs(s), axis=0, keepdims=True)))
            return tuple(peaks)

        def weigh(k_band, carry, tops, diagonal):
            rows = half_at(k_band, BAND)
            results = []
            for head, (total, out) in enumerate(carry):
                s = s_sc[head, rows, :]
                grow = jnp.exp2(s - tops[head])
                shrink = jnp.exp2(-s - tops[head])
                both = grow + shrink
                if diagonal:
                    both = jnp.where(allowed, both, 0.0)
                part = dot(vt[head * HD : (head + 1) * HD, rows], (grow - shrink).astype(BF16))
                results.append((total + jnp.sum(both, axis=0, keepdims=True), out + part))
            return tuple(results)

        none = jnp.zeros((1, BAND), F32)
        tops = score(q_band, (none, none), True)
        tops = lax.fori_loop(0, q_band, lambda k_band, tops: score(k_band, tops, False), tops)
        start = (none, jnp.zeros((HD, BAND), F32))
        carry = weigh(q_band, (start, start), tops, True)
        carry = lax.fori_loop(0, q_band, lambda k_band, carry: weigh(k_band, carry, tops, False), carry)
        for head, (total, out) in enumerate(carry):
            ot[head * HD : (head + 1) * HD, :] = out / total
            lse[0, head : head + 1, spots] = tops[head] + jnp.log2(0.5 * total)
        o_all[spots, :] = ot[...].T.astype(BF16)
        return 0

    lax.fori_loop(0, length // BAND, q_step, 0)
    o_own[...] = o_all[half_at(meta[0], half), :]
    o_other[...] = o_all[half_at(1 - meta[0], half), :]


def attend_back(pair, meta, qkv, o_own, o_other, d_own, d_other, lse, zt, weight, *refs):
    last = pair == 2
    count = (0, 0, 4)[pair]
    extra, refs = refs[:count], refs[count:]
    keep, send, *outs = refs[:3]
    km, vm, kt, do, inner, dk, dv, dqt, dqkv, s_sc, w_sc, p_sc, ds_sc = refs[3:]
    length = qkv.shape[0]
    half = length // 2
    lane = lax.broadcasted_iota(jnp.int32, (1, PAIR), 1)
    low = lane < HD
    keys = qkv[:, PAIR : 2 * PAIR]
    values = qkv[:, 2 * PAIR :]
    zero = jnp.zeros_like(keys)
    km[0] = jnp.where(low, keys, zero)
    km[1] = jnp.where(low, zero, keys)
    vm[0] = jnp.where(low, values, zero)
    vm[1] = jnp.where(low, zero, values)
    kt[...] = keys.T
    pick = (
        lax.broadcasted_iota(jnp.int32, (8, PAIR), 1) // HD == lax.broadcasted_iota(jnp.int32, (8, PAIR), 0)
    ).astype(F32)
    for o_part, d_part, place in ((o_own, d_own, meta[0]), (o_other, d_other, 1 - meta[0])):
        do[half_at(place, half), :] = d_part[...]
        product = o_part[...].astype(F32) * d_part[...].astype(F32)
        inner[:, half_at(place, half)] = lax.dot_general(
            pick, product, (((1,), (1,)), ((), ())), preferred_element_type=F32, precision=lax.Precision.HIGHEST
        )
    allowed = lax.broadcasted_iota(jnp.int32, (BAND, BAND), 0) <= lax.broadcasted_iota(jnp.int32, (BAND, BAND), 1)
    for q_band in range(length // BAND):
        spots = slice(q_band * BAND, (q_band + 1) * BAND)
        end = (q_band + 1) * BAND
        queries = qkv[spots, :PAIR]
        upstream = do[spots, :]
        small = jnp.zeros_like(queries)
        for head in range(2):
            mine = slice(head * HD, (head + 1) * HD)
            q_mine = jnp.where(low, queries, small) if head == 0 else jnp.where(low, small, queries)
            d_mine = jnp.where(low, upstream, small) if head == 0 else jnp.where(low, small, upstream)
            base = lse[0, head : head + 1, spots] + 1.0
            mean = inner[head : head + 1, spots]
            s_sc[head, :end, :] = dot_t(km[head, :end, :], queries)
            w_sc[head, :end, :] = dot_t(vm[head, :end, :], upstream)
            for k_band in range(q_band + 1):
                rows = slice(k_band * BAND, (k_band + 1) * BAND)
                s = s_sc[head, rows, :] * (HD ** -0.5 * LOG2E)
                dw = w_sc[head, rows, :]
                if k_band == q_band:
                    s = jnp.where(allowed, s, 0.0)
                    dw = jnp.where(allowed, dw, 0.0)
                grow = jnp.exp2(s - base)
                shrink = jnp.exp2(-s - base)
                p = grow - shrink
                p_sc[head, rows, :] = p.astype(BF16)
                ds_sc[head, rows, :] = ((grow + shrink) * dw - p * mean).astype(BF16)
            dv_part = dot(p_sc[head, :end, :], d_mine)
            dk_part = dot(ds_sc[head, :end, :], q_mine)
            dqt[mine, :] = dot(kt[mine, :end], ds_sc[head, :end, :])
            old = q_band * BAND if head == 0 else end
            if old:
                dv[:old, :] += dv_part[:old]
                dk[:old, :] += dk_part[:old]
            if head == 0:
                dv[old:end, :] = dv_part[old:]
                dk[old:end, :] = dk_part[old:]
        dqkv[spots, :PAIR] = (dqt[...].T * HD ** -0.5).astype(BF16)
    dqkv[:, PAIR : 2 * PAIR] = (dk[...] * HD ** -0.5).astype(BF16)
    dqkv[:, 2 * PAIR :] = dv[...].astype(BF16)
    middle = keep.shape[0]
    start = keep.shape[1] - 3 * PAIR
    send[:, start:] = dot(zt[middle:, :], dqkv[...]).astype(BF16)
    keep[:, start:] = dot(zt[:middle, :], dqkv[...]).astype(BF16)
    if last:
        for spot in range(2):
            columns = slice(spot * 3 * PAIR, (spot + 1) * 3 * PAIR)
            keep[:, columns] = extra[2 * spot][...]
            send[:, columns] = extra[2 * spot + 1][...]
    outs[0][...] = dqkv[...]


def token_back(meta, t0, t1, t2, weight, away, mine_out):
    half = away.shape[0]
    for side, target in ((1 - meta[0], away), (meta[0], mine_out)):
        part = None
        for spot, token in enumerate((t0, t1, t2)):
            columns = slice(spot * 3 * PAIR, (spot + 1) * 3 * PAIR)
            new = dot_t(token[half_at(side, half), :], weight[:, columns])
            part = new if part is None else part + new
        target[...] = part.astype(target.dtype)


def added(step, total, first, part):
    @pl.when(step == 0)
    def _():
        total[...] = part if first is None else first[...] + part

    @pl.when(step > 0)
    def _():
        total[...] += part


def feed(
    meta, own, mixed, gains, weight, up, down, upstream,
    active, dpre, first, zt, resid, dresid, db, away, mine_out, zb, zt_natural, g_total, turned,
):
    step = pl.program_id(0)
    gain = gains[1:2, :].astype(F32)

    @pl.when(step == 0)
    def _():
        summed = own[...].astype(F32) + dot(mixed[...], weight[...])
        resid[...] = summed
        z = (standardize(summed)[0] * gain).astype(BF16)
        zb[...] = z
        zt_natural[...] = z.T
        rows_in_order(meta, zt_natural, zt)

    width = active.shape[1]
    root = 0.7978845608028654
    for part in range(3):
        mine = slice(part * width // 3, (part + 1) * width // 3)
        v = dot(zb[...], up[:, mine])
        slope_in = dot_t(upstream[...], down[mine, :])
        square = v * v
        t = jnp.tanh(root * v * (1.0 + 0.044715 * square))
        cdf = 0.5 * (1.0 + t)
        active[:, mine] = (v * cdf).astype(BF16)
        slope = cdf + v * (0.5 * root) * (1.0 - t * t) * (1.0 + 0.134145 * square)
        dpre[:, mine] = (slope_in * slope).astype(BF16)
    added(step, g_total, None, dot_t(dpre[...], up[...]))

    @pl.when(step < 2)
    def _():
        turned[...] = active[...].T
        first[:, :width] = dot(zt_natural[...], dpre[...]).astype(BF16)
        first[:, width:] = dot(turned[...], upstream[...]).astype(BF16)

    @pl.when(step == pl.num_programs(0) - 1)
    def _():
        z, rstd = standardize(resid[...])
        grad = upstream[...].astype(F32) + norm_back(z, rstd, g_total[...] * gain)
        low = grad.astype(BF16)
        for side, target in ((1 - meta[0], away), (meta[0], mine_out)):
            target[...] = dot_t(low, weight[half_at(side, 3 * PAIR), :]).astype(BF16)
        dresid[...] = grad
        db[...] = low


def hidden_back(
    meta, zt, active, dpre, upstream, mt, db,
    up_keep, up_send, down_keep, down_send, mixed_keep, mixed_send, turned, picked,
):
    step = pl.program_id(0)
    width = active.shape[1]
    turned[...] = active[...].T
    rows_in_order(meta, turned, picked)
    size = width // 2
    for spot, (up_part, down_part) in enumerate(((up_keep, down_keep), (up_send, down_send))):
        mine = slice(spot * size, (spot + 1) * size)
        up_part[...] = dot(zt[mine, :], dpre[...]).astype(BF16)
        down_part[...] = dot(picked[mine, :], upstream[...]).astype(BF16)

    @pl.when(step == pl.num_programs(0) - 1)
    def _():
        mixed_send[...] = dot(mt[size:, :], db[...]).astype(BF16)
        mixed_keep[...] = dot(mt[:size, :], db[...]).astype(BF16)


def forward_out(meta, before, active, down, out, total):
    step = pl.program_id(0)
    added(step, total, before, dot(active[...], down[...]))

    @pl.when(step == pl.num_programs(0) - 1)
    def _():
        out[...] = total[...].astype(out.dtype)


def input_back(meta, own, mine, other, dresid, gains, out):
    z, rstd = standardize(own[...].astype(F32))
    g = (mine[...] + other[...].astype(F32)) * gains[0:1, :].astype(F32)
    out[...] = dresid[...] + norm_back(z, rstd, g)


def row_sums(values):
    ones = jnp.ones((8, values.shape[1]), F32)
    sums = lax.dot_general(
        ones, values, (((1,), (1,)), ((), ())), preferred_element_type=F32, precision=lax.Precision.HIGHEST
    )
    return sums[0:1, :]


def joint_out(meta, own, other, weight, gain, grad, gain_grad):
    for side, source in ((meta[0], own), (1 - meta[0], other)):
        for pair in range(3):
            for kind in range(3):
                columns = pl.ds(pl.multiple_of((kind * 6 + side * 3 + pair) * PAIR, PAIR), PAIR)
                at = (pair * 3 + kind) * PAIR
                grad[:, columns] = source[:, at : at + PAIR].astype(F32)
    gain_grad[...] = row_sums(grad[...] * weight[...].astype(F32)) / gain[...].astype(F32)


def feed_out(split, meta, first, first_too, last, last_too, weight, gain, up, down, output, gain_grad):
    rows, dim = output.shape
    if split:
        width = dim // 2
        for side, source in ((meta[0], last), (1 - meta[0], last_too)):
            output[:, half_at(side, width)] = source[:, 2 * dim :].astype(F32)
    else:
        output[...] = last[:, -dim:].astype(F32) + last_too[:, -dim:].astype(F32)
    for k in range(4):
        parts = []
        for kind in range(2):
            if k < 2 or not split:
                one, two = (first, first_too) if k < 2 else (last, last_too)
                at = ((2 * k + kind) if k < 2 else (2 * kind + k - 2)) * dim
                parts.append(one[:, at : at + dim].astype(F32) + two[:, at : at + dim].astype(F32))
            else:
                at = kind * dim
                parts.append(jnp.where(meta[0] == k - 2, last[:, at : at + dim], last_too[:, at : at + dim]).astype(F32))
        for owner in range(dim // rows):
            up[:, (4 * owner + k) * rows : (4 * owner + k + 1) * rows] = parts[0][:, owner * rows : (owner + 1) * rows]
        down[k * rows : (k + 1) * rows, :] = parts[1]
    gain_grad[...] = row_sums(up[...] * weight[...].astype(F32)) / gain[...].astype(F32)


SWAP = [(0, 1), (1, 0)]


def flipped(array, parts, bit):
    return lax.ppermute(array, "fsdp", [(spot, spot ^ bit) for spot in range(parts)])


def exchanged(blocks, parts):
    groups = [list(range(side, parts, 4)) for side in range(4)]
    return lax.all_to_all(blocks, "fsdp", 0, 0, axis_index_groups=groups, tiled=True)


def rounded_sum(terms):
    total = terms[0].astype(F32)
    for term in terms[1:]:
        total = total + term.astype(F32)
    return total.astype(BF16)


def pinned(array, mark):
    return lax.optimization_barrier((array, mark))[0]


class Reduction:
    def __init__(self, terms, parts, place):
        self.terms, self.parts, self.place = terms, parts, place

    def go(self, step):
        if step == "seq":
            width = self.terms[0].shape[3] // 2
            away = rounded_sum(
                [lax.dynamic_slice_in_dim(term, (1 - self.place) * width, width, 3) for term in self.terms]
            )
            self.terms = [lax.dynamic_slice_in_dim(term, self.place * width, width, 3) for term in self.terms]
            self.came = lax.ppermute(away, "seq", SWAP)
        else:
            away = rounded_sum([term[:, 1:] for term in self.terms])
            self.terms = [term[:, :1] for term in self.terms]
            self.came = flipped(away, self.parts, 2)
        return away

    def take(self, mark):
        self.terms.append(pinned(self.came, mark))


def body(block_input, lead_gain, joint_weight, output_weight, tail_gain, up_weight, down_weight, cotangent):
    rows, triple = joint_weight.shape
    dim = block_input.shape[2]
    wide = up_weight.shape[1]
    half = block_input.shape[1]
    length = 2 * half
    parts = dim // rows
    group = triple // 6
    chunk = dim // 2
    place = lax.axis_index("seq")
    me = lax.axis_index("fsdp")
    direct = parts == 16
    base = me if direct else jnp.zeros_like(me)
    spots = jnp.arange(16, dtype=jnp.int32)
    few = jnp.arange(8, dtype=jnp.int32)
    eight = (few % 2) * 8 + (few // 2 % 2) * 4 + few // 4 * 2
    meta = jnp.concatenate(
        [
            place[None],
            spots % 8 // 2 * 4 + ((base % 4) ^ (spots % 2 * 2 + spots // 8)),
            base ^ jnp.concatenate([eight, eight ^ 1]) if direct else spots,
        ]
    ).astype(jnp.int32)

    joint_own = lax.dynamic_index_in_dim(joint_weight.reshape(rows, 3, 2, group), place, 2, keepdims=False)
    joint_own = joint_own.reshape(rows, 3, 3, PAIR).transpose(0, 2, 1, 3).reshape(rows, 3 * group)
    packed = pl.pallas_call(
        pack,
        name="pack",
        out_shape=shaped(rows, 9 * dim),
        compiler_params=pltpu.CompilerParams(vmem_limit_bytes=LIMIT),
        cost_estimate=cost(2),
    )(output_weight, up_weight, down_weight)

    own = block_input[0]
    upstream = cotangent[0]
    rest = lax.all_gather(packed, "fsdp", axis=0, tiled=True)
    other = lax.ppermute(own, "seq", SWAP)
    both_gains = jnp.pad(jnp.stack([lead_gain, tail_gain], axis=1), ((0, 0), (0, PAIR - 2)))
    first = jnp.concatenate([joint_own, both_gains], axis=1)
    if direct:
        for bit in (8, 4, 2):
            if bit == 2:
                first, other = lax.optimization_barrier((first, other))
            first = jnp.concatenate([first, flipped(first, parts, bit)], axis=0)
        firsts = (first, flipped(first, parts, 1))
    else:
        first = lax.all_gather(first, "fsdp", axis=0, tiled=True)
        firsts = (first[:chunk], first[chunk:])

    (z_one,) = call(first_norm, "first_norm", (shaped(length, dim, dtype=F32),), meta, (own, other), took=3)
    zb, gains = call(
        first_scale,
        "first_scale",
        (shaped(length, dim), shaped(16, dim)),
        meta,
        (z_one, *firsts),
        [pltpu.VMEM((dim, PAIR), BF16)],
        took=2,
        grid=(1,),
        specs=[VMEM] + [column(chunk, PAIR, lambda step: 9)] * 2,
    )
    triples = column(length, 3 * PAIR)
    pair_tokens = column(half, PAIR)
    lse_spec = pl.BlockSpec((1, 8, length), lambda step: (step, 0, 0))
    qkv, o_own, o_other, lse, weight = call(
        attend,
        "attend",
        (
            shaped(length, 9 * PAIR),
            shaped(half, group),
            shaped(half, group),
            shaped(3, 8, length, dtype=F32),
            shaped(dim, 9 * PAIR),
        ),
        meta,
        (zb, *firsts),
        [
            pltpu.VMEM((2, length, PAIR), BF16),
            pltpu.VMEM((PAIR, length), BF16),
            pltpu.VMEM((2, length, BAND), F32),
            pltpu.VMEM((PAIR, BAND), F32),
            pltpu.VMEM((length, PAIR), BF16),
        ],
        took=22,
        grid=(3,),
        specs=[whole(length, dim)] + [column(chunk, 3 * PAIR)] * 2,
        out_specs=[triples, pair_tokens, pair_tokens, lse_spec, column(dim, 3 * PAIR)],
    )
    o_came = lax.ppermute(o_other, "seq", SWAP)
    store = [pltpu.VMEM((dim, length), BF16)]
    (zt,) = call(turn, "turn", (shaped(dim, length),), meta, (zb,), store, took=2, after=[lse])
    mixed, mixed_t = call(
        mix,
        "mix",
        (shaped(half, dim), shaped(dim, half)),
        meta,
        (o_own, o_came),
        [pltpu.VMEM((dim, half), BF16)],
        took=2,
        after=[zt],
    )
    rest_block = column(dim, dim, lambda step: 0)
    total_f32 = shaped(half, dim, dtype=F32)
    tokens = whole(half, dim)

    turned = whole(dim, half)
    active, dpre, grad_first, zt_two, resid, dresid, db, dm_away, dm_mine = call(
        feed,
        "feed",
        (shaped(half, wide),) * 2
        + (shaped(dim, 4 * dim), shaped(dim, half))
        + (total_f32, total_f32, shaped(half, dim), shaped(half, group), shaped(half, group)),
        meta,
        (own, mixed, gains, rest, rest, rest, upstream),
        [
            pltpu.VMEM((half, dim), BF16),
            pltpu.VMEM((dim, half), BF16),
            pltpu.VMEM((half, dim), F32),
            pltpu.VMEM((dim, half), BF16),
        ],
        took=20,
        grid=(4,),
        specs=[
            tokens,
            tokens,
            whole(16, dim),
            rest_block,
            column(dim, dim, lambda k: 1 + 2 * k),
            column(dim, dim, lambda k: 2 + 2 * k),
            tokens,
        ],
        out_specs=[column(half, dim)] * 2
        + [column(dim, 2 * dim, lambda k: jnp.minimum(k, 1)), turned]
        + [tokens] * 3 + [whole(half, group)] * 2,
    )
    dm_came = lax.ppermute(dm_away, "seq", SWAP)
    up_keep, up_send, down_keep, down_send, mixed_keep, mixed_send = call(
        hidden_back,
        "hidden_back",
        (shaped(chunk, 2 * dim),) * 4 + (shaped(chunk, dim),) * 2,
        meta,
        (zt_two, active, dpre, upstream, mixed_t, db),
        [pltpu.VMEM((dim, half), BF16), pltpu.VMEM((dim, half), BF16)],
        took=7,
        grid=(2,),
        specs=[turned] + [column(half, dim, lambda k: k + 2)] * 2 + [tokens, turned, tokens],
        out_specs=[column(chunk, dim)] * 4 + [whole(chunk, dim)] * 2,
    )
    dm_came = pinned(dm_came, up_keep)

    def blocks_of(part):
        return part.reshape(4, 2, rows, -1)

    marks = [[], [], []]
    if direct:
        first_sum = lax.psum_scatter(grad_first, "fsdp", scatter_dimension=0, tiled=True)
        up_came, down_came, mixed_came = (
            flipped(pinned(part, dm_came), parts, 1) for part in (up_send, down_send, mixed_send)
        )
    def attend_back_call(pair, outs, out_specs, extra, after):
        width = (9 if pair == 2 else 3) * PAIR
        pick = lambda step: pair
        return call(
            functools.partial(attend_back, pair),
            "attend_back",
            (shaped(chunk, width), shaped(chunk, width)) + outs,
            meta,
            (qkv, o_own, o_other, dm_mine, dm_came, lse, zt, weight, *extra),
            [
                pltpu.VMEM((2, length, PAIR), BF16),
                pltpu.VMEM((2, length, PAIR), BF16),
                pltpu.VMEM((PAIR, length), BF16),
                pltpu.VMEM((length, PAIR), BF16),
                pltpu.VMEM((8, length), F32),
                pltpu.VMEM((length, PAIR), F32),
                pltpu.VMEM((length, PAIR), F32),
                pltpu.VMEM((PAIR, BAND), F32),
                pltpu.VMEM((length, 3 * PAIR), BF16),
                pltpu.VMEM((2, length, BAND), F32),
                pltpu.VMEM((2, length, BAND), F32),
                pltpu.VMEM((2, length, BAND), BF16),
                pltpu.VMEM((2, length, BAND), BF16),
            ],
            took=10,
            after=after,
            grid=(1,),
            specs=[column(length, 3 * PAIR, pick)]
            + [column(half, PAIR, pick)] * 4
            + [
                pl.BlockSpec((1, 8, length), lambda step: (pair, 0, 0)),
                whole(dim, length),
                column(dim, 3 * PAIR, pick),
            ]
            + [whole(*part.shape) for part in extra],
            out_specs=[whole(chunk, width)] * 2 + out_specs,
        )

    one = (shaped(length, 3 * PAIR),)
    keep_0, send_0, token_0 = attend_back_call(0, one, [whole(length, 3 * PAIR)], (), marks[0])
    if direct:
        pairs = ((up_keep, up_came), (down_keep, down_came), (mixed_keep, mixed_came))
        up_red, down_red, mixed_red = (
            Reduction([blocks_of(part) for part in (keep, pinned(came, token_0))], parts, place) for keep, came in pairs
        )
        marks[1] += [up_red.go(2), down_red.go("seq"), mixed_red.go("seq")]
    keep_1, send_1, token_1 = attend_back_call(1, one, [whole(length, 3 * PAIR)], (), marks[1] + [token_0])
    marks[2].append(token_1)
    joint_keep, joint_send, token_2 = attend_back_call(
        2, one, [whole(length, 3 * PAIR)], (keep_0, send_0, keep_1, send_1), marks[2]
    )
    if direct:
        reds = (up_red, down_red, mixed_red)
        joint_send, *cames = lax.optimization_barrier((joint_send, *(red.came for red in reds)))
        for red, came in zip(reds, cames):
            red.terms.append(came)
    marks = []
    marks = []
    if direct:
        joint_came = flipped(joint_send, parts, 1)
        joint_red = Reduction([blocks_of(part) for part in (joint_keep, joint_came)], parts, place)
        marks = [up_red.go("seq"), down_red.go(2), mixed_red.go(2)]
        joint_red.terms = list(pinned(joint_red.terms, marks))
        marks.append(joint_red.go(2))
    sent, own_part = call(
        token_back,
        "token_back",
        (shaped(half, dim), total_f32),
        meta,
        (token_0, token_1, token_2, weight),
        took=5,
        after=marks,
    )
    other_part = lax.ppermute(sent, "seq", SWAP)

    def forward_call(before, after):
        return call(
            forward_out,
            "forward_out",
            (shaped(half, dim),),
            meta,
            (before, active, rest),
            [pltpu.VMEM((half, dim), F32)],
            took=3,
            after=after,
            grid=(4,),
            specs=[tokens, column(half, dim), column(dim, dim, lambda k: 2 + 2 * k)],
            out_specs=[tokens],
        )

    marks = [own_part]
    if direct:
        marks = [own_part]
        last_sum = []
        for red in (up_red, down_red, mixed_red):
            red.take(own_part)
            last_sum.append(rounded_sum(red.terms))
        last_sum = jnp.concatenate(last_sum, axis=-1).reshape(4, rows, -1)
        deep = me // 4
        last_parts = [lax.dynamic_index_in_dim(last_sum, deep, 0, keepdims=False)]
        for far in (1, 2, 3):
            away = lax.dynamic_index_in_dim(last_sum, deep ^ far, 0, keepdims=False)
            last_parts.append(flipped(away, parts, 4 * far))
            marks.append(away)
        joint_red.take(marks)
        joint_sum = rounded_sum(joint_red.terms).reshape(4, rows, -1)
        marks.append(joint_sum)
    (out,) = forward_call(resid, marks)
    marks = []
    if direct:
        joint_sum = exchanged(joint_sum, parts)
    marks = [out]
    (input_grad,) = call(
        input_back, "input_back", (total_f32,), meta, (own, own_part, other_part, dresid, gains), after=marks
    )

    if direct:
        last_sum = rounded_sum(last_parts)
        joint_sum = jnp.sum(pinned(joint_sum, out).astype(F32), axis=0).astype(BF16)
    else:

        def scattered(keep, send):
            blocks = jnp.stack([keep, send]).reshape(2, 4, 2, dim // 16, -1).transpose(1, 2, 0, 3, 4).reshape(dim, -1)
            return lax.psum_scatter(blocks, "fsdp", scatter_dimension=0, tiled=True)

        first_sum = lax.psum_scatter(grad_first, "fsdp", scatter_dimension=0, tiled=True)
        last_sum = ((up_keep, up_send), (down_keep, down_send), (mixed_keep, mixed_send))
        last_sum = jnp.concatenate([scattered(*pair) for pair in last_sum], axis=1)
        joint_sum = scattered(joint_keep, joint_send)
    first_sum = pinned(first_sum, input_grad)
    first_sum, last_sum, joint_sum = ((part, lax.ppermute(part, "seq", SWAP)) for part in (first_sum, last_sum, joint_sum))
    up_grad, down_grad, output_grad, tail_grad = call(
        functools.partial(feed_out, direct),
        "feed_out",
        (
            shaped(rows, wide, dtype=F32),
            shaped(4 * rows, dim, dtype=F32),
            shaped(rows, dim, dtype=F32),
            shaped(1, rows, dtype=F32),
        ),
        meta,
        (*first_sum, *last_sum, up_weight, tail_gain[None, :]),
        after=[input_grad],
    )
    joint_grad, lead_grad = call(
        joint_out,
        "joint_out",
        (shaped(rows, triple, dtype=F32), shaped(1, rows, dtype=F32)),
        meta,
        (*joint_sum, joint_weight, lead_gain[None, :]),
        took=2,
        after=[up_grad],
    )
    return (
        out[None],
        input_grad[None],
        lead_grad[0],
        joint_grad,
        output_grad,
        tail_grad[0],
        up_grad,
        down_grad,
    )


def solution(mesh):
    split = P("fsdp", "seq", None)
    placed = (split, P("fsdp"), P("fsdp", None), P("fsdp", None), P("fsdp"), P("fsdp", None), P("fsdp", None), split)
    return jax.shard_map(
        body,
        mesh=mesh,
        in_specs=placed,
        out_specs=(split, split, P("fsdp"), P("fsdp", None), P("fsdp", None), P("fsdp"), P("fsdp", None), P("fsdp", None)),
        check_vma=False,
    )
```
